32 devices in a mesh: dp: 16 (over z, y, core), tensor: 2 (over x).
Axes of the slice: x: 2, y: 2, z: 4, core: 2. Of those that a mesh axis runs over, the one named last changes fastest.
Arguments:
- inputs: bfloat16 [12288, 1024], P(('dp', 'tensor')), may hold values from -6 to 6
- out_grad: bfloat16 [12288, 1024], P(('dp', 'tensor')), may hold values from -6 to 6
- parents: int32 [16, 3], P('dp'), may hold values from 0 to 1, as said below
- ln1_gain: bfloat16 [1024], P('dp'), may hold values from 0.5 to 1.5
- ln1_bias: bfloat16 [1024], P('dp'), may hold values from -1.5 to 1.5
- w_qkv: bfloat16 [3, 1024, 1024], P(None, 'dp', 'tensor'), may hold values from -0.25 to 0.25
- qv_bias: bfloat16 [2, 1024], P(None, 'dp'), may hold values from -1.5 to 1.5
- w_attn_out: bfloat16 [1024, 1024], P('tensor', 'dp'), may hold values from -0.75 to 0.75
- attn_out_bias: bfloat16 [1024], P('dp'), may hold values from -1.5 to 1.5
- ln2_gain: bfloat16 [1024], P('dp'), may hold values from 0.5 to 1.5
- ln2_bias: bfloat16 [1024], P('dp'), may hold values from -1.5 to 1.5
- w_up: bfloat16 [1024, 4096], P('dp', 'tensor'), may hold values from -0.1875 to 0.1875
- up_bias: bfloat16 [4096], P('dp'), may hold values from -1.5 to 1.5
- w_down: bfloat16 [4096, 1024], P('tensor', 'dp'), may hold values from -0.09375 to 0.09375
- down_bias: bfloat16 [1024], P('dp'), may hold values from -1.5 to 1.5
Outputs:
- out: bfloat16 [12288, 1024], P(('dp', 'tensor'))
- in_grad: float32 [12288, 1024], P(('dp', 'tensor'))
- grad_ln1_gain: float32 [1024], P('dp')
- grad_ln1_bias: float32 [1024], P('dp')
- grad_w_qkv: float32 [3, 1024, 1024], P(None, 'dp', 'tensor')
- grad_qv_bias: float32 [2, 1024], P(None, 'dp')
- grad_w_attn_out: float32 [1024, 1024], P('tensor', 'dp')
- grad_attn_out_bias: float32 [1024], P('dp')
- grad_ln2_gain: float32 [1024], P('dp')
- grad_ln2_bias: float32 [1024], P('dp')
- grad_w_up: float32 [1024, 4096], P('dp', 'tensor')
- grad_up_bias: float32 [4096], P('dp')
- grad_w_down: float32 [4096, 1024], P('tensor', 'dp')
- grad_down_bias: float32 [1024], P('dp')
The draws below stay inside these ranges and needn't reach their ends.
Inputs may be any that keep to these rules, and one draw needn't show every extreme that they name: With B = max(1, 0) and L = min(2 B, 2 - B), every tree has the same shape: segments 0 to 3 - B - L - 1 form a trunk in which each segment's parent is the one before it (parents[t, 0] = 0); the next B segments are branches whose parent is the last trunk segment; the last L segments are leaves, two a branch, whose parent is a branch. Which branch holds which pair of leaves varies from tree to tree.
All inputs are finite; a program needn't handle non-finite values.
Results may differ from the reference program's by a relative error of at most 0.014.
Values may be sent and summed in bfloat16 or wider, within the bound.
No kernel may reach another device: no remote copies, remote signals or barrier semaphores. Data moves between devices by JAX's collectives and lax.ppermute only.
A program may use at most 128 MiB of HBM per device.

```python
import math
import jax
import jax.numpy as jnp
from jax import lax

D = 1024
HEADS = 16
FF = 4096
SEG = 256
HEAD_DIM = 64
TREE_TOK = 768
SEGS = 3
TREES = 16
TOKENS = 12288


def draw_parents(key, part):
    branches = max(1, SEGS // 5)
    leaves = min(2 * branches, SEGS - 1 - branches)
    trunk = SEGS - branches - leaves
    tree_keys = jax.random.split(key, TREES)
    orders = jax.vmap(lambda one_key: jax.random.permutation(one_key, branches))(tree_keys).astype(jnp.int32)
    positions = jnp.arange(SEGS, dtype=jnp.int32)
    trunk_parent = jnp.maximum(positions - 1, 0)
    branch_parent = jnp.full((SEGS,), trunk - 1, jnp.int32)
    leaf_index = jnp.clip((positions - trunk - branches) // 2, 0, branches - 1)
    leaf_parent = trunk + orders[:, leaf_index]
    picks = jnp.where(positions[None, :] < trunk, trunk_parent[None, :], jnp.where(positions[None, :] < trunk + branches, branch_parent[None, :], leaf_parent))
    return picks.astype(jnp.int32)


def level_of(own_key, shape, cuts, least, top_value):
    loudness = 1.0
    for position, blocks in cuts:
        draws = jax.random.uniform(jax.random.fold_in(jax.random.fold_in(own_key, 6), position), (blocks,), jnp.float32, least / len(cuts), top_value / len(cuts))
        loudness = loudness * jnp.repeat(jnp.exp(draws), shape[position] // blocks).reshape((-1,) + (1,) * (len(shape) - 1 - position))
    return loudness


def gaussian(rng, dims, width, bound, shards=(), kind=jnp.bfloat16):
    values = jax.random.normal(rng, dims, jnp.float32) * width
    if len(shards) > 0:
        values = level_of(rng, dims, shards, -0.22, 0.18) * values
    return jnp.clip(values, min=-bound, max=bound).astype(kind)


def setup_inputs(seed: int = 0) -> dict:
    key_of = jax.random.split(jax.random.key(seed), 16)
    return {
        "inputs": gaussian(key_of[0], (TOKENS, D), 1.0, 6.0, ((0, 32),)),
        "out_grad": gaussian(key_of[1], (TOKENS, D), 1.0, 6.0, ((0, 32),)),
        "parents": draw_parents(jax.random.fold_in(key_of[15], 71), 0),
        "ln1_gain": jnp.clip(1.0 + 0.1 * jax.random.normal(key_of[3], (D,), jnp.float32), 0.5, 1.5).astype(jnp.bfloat16),
        "ln1_bias": gaussian(key_of[4], (D,), 0.3, 1.5, ((0, 16),)),
        "w_qkv": gaussian(key_of[5], (3, D, D), (D // 2) ** -0.5, 0.25, ((1, 16), (2, 2))),
        "qv_bias": gaussian(key_of[6], (2, D), 0.3, 1.5, ((1, 16),)),
        "w_attn_out": gaussian(key_of[7], (D, D), (D // 16) ** -0.5, 0.75, ((0, 2), (1, 16))),
        "attn_out_bias": gaussian(key_of[8], (D,), 0.3, 1.5, ((0, 16),)),
        "ln2_gain": jnp.clip(1.0 + 0.1 * jax.random.normal(key_of[9], (D,), jnp.float32), 0.5, 1.5).astype(jnp.bfloat16),
        "ln2_bias": gaussian(key_of[10], (D,), 0.3, 1.5, ((0, 16),)),
        "w_up": gaussian(key_of[11], (D, FF), D ** -0.5, 0.1875, ((0, 16), (1, 2))),
        "up_bias": gaussian(key_of[12], (FF,), 0.3, 1.5, ((0, 16),)),
        "w_down": gaussian(key_of[13], (FF, D), FF ** -0.5, 0.09375, ((0, 2), (1, 16))),
        "down_bias": gaussian(key_of[14], (D,), 0.3, 1.5, ((0, 16),)),
    }


@jax.custom_vjp
def low(v):
    return lax.optimization_barrier(v.astype(jnp.bfloat16)).astype(jnp.float32)

@jax.custom_vjp
def low_back(v):
    return v

def low_keep(v):
    return (low(v), None)

def low_pass(kept, grad):
    return (grad,)

def back_keep(v):
    return (v, None)

def back_low(kept, grad):
    return (low(grad),)
low.defvjp(low_keep, low_pass)
low_back.defvjp(back_keep, back_low)
epsilon = 1e-05
gelu_coef = 0.7978845608028654

def highest(left, right):
    return jnp.dot(left, right, precision=lax.Precision.HIGHEST)

def layer_norm(values, scales, shifts):
    centre = lax.optimization_barrier(jnp.mean(values, axis=-1, keepdims=True))
    shifted = values - centre
    spread = lax.optimization_barrier(jnp.mean(shifted * shifted, axis=-1, keepdims=True))
    return shifted * lax.rsqrt(spread + epsilon) * scales + shifts

def gelu_tanh(values):
    return 0.5 * values * (1.0 + jnp.tanh(gelu_coef * (values + 0.044715 * values * values * values)))

def ancestors(parent_row, segment_count):
    labels = jnp.arange(segment_count, dtype=jnp.int32)
    links = ((parent_row[:, None] == labels[None, :]) & (labels[:, None] > 0)).astype(jnp.float32)
    identity = jnp.eye(segment_count, dtype=jnp.float32)

    def extend(turn, reached):
        return jnp.minimum(identity + highest(links, reached), 1.0)
    return lax.fori_loop(0, segment_count, extend, identity)

def tree_mask(reached, first_row, block_rows, length):
    query_pos = first_row + jnp.arange(block_rows, dtype=jnp.int32)
    key_pos = jnp.arange(length, dtype=jnp.int32)
    segment_count = reached.shape[0]
    onehot = ((query_pos // SEG)[:, None] == jnp.arange(segment_count, dtype=jnp.int32)[None, :]).astype(jnp.float32)
    row_reach = highest(onehot, reached)
    spread_out = jnp.repeat(row_reach, SEG, axis=1)
    return (spread_out > 0.5) & (key_pos[None, :] <= query_pos[:, None])

def row_block(length):
    pieces = -(-length // 512)
    while length % pieces:
        pieces += 1
    return length // pieces

def tree_layer(weights, hidden_in, reached):
    gain_one, shift_one, w_proj, proj_bias, w_out, out_bias, gain_two, shift_two, w_hidden, hidden_bias, w_back, back_bias = weights
    length = hidden_in.shape[0]
    scale = 1.0 / math.sqrt(HEAD_DIM)
    norm_one = low(layer_norm(hidden_in, gain_one, shift_one))
    queries = low(low_back(highest(norm_one, w_proj[0]) + proj_bias[0]))
    keys_all = low(low_back(highest(norm_one, w_proj[1])))
    values_all = low(low_back(highest(norm_one, w_proj[2]) + proj_bias[1]))
    query_heads = queries.reshape(length, HEADS, HEAD_DIM)
    key_heads = keys_all.reshape(length, HEADS, HEAD_DIM)
    value_heads = values_all.reshape(length, HEADS, HEAD_DIM)
    block_rows = row_block(length)
    starts = jnp.arange(length // block_rows, dtype=jnp.int32) * block_rows

    def attend(first_row):
        query_block = lax.dynamic_slice_in_dim(query_heads, first_row, block_rows, 0)
        scores = jnp.einsum('qhd,khd->hqk', query_block, key_heads, precision=lax.Precision.HIGHEST) * scale
        scores = low_back(scores)
        allowed = tree_mask(reached, first_row, block_rows, length)
        scores = jnp.where(allowed[None], scores, -1e+30)
        top_score = lax.optimization_barrier(jnp.max(scores, axis=-1, keepdims=True))
        expo = jnp.exp(scores - top_score)
        probs = expo / lax.optimization_barrier(jnp.sum(expo, axis=-1, keepdims=True))
        return jnp.einsum('hqk,khd->qhd', low(probs), value_heads, precision=lax.Precision.HIGHEST)
    attended = lax.map(jax.checkpoint(attend), starts).reshape(length, HEADS * HEAD_DIM)
    attended = low(low_back(attended))
    branch = low_back(highest(attended, w_out) + out_bias)
    resid = hidden_in + branch
    norm_two = low(layer_norm(resid, gain_two, shift_two))
    pre = low_back(highest(norm_two, w_hidden) + hidden_bias)
    act = low(gelu_tanh(pre))
    return resid + highest(act, w_back) + back_bias

def reference(inputs, out_grad, parents, ln1_gain, ln1_bias, w_qkv, qv_bias, w_attn_out, attn_out_bias, ln2_gain, ln2_bias, w_up, up_bias, w_down, down_bias):
    weights = tuple((w.astype(jnp.float32) for w in (ln1_gain, ln1_bias, w_qkv, qv_bias, w_attn_out, attn_out_bias, ln2_gain, ln2_bias, w_up, up_bias, w_down, down_bias)))
    tree_inputs = inputs.astype(jnp.float32).reshape(TREES, TREE_TOK, D)
    tree_grads = out_grad.astype(jnp.float32).reshape(TREES, TREE_TOK, D)

    def per_tree(totals, element):
        hidden_in, cotangent, parent_row = element
        reached = ancestors(parent_row, SEGS)
        result, pull_back = jax.vjp(lambda wts, rows: tree_layer(wts, rows, reached), weights, hidden_in)
        weight_grads, input_grad = pull_back(cotangent)
        totals = jax.tree.map(jnp.add, totals, weight_grads)
        return (totals, (result.astype(jnp.bfloat16), input_grad))
    zeros_start = jax.tree.map(jnp.zeros_like, weights)
    totals, (results, input_grads) = lax.scan(per_tree, zeros_start, (tree_inputs, tree_grads, parents))
    return (results.reshape(TOKENS, D), input_grads.reshape(TOKENS, D), totals[0], totals[1], totals[2], totals[3], totals[4], totals[5], totals[6], totals[7], totals[8], totals[9], totals[10], totals[11])
```

```python
import functools
import math

import jax
import jax.numpy as jnp
from jax import lax
from jax.experimental import pallas as pl
from jax.experimental.pallas import tpu as pltpu
from jax.sharding import PartitionSpec as P

HEADS = 16
SEG = 256


epsilon = 1e-05
gelu_coef = 0.7978845608028654


def layer_norm(values, scales, shifts):
    centre = jnp.mean(values, axis=-1, keepdims=True)
    shifted = values - centre
    spread = jnp.mean(shifted * shifted, axis=-1, keepdims=True)
    return shifted * lax.rsqrt(spread + epsilon) * scales + shifts


def gelu_tanh(values):
    return (
        0.5 * values * (1.0 + jnp.tanh(gelu_coef * (values + 0.044715 * values * values * values)))
    )


def matmul(left, right):
    return jnp.dot(left, right, preferred_element_type=jnp.float32)


def contract_rows(left, right):
    return lax.dot_general(
        left, right, (((0,), (0,)), ((), ())), preferred_element_type=jnp.float32
    )


def contract_last(left, right):
    return lax.dot_general(
        left, right, (((1,), (1,)), ((), ())), preferred_element_type=jnp.float32
    )


def ancestors(parent_row, segment_count):
    labels = jnp.arange(segment_count, dtype=jnp.int32)
    links = ((parent_row[:, None] == labels[None, :]) & (labels[:, None] > 0)).astype(jnp.float32)
    identity = jnp.eye(segment_count, dtype=jnp.float32)

    def extend(turn, reached):
        grown = jnp.dot(
            links, reached, precision=lax.Precision.HIGHEST, preferred_element_type=jnp.float32
        )
        return jnp.minimum(identity + grown, 1.0)

    return lax.fori_loop(0, segment_count, extend, identity)


def tree_mask(reached, first_row, block_rows, length):
    query_pos = first_row + jnp.arange(block_rows, dtype=jnp.int32)
    key_pos = jnp.arange(length, dtype=jnp.int32)
    segment_count = reached.shape[0]
    onehot = (
        (query_pos // SEG)[:, None] == jnp.arange(segment_count, dtype=jnp.int32)[None, :]
    ).astype(jnp.float32)
    row_reach = jnp.dot(
        onehot, reached, precision=lax.Precision.HIGHEST, preferred_element_type=jnp.float32
    )
    spread_out = jnp.repeat(row_reach, SEG, axis=1)
    return (spread_out > 0.5) & (key_pos[None, :] <= query_pos[:, None])


def row_block(length):
    pieces = -(-length // 512)
    while length % pieces:
        pieces += 1
    return length // pieces


def place_block(local_vec, full_length, offset):
    empty_vec = jnp.zeros(local_vec.shape[:-1] + (full_length,), jnp.float32)
    return lax.dynamic_update_slice_in_dim(empty_vec, local_vec, offset, local_vec.ndim - 1)


def generic(
    inputs,
    out_grad,
    parents,
    ln1_gain,
    ln1_bias,
    w_qkv,
    qv_bias,
    w_attn_out,
    attn_out_bias,
    ln2_gain,
    ln2_bias,
    w_up,
    up_bias,
    w_down,
    down_bias,
):
    tensor_ranks = lax.axis_size("tensor")
    tensor_rank = lax.axis_index("tensor")
    rows_own = inputs.shape[0]
    length = rows_own * tensor_ranks
    model_width = inputs.shape[1]
    head_dim = model_width // HEADS
    local_width = w_qkv.shape[2]
    local_hidden = w_up.shape[1]
    heads_here = local_width // head_dim
    scale = 1.0 / math.sqrt(head_dim)
    gathered = (
        lax.all_gather(w_qkv, "dp", axis=1, tiled=True),
        lax.all_gather(w_attn_out, "dp", axis=1, tiled=True),
        lax.all_gather(w_up, "dp", axis=0, tiled=True),
        lax.all_gather(w_down, "dp", axis=1, tiled=True),
        lax.all_gather(ln1_gain, "dp", axis=0, tiled=True),
        lax.all_gather(ln1_bias, "dp", axis=0, tiled=True),
        lax.all_gather(qv_bias, "dp", axis=1, tiled=True),
        lax.all_gather(attn_out_bias, "dp", axis=0, tiled=True),
        lax.all_gather(ln2_gain, "dp", axis=0, tiled=True),
        lax.all_gather(ln2_bias, "dp", axis=0, tiled=True),
        lax.all_gather(up_bias, "dp", axis=0, tiled=True),
        lax.all_gather(down_bias, "dp", axis=0, tiled=True),
    )
    proj_full, out_full, hidden_full, back_full = (
        gathered[0],
        gathered[1],
        gathered[2],
        gathered[3],
    )
    gain_one = gathered[4].astype(jnp.float32)
    shift_one = gathered[5].astype(jnp.float32)
    proj_bias = lax.dynamic_slice_in_dim(
        gathered[6].astype(jnp.float32), tensor_rank * local_width, local_width, 1
    )
    out_bias = gathered[7].astype(jnp.float32)
    gain_two = gathered[8].astype(jnp.float32)
    shift_two = gathered[9].astype(jnp.float32)
    hidden_bias_full = gathered[10].astype(jnp.float32)
    back_bias = gathered[11].astype(jnp.float32)
    full_hidden = hidden_bias_full.shape[0]
    hidden_in = inputs.astype(jnp.float32)
    norm_one, ln1_pull = jax.vjp(layer_norm, hidden_in, gain_one, shift_one)
    norm_one_all = lax.all_gather(norm_one.astype(jnp.bfloat16), "tensor", axis=0, tiled=True)
    queries = (matmul(norm_one_all, proj_full[0]) + proj_bias[0]).astype(jnp.bfloat16)
    keys_low = matmul(norm_one_all, proj_full[1]).astype(jnp.bfloat16)
    values_low = (matmul(norm_one_all, proj_full[2]) + proj_bias[1]).astype(jnp.bfloat16)
    reached = ancestors(parents[0], length // SEG)
    block_rows = row_block(length)
    num_blocks = length // block_rows
    starts = jnp.arange(num_blocks, dtype=jnp.int32) * block_rows
    query_blocks = queries.reshape(num_blocks, block_rows, heads_here, head_dim)
    key_heads = keys_low.reshape(length, heads_here, head_dim)
    value_heads = values_low.reshape(length, heads_here, head_dim)

    def block_scores(query_block, first_row):
        scores = (
            jnp.einsum("qhd,khd->hqk", query_block, key_heads, preferred_element_type=jnp.float32)
            * scale
        )
        allowed = tree_mask(reached, first_row, block_rows, length)
        return jnp.where(allowed[None], scores, -1e30)

    def forward_block(element):
        query_block, first_row = element
        scores = block_scores(query_block, first_row)
        top_score = jnp.max(scores, axis=-1, keepdims=True)
        expo = jnp.exp(scores - top_score)
        totals = jnp.sum(expo, axis=-1, keepdims=True)
        probs = (expo / totals).astype(jnp.bfloat16)
        attended_block = jnp.einsum(
            "hqk,khd->qhd", probs, value_heads, preferred_element_type=jnp.float32
        )
        return (attended_block, (top_score + jnp.log(totals))[..., 0])

    attended_blocks, log_totals = lax.map(forward_block, (query_blocks, starts))
    attended = attended_blocks.reshape(length, local_width).astype(jnp.bfloat16)
    branch = (
        lax.psum_scatter(matmul(attended, out_full), "tensor", scatter_dimension=0, tiled=True)
        + out_bias
    )
    resid = hidden_in + branch
    norm_two, ln2_pull = jax.vjp(layer_norm, resid, gain_two, shift_two)
    norm_two_low = norm_two.astype(jnp.bfloat16)
    grad_back_bias = jnp.sum(out_grad.astype(jnp.float32), axis=0)
    norm_two_all = lax.all_gather(norm_two_low, "tensor", axis=0, tiled=True)
    hidden_slice = lax.dynamic_slice_in_dim(
        hidden_bias_full, tensor_rank * local_hidden, local_hidden, 0
    )
    pre = matmul(norm_two_all, hidden_full) + hidden_slice
    act, gelu_pull = jax.vjp(gelu_tanh, pre)
    act_low = act.astype(jnp.bfloat16)
    mixed = (
        lax.psum_scatter(
            matmul(act_low, back_full).astype(jnp.bfloat16),
            "tensor",
            scatter_dimension=0,
            tiled=True,
        ).astype(jnp.float32)
        + back_bias
    )
    cotangent_all = lax.all_gather(out_grad, "tensor", axis=0, tiled=True)
    grad_back = contract_rows(act_low, cotangent_all)
    (dpre,) = gelu_pull(contract_last(cotangent_all, back_full))
    dpre_low = dpre.astype(jnp.bfloat16)
    grad_hidden = contract_rows(norm_two_all, dpre_low)
    grad_hidden_bias = place_block(
        jnp.sum(dpre_low.astype(jnp.float32), axis=0), full_hidden, tensor_rank * local_hidden
    )
    dnorm_two = lax.psum_scatter(
        contract_last(dpre_low, hidden_full), "tensor", scatter_dimension=0, tiled=True
    )
    result = (resid + mixed).astype(jnp.bfloat16)
    dresid_part, grad_gain_two, grad_shift_two = ln2_pull(dnorm_two)
    dresid = out_grad.astype(jnp.float32) + dresid_part
    dbranch = dresid.astype(jnp.bfloat16)
    grad_out_bias = jnp.sum(dbranch.astype(jnp.float32), axis=0)
    dbranch_all = lax.all_gather(dbranch, "tensor", axis=0, tiled=True)
    grad_out = contract_rows(attended, dbranch_all)
    dattended = contract_last(dbranch_all, out_full).astype(jnp.bfloat16)
    dattended_blocks = dattended.reshape(num_blocks, block_rows, heads_here, head_dim)

    def backward_block(carry, element):
        dkey_acc, dvalue_acc = carry
        query_block, dattended_block, log_block, first_row = element
        scores = block_scores(query_block, first_row)
        probs = jnp.exp(scores - log_block[..., None])
        dvalue_acc = dvalue_acc + jnp.einsum(
            "hqk,qhd->khd",
            probs.astype(jnp.bfloat16),
            dattended_block,
            preferred_element_type=jnp.float32,
        )
        dprobs = jnp.einsum(
            "qhd,khd->hqk", dattended_block, value_heads, preferred_element_type=jnp.float32
        )
        dscores = probs * (dprobs - jnp.sum(dprobs * probs, axis=-1, keepdims=True))
        dscores_low = dscores.astype(jnp.bfloat16)
        dquery_block = (
            jnp.einsum("hqk,khd->qhd", dscores_low, key_heads, preferred_element_type=jnp.float32)
            * scale
        )
        dkey_acc = (
            dkey_acc
            + jnp.einsum(
                "hqk,qhd->khd", dscores_low, query_block, preferred_element_type=jnp.float32
            )
            * scale
        )
        return ((dkey_acc, dvalue_acc), dquery_block)

    zero_heads = jnp.zeros((length, heads_here, head_dim), jnp.float32)
    (dkey_acc, dvalue_acc), dquery_blocks = lax.scan(
        backward_block,
        (zero_heads, zero_heads),
        (query_blocks, dattended_blocks, log_totals, starts),
    )
    dqueries = dquery_blocks.reshape(length, local_width).astype(jnp.bfloat16)
    dkeys = dkey_acc.reshape(length, local_width).astype(jnp.bfloat16)
    dvalues = dvalue_acc.reshape(length, local_width).astype(jnp.bfloat16)
    grad_proj = jnp.stack(
        [
            contract_rows(norm_one_all, dqueries),
            contract_rows(norm_one_all, dkeys),
            contract_rows(norm_one_all, dvalues),
        ]
    )
    local_bias_grad = jnp.stack(
        [
            jnp.sum(dqueries.astype(jnp.float32), axis=0),
            jnp.sum(dvalues.astype(jnp.float32), axis=0),
        ]
    )
    grad_proj_bias = place_block(local_bias_grad, model_width, tensor_rank * local_width)
    dnorm_one = lax.psum_scatter(
        (
            contract_last(dqueries, proj_full[0])
            + contract_last(dkeys, proj_full[1])
            + contract_last(dvalues, proj_full[2])
        ).astype(jnp.bfloat16),
        "tensor",
        scatter_dimension=0,
        tiled=True,
    ).astype(jnp.float32)
    dinput_part, grad_gain_one, grad_shift_one = ln1_pull(dnorm_one)
    input_grad = dresid + dinput_part
    summed = (
        lax.psum_scatter(grad_proj, "dp", scatter_dimension=1, tiled=True),
        lax.psum_scatter(grad_out, "dp", scatter_dimension=1, tiled=True),
        lax.psum_scatter(grad_hidden, "dp", scatter_dimension=0, tiled=True),
        lax.psum_scatter(grad_back, "dp", scatter_dimension=1, tiled=True),
        lax.psum_scatter(grad_gain_one, "dp", scatter_dimension=0, tiled=True),
        lax.psum_scatter(grad_shift_one, "dp", scatter_dimension=0, tiled=True),
        lax.psum_scatter(grad_proj_bias, "dp", scatter_dimension=1, tiled=True),
        lax.psum_scatter(grad_out_bias, "dp", scatter_dimension=0, tiled=True),
        lax.psum_scatter(grad_gain_two, "dp", scatter_dimension=0, tiled=True),
        lax.psum_scatter(grad_shift_two, "dp", scatter_dimension=0, tiled=True),
        lax.psum_scatter(grad_hidden_bias, "dp", scatter_dimension=0, tiled=True),
        lax.psum_scatter(grad_back_bias, "dp", scatter_dimension=0, tiled=True),
    )
    vectors = lax.psum(
        (summed[4], summed[5], summed[6], summed[7], summed[8], summed[9], summed[10], summed[11]),
        "tensor",
    )
    return (
        result,
        input_grad,
        vectors[0],
        vectors[1],
        summed[0],
        vectors[2],
        summed[1],
        vectors[3],
        vectors[4],
        vectors[5],
        summed[2],
        vectors[6],
        summed[3],
        vectors[7],
    )


def attend_kernel(qkv_ref, out_ref, log_ref, *, scale):
    length = qkv_ref.shape[0]
    lane = lax.broadcasted_iota(jnp.int32, (SEG, 128), 1)
    key = qkv_ref[:, 128:256]
    value_t = jnp.transpose(qkv_ref[:, 256:384])
    for seg in range(length // SEG):
        keys_here = (seg + 1) * SEG
        query = qkv_ref[seg * SEG : keys_here, 0:128] * scale
        key_pos = lax.broadcasted_iota(jnp.int32, (keys_here, SEG), 0)
        query_pos = lax.broadcasted_iota(jnp.int32, (keys_here, SEG), 1) + seg * SEG
        parts = []
        for head in range(2):
            mine = jnp.where(lane // 64 == head, query, jnp.zeros_like(query))
            scores = contract_last(key[:keys_here], mine)
            scores = jnp.where(key_pos <= query_pos, scores, -1e30)
            top = jnp.max(scores, axis=0, keepdims=True)
            expo = jnp.exp(scores - top)
            total = jnp.sum(expo, axis=0, keepdims=True)
            mixed = matmul(
                value_t[head * 64 : head * 64 + 64, :keys_here], expo.astype(jnp.bfloat16)
            )
            parts.append(mixed / total)
            log_ref[0, head : head + 1, seg * SEG : keys_here] = top + jnp.log(total)
        out_ref[seg * SEG : keys_here, :] = jnp.transpose(jnp.concatenate(parts, axis=0)).astype(
            jnp.bfloat16
        )


def attend(qkv, scale):
    length, width = qkv.shape
    pairs = width // 384
    return pl.pallas_call(
        functools.partial(attend_kernel, scale=scale),
        grid=(pairs,),
        in_specs=[pl.BlockSpec((length, 384), lambda p: (0, p))],
        out_specs=[
            pl.BlockSpec((length, 128), lambda p: (0, p)),
            pl.BlockSpec((1, 8, length), lambda p: (p, 0, 0)),
        ],
        out_shape=[
            jax.ShapeDtypeStruct((length, pairs * 128), jnp.bfloat16),
            jax.ShapeDtypeStruct((pairs, 8, length), jnp.float32),
        ],
        compiler_params=pltpu.CompilerParams(vmem_limit_bytes=48 * 2**20),
        name="attend",
    )(qkv)


def attend_back_kernel(qkv_ref, grad_ref, log_ref, out_ref, dkey_ref, dvalue_ref, *, scale):
    length = qkv_ref.shape[0]
    lane = lax.broadcasted_iota(jnp.int32, (SEG, 128), 1)
    key = qkv_ref[:, 128:256]
    value = qkv_ref[:, 256:384]
    key_t = jnp.transpose(key)
    dkey_ref[...] = jnp.zeros_like(dkey_ref)
    dvalue_ref[...] = jnp.zeros_like(dvalue_ref)
    for seg in range(length // SEG):
        keys_here = (seg + 1) * SEG
        rows = slice(seg * SEG, keys_here)
        query = qkv_ref[rows, 0:128] * scale
        grad = grad_ref[rows, :]
        key_pos = lax.broadcasted_iota(jnp.int32, (keys_here, SEG), 0)
        query_pos = lax.broadcasted_iota(jnp.int32, (keys_here, SEG), 1) + seg * SEG
        parts = []
        dkey = jnp.zeros((keys_here, 128), jnp.float32)
        dvalue = jnp.zeros((keys_here, 128), jnp.float32)
        for head in range(2):
            here = lane // 64 == head
            query_mine = jnp.where(here, query, jnp.zeros_like(query))
            grad_mine = jnp.where(here, grad, jnp.zeros_like(grad))
            scores = contract_last(key[:keys_here], query_mine)
            scores = jnp.where(key_pos <= query_pos, scores, -1e30)
            probs = jnp.exp(scores - log_ref[0, head : head + 1, rows])
            dprobs = contract_last(value[:keys_here], grad_mine)
            mean = jnp.sum(probs * dprobs, axis=0, keepdims=True)
            dscores = (probs * (dprobs - mean)).astype(jnp.bfloat16)
            dvalue = dvalue + matmul(probs.astype(jnp.bfloat16), grad_mine)
            dkey = dkey + matmul(dscores, query_mine)
            parts.append(matmul(key_t[head * 64 : head * 64 + 64, :keys_here], dscores) * scale)
        dkey_ref[:keys_here, :] += dkey
        dvalue_ref[:keys_here, :] += dvalue
        out_ref[rows, 0:128] = jnp.transpose(jnp.concatenate(parts, axis=0)).astype(jnp.bfloat16)
    out_ref[:, 128:256] = dkey_ref[...].astype(jnp.bfloat16)
    out_ref[:, 256:384] = dvalue_ref[...].astype(jnp.bfloat16)


def attend_back(qkv, grad, logs, scale):
    length, width = qkv.shape
    pairs = width // 384
    return pl.pallas_call(
        functools.partial(attend_back_kernel, scale=scale),
        grid=(pairs,),
        in_specs=[
            pl.BlockSpec((length, 384), lambda p: (0, p)),
            pl.BlockSpec((length, 128), lambda p: (0, p)),
            pl.BlockSpec((1, 8, length), lambda p: (p, 0, 0)),
        ],
        out_specs=pl.BlockSpec((length, 384), lambda p: (0, p)),
        out_shape=jax.ShapeDtypeStruct((length, width), jnp.bfloat16),
        scratch_shapes=[
            pltpu.VMEM((length, 128), jnp.float32),
            pltpu.VMEM((length, 128), jnp.float32),
        ],
        compiler_params=pltpu.CompilerParams(vmem_limit_bytes=48 * 2**20),
        name="attend_back",
    )(qkv, grad, logs)


def dp_shift(value, ranks, dz, dy, dc):
    far, near = 4, ranks // 8

    def goes(rank):
        z, y, c = rank // (near * 2), rank // 2 % near, rank % 2
        return ((z + dz) % far * near + (y + dy) % near) * 2 + (c + dc) % 2

    return lax.ppermute(value, "dp", [(rank, goes(rank)) for rank in range(ranks)])


def dp_gather(shard, ranks):
    near = ranks // 8
    pieces = [shard] + [dp_shift(shard, ranks, k, 0, 0) for k in (1, 2, 3)]
    for step in range(1, near):
        pieces = pieces + [dp_shift(piece, ranks, 0, step, 0) for piece in pieces[:4]]
    half = jnp.concatenate(pieces, axis=0)
    return jnp.concatenate([half, dp_shift(half, ranks, 0, 0, 1)], axis=0)


def dp_reduce(grads, ranks, wire):
    near = ranks // 8
    half = grads.shape[0] // 2
    other = dp_shift(grads[half:].astype(wire), ranks, 0, 0, 1)
    mine = grads[:half].astype(jnp.float32) + other.astype(jnp.float32)
    part = half // near
    total = mine[:part]
    for step in range(1, near):
        sent = mine[step * part : (step + 1) * part].astype(wire)
        total = total + dp_shift(sent, ranks, 0, -step, 0).astype(jnp.float32)
    rows = part // 4
    low = total[rows:].astype(wire)
    result = total[:rows]
    for k in (1, 2, 3):
        result = result + dp_shift(low[(k - 1) * rows : k * rows], ranks, -k, 0, 0).astype(
            jnp.float32
        )
    return result


def swap(value):
    return lax.ppermute(value, "tensor", [(0, 1), (1, 0)])


def paired(
    inputs,
    out_grad,
    parents,
    ln1_gain,
    ln1_bias,
    w_qkv,
    qv_bias,
    w_attn_out,
    attn_out_bias,
    ln2_gain,
    ln2_bias,
    w_up,
    up_bias,
    w_down,
    down_bias,
):
    ranks = lax.axis_size("dp")
    near = ranks // 8
    rank = lax.axis_index("dp")
    side = lax.axis_index("tensor")
    rows, width = inputs.shape
    length = 2 * rows
    shard = width // ranks
    heads_width = w_qkv.shape[2]
    pairs = heads_width // 128
    hidden = w_up.shape[1]
    head_dim = width // HEADS
    scale = 1.0 / math.sqrt(head_dim)
    low = jnp.bfloat16

    slots = jnp.arange(ranks, dtype=jnp.int32)
    core_step, near_step, far_step = slots // (ranks // 2), slots // 4 % near, slots % 4
    my_z, my_y, my_c = rank // (2 * near), rank // 2 % near, rank % 2
    source = ((my_z - far_step) % 4 * near + (my_y - near_step) % near) * 2 + (
        my_c + core_step
    ) % 2
    feature = jnp.repeat(source * shard, shard) + jnp.tile(
        jnp.arange(shard, dtype=jnp.int32), ranks
    )
    to_local = (jnp.arange(width, dtype=jnp.int32)[:, None] == feature[None, :]).astype(low)
    slot_of = (slots[:, None] == source[None, :]).astype(jnp.float32)

    inputs_other = swap(inputs)
    grad_other = swap(out_grad)

    proj_shard = (
        w_qkv.reshape(3, shard, pairs, 128).transpose(1, 2, 0, 3).reshape(shard, 3 * heads_width)
    )
    vectors = jnp.concatenate(
        [ln1_gain, ln1_bias, attn_out_bias, ln2_gain, ln2_bias, down_bias]
        + [qv_bias.reshape(-1), up_bias]
    )
    vector_rows = jnp.pad(vectors, (0, 8 * 3 * heads_width - vectors.shape[0])).reshape(8, -1)
    first = dp_gather(jnp.concatenate([proj_shard, vector_rows], axis=0), ranks)
    first = first.reshape(ranks, shard + 8, 3 * heads_width)
    proj_full = first[:, :shard].reshape(width, 3 * heads_width)
    vector_full = first[:, shard:].reshape(ranks, -1)[:, : vectors.shape[0]].astype(jnp.float32)
    out_full = dp_gather(w_attn_out.T, ranks)
    hidden_full = dp_gather(w_up, ranks)
    back_full = dp_gather(w_down.T, ranks)

    gain_one, shift_one, out_bias, gain_two, shift_two, back_bias = (
        vector_full[:, i * shard : (i + 1) * shard].reshape(width) for i in range(6)
    )
    natural = jnp.dot(slot_of, vector_full[:, 6 * shard :], precision=lax.Precision.HIGHEST)
    query_bias = lax.dynamic_slice_in_dim(
        natural[:, :shard].reshape(width), side * heads_width, heads_width, 0
    )
    value_bias = lax.dynamic_slice_in_dim(
        natural[:, shard : 2 * shard].reshape(width), side * heads_width, heads_width, 0
    )
    hidden_bias = lax.dynamic_slice_in_dim(
        natural[:, 2 * shard :].reshape(-1), side * hidden, hidden, 0
    )
    proj_bias = jnp.stack(
        [
            query_bias.reshape(pairs, 128),
            jnp.zeros((pairs, 128), jnp.float32),
            value_bias.reshape(pairs, 128),
        ],
        axis=1,
    ).reshape(-1)

    def in_order(own, other):
        return jnp.where(
            side == 0,
            jnp.concatenate([own, other], axis=0),
            jnp.concatenate([other, own], axis=0),
        )

    def own_rows(value):
        return lax.dynamic_slice_in_dim(value, side * rows, rows, 0)

    def other_rows(value):
        return lax.dynamic_slice_in_dim(value, (1 - side) * rows, rows, 0)

    hidden_in = matmul(in_order(inputs, inputs_other), to_local)
    cotangent = matmul(in_order(out_grad, grad_other), to_local).astype(low)
    norm_one = layer_norm(hidden_in, gain_one, shift_one).astype(low)
    qkv = (matmul(norm_one, proj_full) + proj_bias).astype(low)
    attended, logs = attend(qkv, scale)
    share = contract_last(attended, out_full).astype(low)
    branch = share.astype(jnp.float32) + swap(share).astype(jnp.float32)
    resid = hidden_in + (branch + out_bias)
    norm_two, ln2_pull = jax.vjp(
        lambda v: layer_norm(v, gain_two, shift_two), resid
    )
    norm_two = norm_two.astype(low)
    pre = matmul(norm_two, hidden_full) + hidden_bias
    act, gelu_pull = jax.vjp(gelu_tanh, pre)
    act = act.astype(low)
    own_out = contract_last(own_rows(act), back_full)
    other_out = swap(contract_last(other_rows(act), back_full).astype(low))
    result = own_rows(resid) + (own_out + other_out.astype(jnp.float32)) + back_bias
    result = contract_last(result.astype(low), to_local).astype(low)
    (dpre,) = gelu_pull(matmul(cotangent, back_full))
    dpre = dpre.astype(low)
    dnorm_share = contract_last(dpre, hidden_full).astype(low)
    dnorm_two = dnorm_share.astype(jnp.float32) + swap(dnorm_share).astype(jnp.float32)
    grad_back = dp_reduce(contract_rows(cotangent, act), ranks, low).T
    grad_hidden = dp_reduce(contract_rows(norm_two, dpre), ranks, low)
    (dresid_part,) = ln2_pull(dnorm_two)
    dresid = cotangent.astype(jnp.float32) + dresid_part
    dbranch = dresid.astype(low)
    dattended = matmul(dbranch, out_full).astype(low)
    grad_out = dp_reduce(contract_rows(dbranch, attended), ranks, low).T
    dqkv = attend_back(qkv, dattended, logs, scale)
    own_dnorm = contract_last(own_rows(dqkv), proj_full)
    other_dnorm = swap(contract_last(other_rows(dqkv), proj_full).astype(low))
    dnorm_one = own_dnorm + other_dnorm.astype(jnp.float32)
    hidden_own = own_rows(hidden_in)
    _, ln1_pull = jax.vjp(layer_norm, hidden_own, gain_one, shift_one)
    dinput, grad_gain_one, grad_shift_one = ln1_pull(dnorm_one)
    input_grad = own_rows(dresid) + dinput
    input_grad = lax.dot_general(
        input_grad,
        to_local.astype(jnp.float32),
        (((1,), (1,)), ((), ())),
        precision=lax.Precision.HIGHEST,
        preferred_element_type=jnp.float32,
    )
    grad_proj = dp_reduce(contract_rows(norm_one, dqkv), ranks, low)
    grad_proj = grad_proj.reshape(shard, pairs, 3, 128).transpose(2, 0, 1, 3)
    grad_proj = grad_proj.reshape(3, shard, heads_width)

    resid_own = own_rows(resid)
    _, ln2_vec_pull = jax.vjp(lambda g, b: layer_norm(resid_own, g, b), gain_two, shift_two)
    grad_gain_two, grad_shift_two = ln2_vec_pull(own_rows(dnorm_two))
    grad_out_bias = jnp.sum(own_rows(dbranch).astype(jnp.float32), axis=0)
    grad_back_bias = jnp.sum(own_rows(cotangent).astype(jnp.float32), axis=0)
    dqkv_sum = jnp.sum(dqkv.astype(jnp.float32), axis=0).reshape(pairs, 3, 128)
    grad_query_bias = place_block(
        dqkv_sum[:, 0].reshape(heads_width), width, side * heads_width
    ).reshape(ranks, shard)
    grad_value_bias = place_block(
        dqkv_sum[:, 2].reshape(heads_width), width, side * heads_width
    ).reshape(ranks, shard)
    grad_hidden_bias = place_block(
        jnp.sum(dpre.astype(jnp.float32), axis=0), 2 * hidden, side * hidden
    ).reshape(ranks, -1)
    to_slot = lax.dot_general(
        slot_of,
        jnp.concatenate([grad_query_bias, grad_value_bias, grad_hidden_bias], axis=1),
        (((0,), (0,)), ((), ())),
        precision=lax.Precision.HIGHEST,
        preferred_element_type=jnp.float32,
    )
    pack = jnp.concatenate(
        [
            value.reshape(ranks, shard)
            for value in (
                grad_gain_one,
                grad_shift_one,
                grad_out_bias,
                grad_gain_two,
                grad_shift_two,
                grad_back_bias,
            )
        ]
        + [to_slot],
        axis=1,
    )
    pack = pack + swap(pack)
    pack = dp_reduce(pack, ranks, jnp.float32).reshape(-1)
    vector_grads = [pack[i * shard : (i + 1) * shard] for i in range(6)]
    return (
        result,
        input_grad,
        vector_grads[0],
        vector_grads[1],
        grad_proj,
        pack[6 * shard : 8 * shard].reshape(2, shard),
        grad_out,
        vector_grads[2],
        vector_grads[3],
        vector_grads[4],
        grad_hidden,
        pack[8 * shard :],
        grad_back,
        vector_grads[5],
    )


def local(*arrays):
    pairs_fit = lax.axis_size("tensor") == 2 and lax.axis_size("dp") % 8 == 0
    if pairs_fit and arrays[2].shape[1] == 3:
        return paired(*arrays)
    return generic(*arrays)


def solution(mesh):
    return jax.shard_map(
        local,
        mesh=mesh,
        in_specs=(
            P(("dp", "tensor"), None),
            P(("dp", "tensor"), None),
            P("dp", None),
            P("dp"),
            P("dp"),
            P(None, "dp", "tensor"),
            P(None, "dp"),
            P("tensor", "dp"),
            P("dp"),
            P("dp"),
            P("dp"),
            P("dp", "tensor"),
            P("dp"),
            P("tensor", "dp"),
            P("dp"),
        ),
        out_specs=(
            P(("dp", "tensor"), None),
            P(("dp", "tensor"), None),
            P("dp"),
            P("dp"),
            P(None, "dp", "tensor"),
            P(None, "dp"),
            P("tensor", "dp"),
            P("dp"),
            P("dp"),
            P("dp"),
            P("dp", "tensor"),
            P("dp"),
            P("tensor", "dp"),
            P("dp"),
        ),
        check_vma=False,
    )
```

```python
import functools
import math

import jax
import jax.numpy as jnp
from jax import lax
from jax.experimental import pallas as pl
from jax.experimental.pallas import tpu as pltpu
from jax.sharding import PartitionSpec as P

HEADS = 16
SEG = 256


epsilon = 1e-05
gelu_coef = 0.7978845608028654


def layer_norm(values, scales, shifts):
    centre = jnp.mean(values, axis=-1, keepdims=True)
    shifted = values - centre
    spread = jnp.mean(shifted * shifted, axis=-1, keepdims=True)
    return shifted * lax.rsqrt(spread + epsilon) * scales + shifts


def gelu_tanh(values):
    return (
        0.5 * values * (1.0 + jnp.tanh(gelu_coef * (values + 0.044715 * values * values * values)))
    )


def matmul(left, right):
    return jnp.dot(left, right, preferred_element_type=jnp.float32)


def contract_rows(left, right):
    return lax.dot_general(
        left, right, (((0,), (0,)), ((), ())), preferred_element_type=jnp.float32
    )


def contract_last(left, right):
    return lax.dot_general(
        left, right, (((1,), (1,)), ((), ())), preferred_element_type=jnp.float32
    )


def ancestors(parent_row, segment_count):
    labels = jnp.arange(segment_count, dtype=jnp.int32)
    links = ((parent_row[:, None] == labels[None, :]) & (labels[:, None] > 0)).astype(jnp.float32)
    identity = jnp.eye(segment_count, dtype=jnp.float32)

    def extend(turn, reached):
        grown = jnp.dot(
            links, reached, precision=lax.Precision.HIGHEST, preferred_element_type=jnp.float32
        )
        return jnp.minimum(identity + grown, 1.0)

    return lax.fori_loop(0, segment_count, extend, identity)


def tree_mask(reached, first_row, block_rows, length):
    query_pos = first_row + jnp.arange(block_rows, dtype=jnp.int32)
    key_pos = jnp.arange(length, dtype=jnp.int32)
    segment_count = reached.shape[0]
    onehot = (
        (query_pos // SEG)[:, None] == jnp.arange(segment_count, dtype=jnp.int32)[None, :]
    ).astype(jnp.float32)
    row_reach = jnp.dot(
        onehot, reached, precision=lax.Precision.HIGHEST, preferred_element_type=jnp.float32
    )
    spread_out = jnp.repeat(row_reach, SEG, axis=1)
    return (spread_out > 0.5) & (key_pos[None, :] <= query_pos[:, None])


def row_block(length):
    pieces = -(-length // 512)
    while length % pieces:
        pieces += 1
    return length // pieces


def place_block(local_vec, full_length, offset):
    empty_vec = jnp.zeros(local_vec.shape[:-1] + (full_length,), jnp.float32)
    return lax.dynamic_update_slice_in_dim(empty_vec, local_vec, offset, local_vec.ndim - 1)


def generic(
    inputs,
    out_grad,
    parents,
    ln1_gain,
    ln1_bias,
    w_qkv,
    qv_bias,
    w_attn_out,
    attn_out_bias,
    ln2_gain,
    ln2_bias,
    w_up,
    up_bias,
    w_down,
    down_bias,
):
    tensor_ranks = lax.axis_size("tensor")
    tensor_rank = lax.axis_index("tensor")
    rows_own = inputs.shape[0]
    length = rows_own * tensor_ranks
    model_width = inputs.shape[1]
    head_dim = model_width // HEADS
    local_width = w_qkv.shape[2]
    local_hidden = w_up.shape[1]
    heads_here = local_width // head_dim
    scale = 1.0 / math.sqrt(head_dim)
    gathered = (
        lax.all_gather(w_qkv, "dp", axis=1, tiled=True),
        lax.all_gather(w_attn_out, "dp", axis=1, tiled=True),
        lax.all_gather(w_up, "dp", axis=0, tiled=True),
        lax.all_gather(w_down, "dp", axis=1, tiled=True),
        lax.all_gather(ln1_gain, "dp", axis=0, tiled=True),
        lax.all_gather(ln1_bias, "dp", axis=0, tiled=True),
        lax.all_gather(qv_bias, "dp", axis=1, tiled=True),
        lax.all_gather(attn_out_bias, "dp", axis=0, tiled=True),
        lax.all_gather(ln2_gain, "dp", axis=0, tiled=True),
        lax.all_gather(ln2_bias, "dp", axis=0, tiled=True),
        lax.all_gather(up_bias, "dp", axis=0, tiled=True),
        lax.all_gather(down_bias, "dp", axis=0, tiled=True),
    )
    proj_full, out_full, hidden_full, back_full = (
        gathered[0],
        gathered[1],
        gathered[2],
        gathered[3],
    )
    gain_one = gathered[4].astype(jnp.float32)
    shift_one = gathered[5].astype(jnp.float32)
    proj_bias = lax.dynamic_slice_in_dim(
        gathered[6].astype(jnp.float32), tensor_rank * local_width, local_width, 1
    )
    out_bias = gathered[7].astype(jnp.float32)
    gain_two = gathered[8].astype(jnp.float32)
    shift_two = gathered[9].astype(jnp.float32)
    hidden_bias_full = gathered[10].astype(jnp.float32)
    back_bias = gathered[11].astype(jnp.float32)
    full_hidden = hidden_bias_full.shape[0]
    hidden_in = inputs.astype(jnp.float32)
    norm_one, ln1_pull = jax.vjp(layer_norm, hidden_in, gain_one, shift_one)
    norm_one_all = lax.all_gather(norm_one.astype(jnp.bfloat16), "tensor", axis=0, tiled=True)
    queries = (matmul(norm_one_all, proj_full[0]) + proj_bias[0]).astype(jnp.bfloat16)
    keys_low = matmul(norm_one_all, proj_full[1]).astype(jnp.bfloat16)
    values_low = (matmul(norm_one_all, proj_full[2]) + proj_bias[1]).astype(jnp.bfloat16)
    reached = ancestors(parents[0], length // SEG)
    block_rows = row_block(length)
    num_blocks = length // block_rows
    starts = jnp.arange(num_blocks, dtype=jnp.int32) * block_rows
    query_blocks = queries.reshape(num_blocks, block_rows, heads_here, head_dim)
    key_heads = keys_low.reshape(length, heads_here, head_dim)
    value_heads = values_low.reshape(length, heads_here, head_dim)

    def block_scores(query_block, first_row):
        scores = (
            jnp.einsum("qhd,khd->hqk", query_block, key_heads, preferred_element_type=jnp.float32)
            * scale
        )
        allowed = tree_mask(reached, first_row, block_rows, length)
        return jnp.where(allowed[None], scores, -1e30)

    def forward_block(element):
        query_block, first_row = element
        scores = block_scores(query_block, first_row)
        top_score = jnp.max(scores, axis=-1, keepdims=True)
        expo = jnp.exp(scores - top_score)
        totals = jnp.sum(expo, axis=-1, keepdims=True)
        probs = (expo / totals).astype(jnp.bfloat16)
        attended_block = jnp.einsum(
            "hqk,khd->qhd", probs, value_heads, preferred_element_type=jnp.float32
        )
        return (attended_block, (top_score + jnp.log(totals))[..., 0])

    attended_blocks, log_totals = lax.map(forward_block, (query_blocks, starts))
    attended = attended_blocks.reshape(length, local_width).astype(jnp.bfloat16)
    branch = (
        lax.psum_scatter(matmul(attended, out_full), "tensor", scatter_dimension=0, tiled=True)
        + out_bias
    )
    resid = hidden_in + branch
    norm_two, ln2_pull = jax.vjp(layer_norm, resid, gain_two, shift_two)
    norm_two_low = norm_two.astype(jnp.bfloat16)
    grad_back_bias = jnp.sum(out_grad.astype(jnp.float32), axis=0)
    norm_two_all = lax.all_gather(norm_two_low, "tensor", axis=0, tiled=True)
    hidden_slice = lax.dynamic_slice_in_dim(
        hidden_bias_full, tensor_rank * local_hidden, local_hidden, 0
    )
    pre = matmul(norm_two_all, hidden_full) + hidden_slice
    act, gelu_pull = jax.vjp(gelu_tanh, pre)
    act_low = act.astype(jnp.bfloat16)
    mixed = (
        lax.psum_scatter(
            matmul(act_low, back_full).astype(jnp.bfloat16),
            "tensor",
            scatter_dimension=0,
            tiled=True,
        ).astype(jnp.float32)
        + back_bias
    )
    cotangent_all = lax.all_gather(out_grad, "tensor", axis=0, tiled=True)
    grad_back = contract_rows(act_low, cotangent_all)
    (dpre,) = gelu_pull(contract_last(cotangent_all, back_full))
    dpre_low = dpre.astype(jnp.bfloat16)
    grad_hidden = contract_rows(norm_two_all, dpre_low)
    grad_hidden_bias = place_block(
        jnp.sum(dpre_low.astype(jnp.float32), axis=0), full_hidden, tensor_rank * local_hidden
    )
    dnorm_two = lax.psum_scatter(
        contract_last(dpre_low, hidden_full), "tensor", scatter_dimension=0, tiled=True
    )
    result = (resid + mixed).astype(jnp.bfloat16)
    dresid_part, grad_gain_two, grad_shift_two = ln2_pull(dnorm_two)
    dresid = out_grad.astype(jnp.float32) + dresid_part
    dbranch = dresid.astype(jnp.bfloat16)
    grad_out_bias = jnp.sum(dbranch.astype(jnp.float32), axis=0)
    dbranch_all = lax.all_gather(dbranch, "tensor", axis=0, tiled=True)
    grad_out = contract_rows(attended, dbranch_all)
    dattended = contract_last(dbranch_all, out_full).astype(jnp.bfloat16)
    dattended_blocks = dattended.reshape(num_blocks, block_rows, heads_here, head_dim)

    def backward_block(carry, element):
        dkey_acc, dvalue_acc = carry
        query_block, dattended_block, log_block, first_row = element
        scores = block_scores(query_block, first_row)
        probs = jnp.exp(scores - log_block[..., None])
        dvalue_acc = dvalue_acc + jnp.einsum(
            "hqk,qhd->khd",
            probs.astype(jnp.bfloat16),
            dattended_block,
            preferred_element_type=jnp.float32,
        )
        dprobs = jnp.einsum(
            "qhd,khd->hqk", dattended_block, value_heads, preferred_element_type=jnp.float32
        )
        dscores = probs * (dprobs - jnp.sum(dprobs * probs, axis=-1, keepdims=True))
        dscores_low = dscores.astype(jnp.bfloat16)
        dquery_block = (
            jnp.einsum("hqk,khd->qhd", dscores_low, key_heads, preferred_element_type=jnp.float32)
            * scale
        )
        dkey_acc = (
            dkey_acc
            + jnp.einsum(
                "hqk,qhd->khd", dscores_low, query_block, preferred_element_type=jnp.float32
            )
            * scale
        )
        return ((dkey_acc, dvalue_acc), dquery_block)

    zero_heads = jnp.zeros((length, heads_here, head_dim), jnp.float32)
    (dkey_acc, dvalue_acc), dquery_blocks = lax.scan(
        backward_block,
        (zero_heads, zero_heads),
        (query_blocks, dattended_blocks, log_totals, starts),
    )
    dqueries = dquery_blocks.reshape(length, local_width).astype(jnp.bfloat16)
    dkeys = dkey_acc.reshape(length, local_width).astype(jnp.bfloat16)
    dvalues = dvalue_acc.reshape(length, local_width).astype(jnp.bfloat16)
    grad_proj = jnp.stack(
        [
            contract_rows(norm_one_all, dqueries),
            contract_rows(norm_one_all, dkeys),
            contract_rows(norm_one_all, dvalues),
        ]
    )
    local_bias_grad = jnp.stack(
        [
            jnp.sum(dqueries.astype(jnp.float32), axis=0),
            jnp.sum(dvalues.astype(jnp.float32), axis=0),
        ]
    )
    grad_proj_bias = place_block(local_bias_grad, model_width, tensor_rank * local_width)
    dnorm_one = lax.psum_scatter(
        (
            contract_last(dqueries, proj_full[0])
            + contract_last(dkeys, proj_full[1])
            + contract_last(dvalues, proj_full[2])
        ).astype(jnp.bfloat16),
        "tensor",
        scatter_dimension=0,
        tiled=True,
    ).astype(jnp.float32)
    dinput_part, grad_gain_one, grad_shift_one = ln1_pull(dnorm_one)
    input_grad = dresid + dinput_part
    summed = (
        lax.psum_scatter(grad_proj, "dp", scatter_dimension=1, tiled=True),
        lax.psum_scatter(grad_out, "dp", scatter_dimension=1, tiled=True),
        lax.psum_scatter(grad_hidden, "dp", scatter_dimension=0, tiled=True),
        lax.psum_scatter(grad_back, "dp", scatter_dimension=1, tiled=True),
        lax.psum_scatter(grad_gain_one, "dp", scatter_dimension=0, tiled=True),
        lax.psum_scatter(grad_shift_one, "dp", scatter_dimension=0, tiled=True),
        lax.psum_scatter(grad_proj_bias, "dp", scatter_dimension=1, tiled=True),
        lax.psum_scatter(grad_out_bias, "dp", scatter_dimension=0, tiled=True),
        lax.psum_scatter(grad_gain_two, "dp", scatter_dimension=0, tiled=True),
        lax.psum_scatter(grad_shift_two, "dp", scatter_dimension=0, tiled=True),
        lax.psum_scatter(grad_hidden_bias, "dp", scatter_dimension=0, tiled=True),
        lax.psum_scatter(grad_back_bias, "dp", scatter_dimension=0, tiled=True),
    )
    vectors = lax.psum(
        (summed[4], summed[5], summed[6], summed[7], summed[8], summed[9], summed[10], summed[11]),
        "tensor",
    )
    return (
        result,
        input_grad,
        vectors[0],
        vectors[1],
        summed[0],
        vectors[2],
        summed[1],
        vectors[3],
        vectors[4],
        vectors[5],
        summed[2],
        vectors[6],
        summed[3],
        vectors[7],
    )


LOW = jnp.bfloat16
SLOT = 64


def settings():
    return pltpu.CompilerParams(vmem_limit_bytes=56 * 2**20)


def cost(flops, moved, exps=0):
    return pl.CostEstimate(
        flops=int(flops), bytes_accessed=int(moved), transcendentals=int(exps)
    )


def whole(shape):
    return pl.BlockSpec(shape, lambda *_: (0,) * len(shape))


def piece_specs(pieces, block, first=0):
    return [
        pl.BlockSpec((piece.shape[0], block), lambda p, *_: (0, first + p)) for piece in pieces
    ]


def fixed_specs(pieces, block, index):
    return [pl.BlockSpec((piece.shape[0], block), lambda *_: (0, index)) for piece in pieces]


def fill(scratch, refs):
    row = 0
    for ref in refs:
        scratch[row : row + ref.shape[0], :] = ref[...]
        row += ref.shape[0]


def fill_slots(place_ref, scratch, ref):
    for slot in range(scratch.shape[0] // SLOT):
        start = pl.multiple_of(place_ref[4 + slot] * SLOT, SLOT)
        scratch[slot * SLOT : slot * SLOT + SLOT, :] = ref[pl.ds(start, SLOT), :]


def row_stats(rows):
    centre = jnp.mean(rows, axis=-1, keepdims=True)
    shifted = rows - centre
    spread = jnp.mean(shifted * shifted, axis=-1, keepdims=True)
    inverse = lax.rsqrt(spread + epsilon)
    return shifted * inverse, inverse


def norm_back(dnorm, xhat, inverse, gain):
    scaled = dnorm * gain
    return inverse * (
        scaled
        - jnp.mean(scaled, axis=-1, keepdims=True)
        - xhat * jnp.mean(scaled * xhat, axis=-1, keepdims=True)
    )


def attend_pair(qkv_ref, out_ref, log_ref, scale):
    length = qkv_ref.shape[0]
    lane = lax.broadcasted_iota(jnp.int32, (SEG, 128), 1)
    key = qkv_ref[:, 128:256]
    value_t = jnp.transpose(qkv_ref[:, 256:384])
    for seg in range(length // SEG):
        keys_here = (seg + 1) * SEG
        query = qkv_ref[seg * SEG : keys_here, 0:128] * scale
        key_pos = lax.broadcasted_iota(jnp.int32, (keys_here, SEG), 0)
        query_pos = lax.broadcasted_iota(jnp.int32, (keys_here, SEG), 1) + seg * SEG
        parts = []
        for head in range(2):
            mine = jnp.where(lane // 64 == head, query, jnp.zeros_like(query))
            scores = contract_last(key[:keys_here], mine)
            scores = jnp.where(key_pos <= query_pos, scores, -1e30)
            top = jnp.max(scores, axis=0, keepdims=True)
            expo = jnp.exp(scores - top)
            total = jnp.sum(expo, axis=0, keepdims=True)
            mixed = matmul(value_t[head * 64 : head * 64 + 64, :keys_here], expo.astype(LOW))
            parts.append(mixed / total)
            log_ref[0, head : head + 1, seg * SEG : keys_here] = top + jnp.log(total)
        out_ref[seg * SEG : keys_here, :] = jnp.transpose(jnp.concatenate(parts, axis=0)).astype(
            LOW
        )


def front_kernel(place_ref, xhat_ref, vec_ref, bias_ref, *refs, scale, count):
    pieces = refs[:count]
    norm_ref, qkv_ref, out_ref, log_ref, weight_ref = refs[count:]

    @pl.when(pl.program_id(0) == 0)
    def _():
        norm_ref[...] = (xhat_ref[...] * vec_ref[0:1, :] + vec_ref[1:2, :]).astype(LOW)

    fill(weight_ref, pieces)
    bias = jnp.concatenate(
        [bias_ref[0:1, :], jnp.zeros((1, 128), jnp.float32), bias_ref[1:2, :]], axis=1
    )
    qkv_ref[...] = (matmul(norm_ref[...], weight_ref[...]) + bias).astype(LOW)
    attend_pair(qkv_ref, out_ref, log_ref, scale)


def front(place, xhat, vectors, bias, pieces, pairs, scale):
    length, width = xhat.shape
    return pl.pallas_call(
        functools.partial(front_kernel, scale=scale, count=len(pieces)),
        grid_spec=pltpu.PrefetchScalarGridSpec(
            num_scalar_prefetch=1,
            grid=(pairs,),
            in_specs=[
                whole((length, width)),
                whole(vectors.shape),
                pl.BlockSpec((8, 128), lambda p, place: (0, place[0] * pairs + p)),
            ]
            + piece_specs(pieces, 384),
            out_specs=[
                whole((length, width)),
                pl.BlockSpec((length, 384), lambda p, _: (0, p)),
                pl.BlockSpec((length, 128), lambda p, _: (0, p)),
                pl.BlockSpec((1, 8, length), lambda p, _: (p, 0, 0)),
            ],
            scratch_shapes=[pltpu.VMEM((width, 384), LOW)],
        ),
        out_shape=[
            jax.ShapeDtypeStruct((length, width), LOW),
            jax.ShapeDtypeStruct((length, pairs * 384), LOW),
            jax.ShapeDtypeStruct((length, pairs * 128), LOW),
            jax.ShapeDtypeStruct((pairs, 8, length), jnp.float32),
        ],
        compiler_params=settings(),
        cost_estimate=cost(2 * length * width * pairs * 384 * 4, 12 * length * width),
        name="front",
    )(place, xhat, vectors, bias, *pieces)


def share_kernel(att_ref, *refs):
    pieces, out_ref, weight_ref = refs[:-2], refs[-2], refs[-1]

    @pl.when(pl.program_id(0) == 0)
    def _():
        fill(weight_ref, pieces)

    out_ref[...] = contract_last(att_ref[...], weight_ref[...]).astype(LOW)


def share_product(att, pieces):
    length, inner = att.shape
    width = sum(piece.shape[0] for piece in pieces)
    return pl.pallas_call(
        share_kernel,
        grid=(length // SEG,),
        in_specs=[pl.BlockSpec((SEG, inner), lambda p: (p, 0))] + fixed_specs(pieces, inner, 3),
        out_specs=pl.BlockSpec((SEG, width), lambda p: (p, 0)),
        out_shape=jax.ShapeDtypeStruct((length, width), LOW),
        scratch_shapes=[pltpu.VMEM((width, inner), LOW)],
        compiler_params=settings(),
        cost_estimate=cost(2 * length * width * inner, 4 * length * width),
        name="share",
    )(att, *pieces)


def up_kernel(
    place_ref,
    x_ref,
    own_ref,
    other_ref,
    vec_ref,
    bias_ref,
    *refs,
):
    grad_ref, up_all_ref, resid_ref, left_ref, act_ref, slope_ref, weight_ref, norm_ref = refs
    length = x_ref.shape[0]

    @pl.when(pl.program_id(0) == 0)
    def _():
        for start in range(0, length, SEG):
            rows = slice(start, start + SEG)
            branch = own_ref[rows, :].astype(jnp.float32) + other_ref[rows, :].astype(jnp.float32)
            resid = x_ref[rows, :].astype(jnp.float32) + (branch + vec_ref[2:3, :])
            resid_ref[rows, :] = resid
            xhat, _ = row_stats(resid)
            norm = xhat * vec_ref[3:4, :] + vec_ref[4:5, :]
            norm_ref[rows, :] = norm.astype(LOW)
            put_natural(place_ref, left_ref.at[1, rows, :], norm)
            left_ref[0, rows, :] = grad_ref[rows, :]

    fill_slots(place_ref, weight_ref, up_all_ref)
    for start in range(0, length, SEG):
        rows = slice(start, start + SEG)
        pre = matmul(norm_ref[rows, :], weight_ref[...]) + bias_ref[...]
        square = pre * pre
        bent = jnp.tanh(gelu_coef * pre * (1.0 + 0.044715 * square))
        half = 0.5 * (1.0 + bent)
        act_ref[0, rows, :] = (pre * half).astype(LOW)
        slope_ref[rows, :] = (
            half
            + (0.5 * gelu_coef) * pre * (1.0 - bent * bent) * (1.0 + (3 * 0.044715) * square)
        ).astype(LOW)


def up_product(place, x, own, other, vectors, bias, grad, pair, block=512):
    length, width = x.shape
    hidden = pair.shape[1] // 2
    steps = hidden // block
    return pl.pallas_call(
        up_kernel,
        grid_spec=pltpu.PrefetchScalarGridSpec(
            num_scalar_prefetch=1,
            grid=(steps,),
            in_specs=[whole((length, width))] * 3
            + [
                whole(vectors.shape),
                pl.BlockSpec((1, block), lambda p, place: (0, place[0] * steps + p)),
                whole((length, width)),
                pl.BlockSpec((width, block), lambda p, _: (0, p)),
            ],
            out_specs=[
                whole((length, width)),
                whole((2, length, width)),
                pl.BlockSpec((1, length, block), lambda p, _: (0, 0, p)),
                pl.BlockSpec((length, block), lambda p, _: (0, p)),
            ],
            scratch_shapes=[pltpu.VMEM((width, block), LOW), pltpu.VMEM((length, width), LOW)],
        ),
        out_shape=[
            jax.ShapeDtypeStruct((length, width), jnp.float32),
            jax.ShapeDtypeStruct((2, length, width), LOW),
            jax.ShapeDtypeStruct((2, length, hidden), LOW),
            jax.ShapeDtypeStruct((length, hidden), LOW),
        ],
        compiler_params=settings(),
        cost_estimate=cost(3 * length * width * hidden, 16 * length * width),
        name="up",
    )(place, x, own, other, vectors, bias, grad, pair)


def turn_kernel(
    place_ref,
    grad_ref,
    act_ref,
    slope_ref,
    up_all_ref,
    down_all_ref,
    own_ref,
    other_ref,
    dnorm_ref,
    dpre_ref,
    sum_ref,
    up_ref,
    down_ref,
    out_acc,
    norm_acc,
):
    length = grad_ref.shape[0]
    rows_own = length // 2
    step = pl.program_id(0)
    fill_slots(place_ref, up_ref, up_all_ref)
    fill_slots(place_ref, down_ref, down_all_ref)
    total = jnp.zeros((1, up_ref.shape[1]), jnp.float32)
    for start in range(0, length, SEG):
        rows = slice(start, start + SEG)
        dact = matmul(grad_ref[rows, :], down_ref[...])
        dpre = (dact * slope_ref[rows, :].astype(jnp.float32)).astype(LOW)
        dpre_ref[0, rows, :] = dpre
        total = total + jnp.sum(dpre.astype(jnp.float32), axis=0, keepdims=True)
        mixed = contract_last(act_ref[0, rows, :], down_ref[...])
        dnorm = contract_last(dpre, up_ref[...])

        @pl.when(step == 0)
        def _():
            out_acc[rows, :] = mixed
            norm_acc[rows, :] = dnorm

        @pl.when(step > 0)
        def _():
            out_acc[rows, :] += mixed
            norm_acc[rows, :] += dnorm

    sum_ref[...] = jnp.broadcast_to(total, sum_ref.shape)

    @pl.when(step == pl.num_programs(0) - 1)
    def _():
        side = place_ref[0]
        own_ref[...] = out_acc[pl.ds(pl.multiple_of(side * rows_own, rows_own), rows_own), :]
        other_ref[...] = out_acc[
            pl.ds(pl.multiple_of((1 - side) * rows_own, rows_own), rows_own), :
        ].astype(LOW)
        dnorm_ref[...] = norm_acc[...].astype(LOW)


def turn_product(place, grad, act, slope, pair, block=512):
    length, width = grad.shape
    hidden = act.shape[2]
    steps = hidden // block
    return pl.pallas_call(
        turn_kernel,
        grid_spec=pltpu.PrefetchScalarGridSpec(
            num_scalar_prefetch=1,
            grid=(hidden // block,),
            in_specs=[
                whole((length, width)),
                pl.BlockSpec((1, length, block), lambda p, _: (0, 0, p)),
                pl.BlockSpec((length, block), lambda p, _: (0, p)),
                pl.BlockSpec((width, block), lambda p, _: (0, p)),
                pl.BlockSpec((width, block), lambda p, _: (0, steps + p)),
            ],
            out_specs=[
                whole((length // 2, width)),
                whole((length // 2, width)),
                whole((length, width)),
                pl.BlockSpec((1, length, block), lambda p, _: (1, 0, p)),
                pl.BlockSpec((8, block), lambda p, _: (0, p)),
            ],
            scratch_shapes=[
                pltpu.VMEM((width, block), LOW),
                pltpu.VMEM((width, block), LOW),
                pltpu.VMEM((length, width), jnp.float32),
                pltpu.VMEM((length, width), jnp.float32),
            ],
        ),
        out_shape=[
            jax.ShapeDtypeStruct((length // 2, width), jnp.float32),
            jax.ShapeDtypeStruct((length // 2, width), LOW),
            jax.ShapeDtypeStruct((length, width), LOW),
            jax.ShapeDtypeStruct((2, length, hidden), LOW),
            jax.ShapeDtypeStruct((8, hidden), jnp.float32),
        ],
        input_output_aliases={2: 3},
        compiler_params=settings(),
        cost_estimate=cost(6 * length * width * hidden, 24 * length * width),
        name="turn",
    )(place, grad, act, slope, pair, pair)


def mid_kernel(resid_ref, own_ref, other_ref, grad_ref, vec_ref, *refs, count):
    pieces = refs[:count]
    dresid_ref, dbranch_ref, datt_ref, sum_ref, weight_ref = refs[count:]

    @pl.when(pl.program_id(0) == 0)
    def _():
        fill(weight_ref, pieces)
        sum_ref[...] = jnp.zeros_like(sum_ref)

    dnorm = own_ref[...].astype(jnp.float32) + other_ref[...].astype(jnp.float32)
    grad = grad_ref[...].astype(jnp.float32)
    xhat, inverse = row_stats(resid_ref[...])
    dresid = grad + norm_back(dnorm, xhat, inverse, vec_ref[3:4, :])
    dresid_ref[...] = dresid
    dbranch = dresid.astype(LOW)
    dbranch_ref[...] = dbranch
    datt_ref[...] = matmul(dbranch, weight_ref[...]).astype(LOW)
    for row, value in enumerate((dnorm * xhat, dnorm, dbranch.astype(jnp.float32), grad)):
        sum_ref[row : row + 1, :] += 0.5 * jnp.sum(value, axis=0, keepdims=True)


def mid_product(resid, own, other, grad, vectors, pieces, inner):
    length, width = resid.shape
    rows = pl.BlockSpec((SEG, width), lambda p: (p, 0))
    return pl.pallas_call(
        functools.partial(mid_kernel, count=len(pieces)),
        grid=(length // SEG,),
        in_specs=[rows] * 4 + [whole(vectors.shape)] + fixed_specs(pieces, inner, 3),
        out_specs=[rows, rows, pl.BlockSpec((SEG, inner), lambda p: (p, 0)), whole((8, width))],
        out_shape=[
            jax.ShapeDtypeStruct((length, width), jnp.float32),
            jax.ShapeDtypeStruct((length, width), LOW),
            jax.ShapeDtypeStruct((length, inner), LOW),
            jax.ShapeDtypeStruct((8, width), jnp.float32),
        ],
        scratch_shapes=[pltpu.VMEM((width, inner), LOW)],
        compiler_params=settings(),
        cost_estimate=cost(2 * length * width * inner * 16, 16 * length * width),
        name="mid",
    )(resid, own, other, grad, vectors, *pieces)


def attend_back_pair(qkv_ref, grad_ref, log_ref, out_ref, dkey_ref, dvalue_ref, scale):
    length = qkv_ref.shape[0]
    lane = lax.broadcasted_iota(jnp.int32, (SEG, 128), 1)
    key = qkv_ref[:, 128:256]
    value = qkv_ref[:, 256:384]
    key_t = jnp.transpose(key)
    dkey_ref[...] = jnp.zeros_like(dkey_ref)
    dvalue_ref[...] = jnp.zeros_like(dvalue_ref)
    for seg in range(length // SEG):
        keys_here = (seg + 1) * SEG
        rows = slice(seg * SEG, keys_here)
        query = qkv_ref[rows, 0:128] * scale
        grad = grad_ref[rows, :]
        key_pos = lax.broadcasted_iota(jnp.int32, (keys_here, SEG), 0)
        query_pos = lax.broadcasted_iota(jnp.int32, (keys_here, SEG), 1) + seg * SEG
        parts = []
        dkey = jnp.zeros((keys_here, 128), jnp.float32)
        dvalue = jnp.zeros((keys_here, 128), jnp.float32)
        for head in range(2):
            here = lane // 64 == head
            query_mine = jnp.where(here, query, jnp.zeros_like(query))
            grad_mine = jnp.where(here, grad, jnp.zeros_like(grad))
            scores = contract_last(key[:keys_here], query_mine)
            scores = jnp.where(key_pos <= query_pos, scores, -1e30)
            probs = jnp.exp(scores - log_ref[0, head : head + 1, rows])
            dprobs = contract_last(value[:keys_here], grad_mine)
            mean = jnp.sum(probs * dprobs, axis=0, keepdims=True)
            dscores = (probs * (dprobs - mean)).astype(LOW)
            dvalue = dvalue + matmul(probs.astype(LOW), grad_mine)
            dkey = dkey + matmul(dscores, query_mine)
            parts.append(matmul(key_t[head * 64 : head * 64 + 64, :keys_here], dscores) * scale)
        dkey_ref[:keys_here, :] += dkey
        dvalue_ref[:keys_here, :] += dvalue
        out_ref[rows, 0:128] = jnp.transpose(jnp.concatenate(parts, axis=0)).astype(LOW)
    out_ref[:, 128:256] = dkey_ref[...].astype(LOW)
    out_ref[:, 256:384] = dvalue_ref[...].astype(LOW)


def back_kernel(place_ref, xhat_ref, qkv_ref, grad_ref, log_ref, *refs, scale, count):
    pieces = refs[:count]
    dqkv_ref, own_ref, other_ref, sum_ref, vec_ref = refs[count : count + 5]
    weight_ref, dkey_ref, dvalue_ref, acc_ref = refs[count + 5 :]
    rows_own = own_ref.shape[0]
    step = pl.program_id(0)
    fill(weight_ref, pieces)
    attend_back_pair(qkv_ref, grad_ref, log_ref, dqkv_ref, dkey_ref, dvalue_ref, scale)
    dnorm = contract_last(dqkv_ref[...], weight_ref[...])
    sum_ref[...] = jnp.broadcast_to(
        jnp.sum(dqkv_ref[...].astype(jnp.float32), axis=0, keepdims=True)[None], sum_ref.shape
    )

    @pl.when(step == 0)
    def _():
        acc_ref[...] = dnorm

    @pl.when(step > 0)
    def _():
        acc_ref[...] += dnorm

    @pl.when(step == pl.num_programs(0) - 1)
    def _():
        side = place_ref[0]
        total = acc_ref[...]
        vec_ref[0:1, :] = jnp.sum(total * xhat_ref[...], axis=0, keepdims=True)
        vec_ref[1:8, :] = jnp.broadcast_to(jnp.sum(total, axis=0, keepdims=True), (7, total.shape[1]))
        own_ref[...] = acc_ref[pl.ds(pl.multiple_of(side * rows_own, rows_own), rows_own), :]
        other_ref[...] = acc_ref[
            pl.ds(pl.multiple_of((1 - side) * rows_own, rows_own), rows_own), :
        ].astype(LOW)


def back_product(place, xhat, qkv, grad, logs, pieces, scale):
    length, columns = qkv.shape
    width = sum(piece.shape[0] for piece in pieces)
    pairs = columns // 384
    return pl.pallas_call(
        functools.partial(back_kernel, scale=scale, count=len(pieces)),
        grid_spec=pltpu.PrefetchScalarGridSpec(
            num_scalar_prefetch=1,
            grid=(pairs,),
            in_specs=[
                whole((length, width)),
                pl.BlockSpec((length, 384), lambda p, _: (0, p)),
                pl.BlockSpec((length, 128), lambda p, _: (0, p)),
                pl.BlockSpec((1, 8, length), lambda p, _: (p, 0, 0)),
            ]
            + piece_specs(pieces, 384),
            out_specs=[
                pl.BlockSpec((length, 384), lambda p, _: (0, p)),
                whole((length // 2, width)),
                whole((length // 2, width)),
                pl.BlockSpec((1, 8, 384), lambda p, _: (p, 0, 0)),
                whole((8, width)),
            ],
            scratch_shapes=[
                pltpu.VMEM((width, 384), LOW),
                pltpu.VMEM((length, 128), jnp.float32),
                pltpu.VMEM((length, 128), jnp.float32),
                pltpu.VMEM((length, width), jnp.float32),
            ],
        ),
        out_shape=[
            jax.ShapeDtypeStruct((length, columns), LOW),
            jax.ShapeDtypeStruct((length // 2, width), jnp.float32),
            jax.ShapeDtypeStruct((length // 2, width), LOW),
            jax.ShapeDtypeStruct((pairs, 8, 384), jnp.float32),
            jax.ShapeDtypeStruct((8, width), jnp.float32),
        ],
        compiler_params=settings(),
        cost_estimate=cost(2 * length * width * columns * 48, 12 * length * width),
        name="back",
    )(place, xhat, qkv, grad, logs, *pieces)


def put_natural(place_ref, out_ref, value):
    near = value.shape[1] // 512
    lane = lax.broadcasted_iota(jnp.int32, (value.shape[0], 128), 1)
    half = value.shape[1] // 2
    for slot in range(4 * near):
        first = value[:, slot // 2 * 128 : slot // 2 * 128 + 128]
        second = value[:, half + slot // 2 * 128 : half + slot // 2 * 128 + 128]
        if slot % 2 == 0:
            second = pltpu.roll(second, 64, 1)
        else:
            first = pltpu.roll(first, 64, 1)
        block = jnp.where(lane < 64, first, second)
        block = jnp.where(place_ref[3] == 1, pltpu.roll(block, 64, 1), block)
        far_index = lax.rem(place_ref[1] + 4 - slot % 4, 4)
        near_index = lax.rem(place_ref[2] + near - slot // 4, near)
        target = far_index * near + near_index
        out_ref[:, pl.ds(pl.multiple_of(target * 128, 128), 128)] = block.astype(out_ref.dtype)


def last_kernel(
    place_ref, x_ref, dresid_ref, own_ref, other_ref, vec_ref, out_ref
):
    dnorm = own_ref[...] + other_ref[...].astype(jnp.float32)
    xhat, inverse = row_stats(x_ref[...].astype(jnp.float32))
    total = dresid_ref[...] + norm_back(dnorm, xhat, inverse, vec_ref[0:1, :])
    put_natural(place_ref, out_ref, total)


def last_product(place, x, dresid, own, other, vectors):
    rows, width = own.shape
    block = 128
    steps = rows // block
    mine = pl.BlockSpec((block, width), lambda p, place: (place[0] * steps + p, 0))
    plain = pl.BlockSpec((block, width), lambda p, _: (p, 0))
    return pl.pallas_call(
        last_kernel,
        grid_spec=pltpu.PrefetchScalarGridSpec(
            num_scalar_prefetch=1,
            grid=(steps,),
            in_specs=[mine, mine, plain, plain, whole(vectors.shape)],
            out_specs=plain,
        ),
        out_shape=jax.ShapeDtypeStruct((rows, width), jnp.float32),
        compiler_params=settings(),
        cost_estimate=cost(40 * rows * width, 320 * rows * width),
        name="last",
    )(place, x, dresid, own, other, vectors)


def result_kernel(place_ref, resid_ref, own_ref, other_ref, vec_ref, out_ref):
    mixed = own_ref[...] + other_ref[...].astype(jnp.float32)
    total = resid_ref[...] + mixed + vec_ref[5:6, :]
    put_natural(place_ref, out_ref, total)


def result_product(place, resid, own, other, vectors):
    rows, width = own.shape
    block = 128
    steps = rows // block
    mine = pl.BlockSpec((block, width), lambda p, place: (place[0] * steps + p, 0))
    plain = pl.BlockSpec((block, width), lambda p, _: (p, 0))
    return pl.pallas_call(
        result_kernel,
        grid_spec=pltpu.PrefetchScalarGridSpec(
            num_scalar_prefetch=1,
            grid=(steps,),
            in_specs=[mine, plain, plain, whole(vectors.shape)],
            out_specs=plain,
        ),
        out_shape=jax.ShapeDtypeStruct((rows, width), LOW),
        compiler_params=settings(),
        cost_estimate=cost(10 * rows * width, 320 * rows * width),
        name="result",
    )(place, resid, own, other, vectors)


def pack_kernel(proj_ref, out_ref, up_ref, down_ref, vec_ref, narrow_ref, wide_ref):
    columns = proj_ref.shape[2]
    for pair in range(columns // 128):
        for kind in range(3):
            start = (pair * 3 + kind) * 128
            narrow_ref[:, start : start + 128] = proj_ref[kind, :, pair * 128 : pair * 128 + 128]
    narrow_ref[:, 3 * columns : 4 * columns] = out_ref[...]
    turned = jnp.transpose(vec_ref[...].astype(jnp.float32))
    turned = jnp.concatenate([turned, jnp.zeros((SLOT, 112), jnp.float32)], axis=1)
    narrow_ref[:, 4 * columns :] = turned.astype(LOW)
    hidden = up_ref.shape[1]
    wide_ref[:, :hidden] = up_ref[...]
    wide_ref[:, hidden:] = down_ref[...]


def pack_shards(proj, out, up, down, vec):
    rows, columns = out.shape
    return pl.pallas_call(
        pack_kernel,
        out_shape=[
            jax.ShapeDtypeStruct((rows, 4 * columns + 128), LOW),
            jax.ShapeDtypeStruct((rows, 2 * up.shape[1]), LOW),
        ],
        compiler_params=settings(),
        cost_estimate=cost(0, 4 * rows * (4 * columns + 2 * up.shape[1])),
        name="pack",
    )(proj, out, up, down, vec)


def vector_kernel(place_ref, *refs):
    pieces = refs[:-4]
    slot_ref, bias_ref, hidden_ref, joined_ref = refs[-4:]
    fill(joined_ref, pieces)
    turned = jnp.transpose(joined_ref[...]).astype(jnp.float32)
    slot_ref[...] = turned[0:8]
    put_natural(place_ref, bias_ref, turned[8:16])
    lane = lax.broadcasted_iota(jnp.int32, (1, 128), 1)
    for pair in range(bias_ref.shape[1] // 128):
        rows = [bias_ref[2 + q : 3 + q, pair * 128 : pair * 128 + 128] for q in range(4)]
        flipped = [pltpu.roll(row, 64, 1) for row in rows]
        for q in (0, 2):
            start = pair * 512 + q * 64
            hidden_ref[:, start : start + 128] = jnp.where(lane < 64, rows[q], flipped[q + 1])
            hidden_ref[:, start + 256 : start + 384] = jnp.where(
                lane < 64, flipped[q], rows[q + 1]
            )


def spread_vectors(place, pieces, index):
    width = sum(piece.shape[0] for piece in pieces)
    return pl.pallas_call(
        vector_kernel,
        grid_spec=pltpu.PrefetchScalarGridSpec(
            num_scalar_prefetch=1,
            grid=(1,),
            in_specs=fixed_specs(pieces, 128, index),
            out_specs=[whole((8, width)), whole((8, width)), whole((1, 4 * width))],
            scratch_shapes=[pltpu.VMEM((width, 128), LOW)],
        ),
        out_shape=[
            jax.ShapeDtypeStruct((8, width), jnp.float32),
            jax.ShapeDtypeStruct((8, width), jnp.float32),
            jax.ShapeDtypeStruct((1, 4 * width), jnp.float32),
        ],
        compiler_params=settings(),
        cost_estimate=cost(width * 128, 2 * width * 128),
        name="vectors",
    )(place, *pieces)


def after(value, *events):
    return lax.optimization_barrier((value,) + events)[0]


def dp_shift(value, ranks, dz, dy, dc):
    far, near = 4, ranks // 8

    def goes(rank):
        z, y, c = rank // (near * 2), rank // 2 % near, rank % 2
        return ((z + dz) % far * near + (y + dy) % near) * 2 + (c + dc) % 2

    return lax.ppermute(value, "dp", [(rank, goes(rank)) for rank in range(ranks)])


def dp_gather(shard, ranks):
    far = [shard] + [dp_shift(shard, ranks, k, 0, 0) for k in (1, 2, 3)]
    near = [dp_shift(piece, ranks, 0, 1, 0) for piece in far]
    pieces = far + near
    return pieces + [dp_shift(piece, ranks, 0, 0, 1) for piece in pieces], pieces


def far_reduce(total, ranks, wire):
    rows = total.shape[0] // 4
    sent = {
        k: dp_shift(total[k * rows : (k + 1) * rows].astype(wire), ranks, -k, 0, 0)
        for k in (1, 3, 2)
    }
    result = total[:rows]
    for k in (1, 2, 3):
        result = result + sent[k].astype(jnp.float32)
    return result


def dp_reduce_small(grads, ranks):
    near = ranks // 8
    half = grads.shape[0] // 2
    mine = grads[:half] + dp_shift(grads[half:], ranks, 0, 0, 1)
    part = half // near
    total = mine[:part]
    for step in range(1, near):
        total = total + dp_shift(mine[step * part : (step + 1) * part], ranks, 0, -step, 0)
    return far_reduce(total, ranks, jnp.float32)


def reduce_core(left, right, ranks):
    half = left.shape[1] // 2
    return dp_shift(contract_rows(left[:, half:], right).astype(LOW), ranks, 0, 0, 1)


def reduce_near(left, right, other):
    half = left.shape[1] // 2
    part = half // 2
    sent = contract_rows(left[:, part:half], right) + other[part:].astype(jnp.float32)
    return sent.astype(LOW)


def reduce_sum(left, right, other, arrived):
    part = left.shape[1] // 4
    total = contract_rows(left[:, :part], right) + other[:part].astype(jnp.float32)
    return total + arrived.astype(jnp.float32)


def far_send(total, ranks):
    rows = total.shape[0] // 4
    low = total.astype(LOW)
    return [dp_shift(low[k * rows : (k + 1) * rows], ranks, -k, 0, 0) for k in (1, 3, 2)]


def far_sum(total, sent):
    result = total[: total.shape[0] // 4]
    for value in sent:
        result = result + value.astype(jnp.float32)
    return result


def swap(value):
    return lax.ppermute(value, "tensor", [(0, 1), (1, 0)])


def paired(
    inputs,
    out_grad,
    parents,
    ln1_gain,
    ln1_bias,
    w_qkv,
    qv_bias,
    w_attn_out,
    attn_out_bias,
    ln2_gain,
    ln2_bias,
    w_up,
    up_bias,
    w_down,
    down_bias,
):
    ranks = lax.axis_size("dp")
    near = ranks // 8
    rank = lax.axis_index("dp")
    side = lax.axis_index("tensor")
    rows, width = inputs.shape
    shard = width // ranks
    heads_width = w_qkv.shape[2]
    pairs = heads_width // 128
    hidden = w_up.shape[1]
    scale = 1.0 / math.sqrt(width // HEADS)

    slots = jnp.arange(ranks, dtype=jnp.int32)
    core_step, near_step, far_step = slots // (ranks // 2), slots // 4 % near, slots % 4
    my_z, my_y, my_c = rank // (2 * near), rank // 2 % near, rank % 2
    source = ((my_z - far_step) % 4 * near + (my_y - near_step) % near) * 2 + (
        my_c + core_step
    ) % 2
    place = jnp.concatenate([jnp.stack([side, my_z, my_y, my_c]), source]).astype(jnp.int32)
    feature = jnp.repeat(source * shard, shard) + jnp.tile(
        jnp.arange(shard, dtype=jnp.int32), ranks
    )
    to_local = (jnp.arange(width, dtype=jnp.int32)[:, None] == feature[None, :]).astype(LOW)
    slot_of = (slots[:, None] == source[None, :]).astype(jnp.float32)

    zero = jnp.zeros_like(ln1_gain)
    vec = [ln1_gain, ln1_bias, attn_out_bias, ln2_gain, ln2_bias, down_bias, zero, zero]
    vec = jnp.concatenate(
        [jnp.stack(vec), qv_bias, up_bias.reshape(4, shard), jnp.zeros((2, shard), LOW)], axis=0
    )
    narrow_shard, wide_shard = pack_shards(w_qkv, w_attn_out.T, w_up, w_down.T, vec)
    inputs_other = swap(inputs)
    grad_other = swap(after(out_grad, inputs_other))
    narrow, narrow_far = dp_gather(narrow_shard, ranks)
    wide = lax.all_gather(
        after(wide_shard, inputs_other, *narrow_far[1:7]), "dp", axis=0, tiled=True
    )
    vectors, query_bias, hidden_bias = spread_vectors(place, narrow, 16)

    def in_order(own, other):
        return jnp.where(
            side == 0,
            jnp.concatenate([own, other], axis=0),
            jnp.concatenate([other, own], axis=0),
        )

    hidden_in = matmul(
        after(in_order(inputs, inputs_other), *narrow_far[1:4]), to_local
    )
    xhat, _ = row_stats(hidden_in)
    hidden_in = hidden_in.astype(LOW)
    norm_one, qkv, attended, logs = front(
        place, xhat, vectors, query_bias, narrow, pairs, scale
    )
    share = share_product(after(attended, grad_other), narrow)
    grad_rows = after(in_order(out_grad, grad_other), share)
    cotangent = matmul(grad_rows, to_local).astype(LOW)
    resid, lefts, rights, slope = up_product(
        place, hidden_in, share, swap(share), vectors, hidden_bias, grad_rows, wide
    )
    own_out, other_out, dnorm_share, rights, dpre_sum = turn_product(
        place, cotangent, rights, slope, wide
    )
    dnorm_other = swap(dnorm_share)
    wide_share = lax.dot_general(
        lefts,
        after(rights, dnorm_share),
        (((1,), (1,)), ((0,), (0,))),
        preferred_element_type=jnp.float32,
    ).astype(LOW)
    wide_grad = lax.psum_scatter(wide_share, "dp", scatter_dimension=1, tiled=True)
    dresid, dbranch, dattended, mid_sum = mid_product(
        after(resid, wide_share),
        dnorm_share,
        dnorm_other,
        cotangent,
        vectors,
        narrow,
        heads_width,
    )
    dqkv, own_dnorm, other_dnorm, dqkv_sum, front_sum = back_product(
        place, xhat, qkv, dattended, logs, narrow, scale
    )
    proj_core = reduce_core(norm_one, dqkv, ranks)
    proj_near = reduce_near(norm_one, dqkv, proj_core)
    proj_arrived = dp_shift(proj_near, ranks, 0, 1, 0)
    out_core = reduce_core(dbranch, attended, ranks)
    out_near = reduce_near(dbranch, attended, out_core)
    out_arrived = dp_shift(after(out_near, proj_near), ranks, 0, 1, 0)
    grad_back = wide_grad[0].T.astype(jnp.float32)
    grad_hidden = wide_grad[1].astype(jnp.float32)
    own_other, back_other = swap(other_out), swap(other_dnorm)
    proj_total = reduce_sum(
        norm_one, dqkv, proj_core, after(proj_arrived, own_other, back_other)
    )
    grad_proj = far_sum(proj_total, far_send(proj_total, ranks))
    out_total = reduce_sum(dbranch, attended, out_core, out_arrived)
    grad_out = far_sum(out_total, far_send(out_total, ranks)).T
    result = result_product(
        place, after(resid, proj_total, out_total), own_out, own_other, vectors
    )
    input_grad = last_product(
        place,
        hidden_in,
        dresid,
        own_dnorm,
        after(back_other, proj_total, out_total),
        vectors,
    )
    grad_proj = grad_proj.reshape(shard, pairs, 3, 128).transpose(2, 0, 1, 3)
    grad_proj = grad_proj.reshape(3, shard, heads_width)

    dqkv_sum = dqkv_sum[:, 0].reshape(pairs, 3, 128)
    placed = [
        place_block(value, 2 * value.shape[0], side * value.shape[0]).reshape(ranks, -1)
        for value in (
            dqkv_sum[:, 0].reshape(heads_width),
            dqkv_sum[:, 2].reshape(heads_width),
            dpre_sum[0],
        )
    ]
    to_slot = lax.dot_general(
        slot_of,
        jnp.concatenate(placed, axis=1),
        (((0,), (0,)), ((), ())),
        precision=lax.Precision.HIGHEST,
        preferred_element_type=jnp.float32,
    )
    pack = jnp.stack([front_sum[0], front_sum[1], mid_sum[2], mid_sum[0], mid_sum[1], mid_sum[3]])
    pack = pack.reshape(6, ranks, shard).transpose(1, 0, 2).reshape(ranks, -1)
    pack = after(jnp.concatenate([pack, to_slot], axis=1), proj_near)
    pack = dp_reduce_small(pack + swap(pack), ranks)
    pack = pack.reshape(-1)
    vector_grads = [pack[i * shard : (i + 1) * shard] for i in range(6)]
    return (
        result,
        input_grad,
        vector_grads[0],
        vector_grads[1],
        grad_proj,
        pack[6 * shard : 8 * shard].reshape(2, shard),
        grad_out,
        vector_grads[2],
        vector_grads[3],
        vector_grads[4],
        grad_hidden,
        pack[8 * shard :],
        grad_back,
        vector_grads[5],
    )


def local(*arrays):
    fits = lax.axis_size("tensor") == 2 and lax.axis_size("dp") == 16
    if fits and arrays[2].shape[1] == 3:
        return paired(*arrays)
    return generic(*arrays)


def solution(mesh):
    return jax.shard_map(
        local,
        mesh=mesh,
        in_specs=(
            P(("dp", "tensor"), None),
            P(("dp", "tensor"), None),
            P("dp", None),
            P("dp"),
            P("dp"),
            P(None, "dp", "tensor"),
            P(None, "dp"),
            P("tensor", "dp"),
            P("dp"),
            P("dp"),
            P("dp"),
            P("dp", "tensor"),
            P("dp"),
            P("tensor", "dp"),
            P("dp"),
        ),
        out_specs=(
            P(("dp", "tensor"), None),
            P(("dp", "tensor"), None),
            P("dp"),
            P("dp"),
            P(None, "dp", "tensor"),
            P(None, "dp"),
            P("tensor", "dp"),
            P("dp"),
            P("dp"),
            P("dp"),
            P("dp", "tensor"),
            P("dp"),
            P("tensor", "dp"),
            P("dp"),
        ),
        check_vma=False,
    )
```

```python
import functools
import math

import jax
import jax.numpy as jnp
from jax import lax
from jax.experimental import pallas as pl
from jax.experimental.pallas import tpu as pltpu
from jax.sharding import PartitionSpec as P

HEADS = 16
SEG = 256


epsilon = 1e-05
gelu_coef = 0.7978845608028654


def layer_norm(values, scales, shifts):
    centre = jnp.mean(values, axis=-1, keepdims=True)
    shifted = values - centre
    spread = jnp.mean(shifted * shifted, axis=-1, keepdims=True)
    return shifted * lax.rsqrt(spread + epsilon) * scales + shifts


def gelu_tanh(values):
    return (
        0.5 * values * (1.0 + jnp.tanh(gelu_coef * (values + 0.044715 * values * values * values)))
    )


def matmul(left, right):
    return jnp.dot(left, right, preferred_element_type=jnp.float32)


def contract_rows(left, right):
    return lax.dot_general(
        left, right, (((0,), (0,)), ((), ())), preferred_element_type=jnp.float32
    )


def contract_last(left, right):
    return lax.dot_general(
        left, right, (((1,), (1,)), ((), ())), preferred_element_type=jnp.float32
    )


def ancestors(parent_row, segment_count):
    labels = jnp.arange(segment_count, dtype=jnp.int32)
    links = ((parent_row[:, None] == labels[None, :]) & (labels[:, None] > 0)).astype(jnp.float32)
    identity = jnp.eye(segment_count, dtype=jnp.float32)

    def extend(turn, reached):
        grown = jnp.dot(
            links, reached, precision=lax.Precision.HIGHEST, preferred_element_type=jnp.float32
        )
        return jnp.minimum(identity + grown, 1.0)

    return lax.fori_loop(0, segment_count, extend, identity)


def tree_mask(reached, first_row, block_rows, length):
    query_pos = first_row + jnp.arange(block_rows, dtype=jnp.int32)
    key_pos = jnp.arange(length, dtype=jnp.int32)
    segment_count = reached.shape[0]
    onehot = (
        (query_pos // SEG)[:, None] == jnp.arange(segment_count, dtype=jnp.int32)[None, :]
    ).astype(jnp.float32)
    row_reach = jnp.dot(
        onehot, reached, precision=lax.Precision.HIGHEST, preferred_element_type=jnp.float32
    )
    spread_out = jnp.repeat(row_reach, SEG, axis=1)
    return (spread_out > 0.5) & (key_pos[None, :] <= query_pos[:, None])


def row_block(length):
    pieces = -(-length // 512)
    while length % pieces:
        pieces += 1
    return length // pieces


def place_block(local_vec, full_length, offset):
    empty_vec = jnp.zeros(local_vec.shape[:-1] + (full_length,), jnp.float32)
    return lax.dynamic_update_slice_in_dim(empty_vec, local_vec, offset, local_vec.ndim - 1)


def generic(
    inputs,
    out_grad,
    parents,
    ln1_gain,
    ln1_bias,
    w_qkv,
    qv_bias,
    w_attn_out,
    attn_out_bias,
    ln2_gain,
    ln2_bias,
    w_up,
    up_bias,
    w_down,
    down_bias,
):
    tensor_ranks = lax.axis_size("tensor")
    tensor_rank = lax.axis_index("tensor")
    rows_own = inputs.shape[0]
    length = rows_own * tensor_ranks
    model_width = inputs.shape[1]
    head_dim = model_width // HEADS
    local_width = w_qkv.shape[2]
    local_hidden = w_up.shape[1]
    heads_here = local_width // head_dim
    scale = 1.0 / math.sqrt(head_dim)
    gathered = (
        lax.all_gather(w_qkv, "dp", axis=1, tiled=True),
        lax.all_gather(w_attn_out, "dp", axis=1, tiled=True),
        lax.all_gather(w_up, "dp", axis=0, tiled=True),
        lax.all_gather(w_down, "dp", axis=1, tiled=True),
        lax.all_gather(ln1_gain, "dp", axis=0, tiled=True),
        lax.all_gather(ln1_bias, "dp", axis=0, tiled=True),
        lax.all_gather(qv_bias, "dp", axis=1, tiled=True),
        lax.all_gather(attn_out_bias, "dp", axis=0, tiled=True),
        lax.all_gather(ln2_gain, "dp", axis=0, tiled=True),
        lax.all_gather(ln2_bias, "dp", axis=0, tiled=True),
        lax.all_gather(up_bias, "dp", axis=0, tiled=True),
        lax.all_gather(down_bias, "dp", axis=0, tiled=True),
    )
    proj_full, out_full, hidden_full, back_full = (
        gathered[0],
        gathered[1],
        gathered[2],
        gathered[3],
    )
    gain_one = gathered[4].astype(jnp.float32)
    shift_one = gathered[5].astype(jnp.float32)
    proj_bias = lax.dynamic_slice_in_dim(
        gathered[6].astype(jnp.float32), tensor_rank * local_width, local_width, 1
    )
    out_bias = gathered[7].astype(jnp.float32)
    gain_two = gathered[8].astype(jnp.float32)
    shift_two = gathered[9].astype(jnp.float32)
    hidden_bias_full = gathered[10].astype(jnp.float32)
    back_bias = gathered[11].astype(jnp.float32)
    full_hidden = hidden_bias_full.shape[0]
    hidden_in = inputs.astype(jnp.float32)
    norm_one, ln1_pull = jax.vjp(layer_norm, hidden_in, gain_one, shift_one)
    norm_one_all = lax.all_gather(norm_one.astype(jnp.bfloat16), "tensor", axis=0, tiled=True)
    queries = (matmul(norm_one_all, proj_full[0]) + proj_bias[0]).astype(jnp.bfloat16)
    keys_low = matmul(norm_one_all, proj_full[1]).astype(jnp.bfloat16)
    values_low = (matmul(norm_one_all, proj_full[2]) + proj_bias[1]).astype(jnp.bfloat16)
    reached = ancestors(parents[0], length // SEG)
    block_rows = row_block(length)
    num_blocks = length // block_rows
    starts = jnp.arange(num_blocks, dtype=jnp.int32) * block_rows
    query_blocks = queries.reshape(num_blocks, block_rows, heads_here, head_dim)
    key_heads = keys_low.reshape(length, heads_here, head_dim)
    value_heads = values_low.reshape(length, heads_here, head_dim)

    def block_scores(query_block, first_row):
        scores = (
            jnp.einsum("qhd,khd->hqk", query_block, key_heads, preferred_element_type=jnp.float32)
            * scale
        )
        allowed = tree_mask(reached, first_row, block_rows, length)
        return jnp.where(allowed[None], scores, -1e30)

    def forward_block(element):
        query_block, first_row = element
        scores = block_scores(query_block, first_row)
        top_score = jnp.max(scores, axis=-1, keepdims=True)
        expo = jnp.exp(scores - top_score)
        totals = jnp.sum(expo, axis=-1, keepdims=True)
        probs = (expo / totals).astype(jnp.bfloat16)
        attended_block = jnp.einsum(
            "hqk,khd->qhd", probs, value_heads, preferred_element_type=jnp.float32
        )
        return (attended_block, (top_score + jnp.log(totals))[..., 0])

    attended_blocks, log_totals = lax.map(forward_block, (query_blocks, starts))
    attended = attended_blocks.reshape(length, local_width).astype(jnp.bfloat16)
    branch = (
        lax.psum_scatter(matmul(attended, out_full), "tensor", scatter_dimension=0, tiled=True)
        + out_bias
    )
    resid = hidden_in + branch
    norm_two, ln2_pull = jax.vjp(layer_norm, resid, gain_two, shift_two)
    norm_two_low = norm_two.astype(jnp.bfloat16)
    grad_back_bias = jnp.sum(out_grad.astype(jnp.float32), axis=0)
    norm_two_all = lax.all_gather(norm_two_low, "tensor", axis=0, tiled=True)
    hidden_slice = lax.dynamic_slice_in_dim(
        hidden_bias_full, tensor_rank * local_hidden, local_hidden, 0
    )
    pre = matmul(norm_two_all, hidden_full) + hidden_slice
    act, gelu_pull = jax.vjp(gelu_tanh, pre)
    act_low = act.astype(jnp.bfloat16)
    mixed = (
        lax.psum_scatter(
            matmul(act_low, back_full).astype(jnp.bfloat16),
            "tensor",
            scatter_dimension=0,
            tiled=True,
        ).astype(jnp.float32)
        + back_bias
    )
    cotangent_all = lax.all_gather(out_grad, "tensor", axis=0, tiled=True)
    grad_back = contract_rows(act_low, cotangent_all)
    (dpre,) = gelu_pull(contract_last(cotangent_all, back_full))
    dpre_low = dpre.astype(jnp.bfloat16)
    grad_hidden = contract_rows(norm_two_all, dpre_low)
    grad_hidden_bias = place_block(
        jnp.sum(dpre_low.astype(jnp.float32), axis=0), full_hidden, tensor_rank * local_hidden
    )
    dnorm_two = lax.psum_scatter(
        contract_last(dpre_low, hidden_full), "tensor", scatter_dimension=0, tiled=True
    )
    result = (resid + mixed).astype(jnp.bfloat16)
    dresid_part, grad_gain_two, grad_shift_two = ln2_pull(dnorm_two)
    dresid = out_grad.astype(jnp.float32) + dresid_part
    dbranch = dresid.astype(jnp.bfloat16)
    grad_out_bias = jnp.sum(dbranch.astype(jnp.float32), axis=0)
    dbranch_all = lax.all_gather(dbranch, "tensor", axis=0, tiled=True)
    grad_out = contract_rows(attended, dbranch_all)
    dattended = contract_last(dbranch_all, out_full).astype(jnp.bfloat16)
    dattended_blocks = dattended.reshape(num_blocks, block_rows, heads_here, head_dim)

    def backward_block(carry, element):
        dkey_acc, dvalue_acc = carry
        query_block, dattended_block, log_block, first_row = element
        scores = block_scores(query_block, first_row)
        probs = jnp.exp(scores - log_block[..., None])
        dvalue_acc = dvalue_acc + jnp.einsum(
            "hqk,qhd->khd",
            probs.astype(jnp.bfloat16),
            dattended_block,
            preferred_element_type=jnp.float32,
        )
        dprobs = jnp.einsum(
            "qhd,khd->hqk", dattended_block, value_heads, preferred_element_type=jnp.float32
        )
        dscores = probs * (dprobs - jnp.sum(dprobs * probs, axis=-1, keepdims=True))
        dscores_low = dscores.astype(jnp.bfloat16)
        dquery_block = (
            jnp.einsum("hqk,khd->qhd", dscores_low, key_heads, preferred_element_type=jnp.float32)
            * scale
        )
        dkey_acc = (
            dkey_acc
            + jnp.einsum(
                "hqk,qhd->khd", dscores_low, query_block, preferred_element_type=jnp.float32
            )
            * scale
        )
        return ((dkey_acc, dvalue_acc), dquery_block)

    zero_heads = jnp.zeros((length, heads_here, head_dim), jnp.float32)
    (dkey_acc, dvalue_acc), dquery_blocks = lax.scan(
        backward_block,
        (zero_heads, zero_heads),
        (query_blocks, dattended_blocks, log_totals, starts),
    )
    dqueries = dquery_blocks.reshape(length, local_width).astype(jnp.bfloat16)
    dkeys = dkey_acc.reshape(length, local_width).astype(jnp.bfloat16)
    dvalues = dvalue_acc.reshape(length, local_width).astype(jnp.bfloat16)
    grad_proj = jnp.stack(
        [
            contract_rows(norm_one_all, dqueries),
            contract_rows(norm_one_all, dkeys),
            contract_rows(norm_one_all, dvalues),
        ]
    )
    local_bias_grad = jnp.stack(
        [
            jnp.sum(dqueries.astype(jnp.float32), axis=0),
            jnp.sum(dvalues.astype(jnp.float32), axis=0),
        ]
    )
    grad_proj_bias = place_block(local_bias_grad, model_width, tensor_rank * local_width)
    dnorm_one = lax.psum_scatter(
        (
            contract_last(dqueries, proj_full[0])
            + contract_last(dkeys, proj_full[1])
            + contract_last(dvalues, proj_full[2])
        ).astype(jnp.bfloat16),
        "tensor",
        scatter_dimension=0,
        tiled=True,
    ).astype(jnp.float32)
    dinput_part, grad_gain_one, grad_shift_one = ln1_pull(dnorm_one)
    input_grad = dresid + dinput_part
    summed = (
        lax.psum_scatter(grad_proj, "dp", scatter_dimension=1, tiled=True),
        lax.psum_scatter(grad_out, "dp", scatter_dimension=1, tiled=True),
        lax.psum_scatter(grad_hidden, "dp", scatter_dimension=0, tiled=True),
        lax.psum_scatter(grad_back, "dp", scatter_dimension=1, tiled=True),
        lax.psum_scatter(grad_gain_one, "dp", scatter_dimension=0, tiled=True),
        lax.psum_scatter(grad_shift_one, "dp", scatter_dimension=0, tiled=True),
        lax.psum_scatter(grad_proj_bias, "dp", scatter_dimension=1, tiled=True),
        lax.psum_scatter(grad_out_bias, "dp", scatter_dimension=0, tiled=True),
        lax.psum_scatter(grad_gain_two, "dp", scatter_dimension=0, tiled=True),
        lax.psum_scatter(grad_shift_two, "dp", scatter_dimension=0, tiled=True),
        lax.psum_scatter(grad_hidden_bias, "dp", scatter_dimension=0, tiled=True),
        lax.psum_scatter(grad_back_bias, "dp", scatter_dimension=0, tiled=True),
    )
    vectors = lax.psum(
        (summed[4], summed[5], summed[6], summed[7], summed[8], summed[9], summed[10], summed[11]),
        "tensor",
    )
    return (
        result,
        input_grad,
        vectors[0],
        vectors[1],
        summed[0],
        vectors[2],
        summed[1],
        vectors[3],
        vectors[4],
        vectors[5],
        summed[2],
        vectors[6],
        summed[3],
        vectors[7],
    )


LOW = jnp.bfloat16
SLOT = 64


def settings(mib):
    return pltpu.CompilerParams(vmem_limit_bytes=mib * 2**20)


def cost(flops, moved, exps=0):
    return pl.CostEstimate(
        flops=int(flops), bytes_accessed=int(moved), transcendentals=int(exps)
    )


def whole(shape):
    return pl.BlockSpec(shape, lambda *_: (0,) * len(shape))


def piece_specs(pieces, block, first=0):
    return [
        pl.BlockSpec((piece.shape[0], block), lambda p, *_: (0, first + p)) for piece in pieces
    ]


def fixed_specs(pieces, block, index):
    return [pl.BlockSpec((piece.shape[0], block), lambda *_: (0, index)) for piece in pieces]


def fill_natural(place_ref, scratch, refs):
    for slot, ref in enumerate(refs):
        start = pl.multiple_of(place_ref[4 + slot] * SLOT, SLOT)
        scratch[pl.ds(start, SLOT), :] = ref[...]


def row_stats(rows):
    centre = jnp.mean(rows, axis=-1, keepdims=True)
    shifted = rows - centre
    spread = jnp.mean(shifted * shifted, axis=-1, keepdims=True)
    inverse = lax.rsqrt(spread + epsilon)
    return shifted * inverse, inverse


def norm_back(dnorm, xhat, inverse, gain):
    scaled = dnorm * gain
    return inverse * (
        scaled
        - jnp.mean(scaled, axis=-1, keepdims=True)
        - xhat * jnp.mean(scaled * xhat, axis=-1, keepdims=True)
    )


def attend_pair(qkv_ref, out_ref, log_ref, scale):
    length = qkv_ref.shape[0]
    lane = lax.broadcasted_iota(jnp.int32, (SEG, 128), 1)
    reach = lax.broadcasted_iota(jnp.int32, (SEG, SEG), 0) <= lax.broadcasted_iota(
        jnp.int32, (SEG, SEG), 1
    )
    value_t = jnp.transpose(qkv_ref[:, 256:384])
    for seg in range(length // SEG):
        before = seg * SEG
        rows = slice(before, before + SEG)
        query = qkv_ref[rows, 0:128] * scale
        parts = []
        for head in range(2):
            lanes = slice(head * 64, head * 64 + 64)
            mine = jnp.where(lane // 64 == head, query, jnp.zeros_like(query))
            scores = contract_last(qkv_ref[rows, 128:256], mine)
            scores = jnp.where(reach, scores, -1e30)
            top = jnp.max(scores, axis=0, keepdims=True)
            if seg > 0:
                early = contract_last(qkv_ref[0:before, 128:256], mine)
                top = jnp.maximum(top, jnp.max(early, axis=0, keepdims=True))
            expo = jnp.exp(scores - top)
            total = jnp.sum(expo, axis=0, keepdims=True)
            mixed = matmul(value_t[lanes, rows], expo.astype(LOW))
            if seg > 0:
                expo = jnp.exp(early - top)
                total = total + jnp.sum(expo, axis=0, keepdims=True)
                mixed = mixed + matmul(value_t[lanes, 0:before], expo.astype(LOW))
            parts.append(mixed / total)
            log_ref[0, head : head + 1, rows] = top + jnp.log(total)
        out_ref[rows, :] = jnp.transpose(jnp.concatenate(parts, axis=0)).astype(LOW)


def front_kernel(place_ref, x_ref, vec_ref, bias_ref, *refs, scale, count):
    pieces, outs = refs[:count], refs[count : 2 * count]
    xhat_ref, norm_ref, qkv_ref, att_ref, log_ref, share_ref = refs[2 * count : 2 * count + 6]
    weight_ref, out_ref, joined_ref = refs[2 * count + 6 :]
    length = x_ref.shape[0]
    step = pl.program_id(0)

    @pl.when(step == 0)
    def _():
        for start in range(0, length, SEG):
            rows = slice(start, start + SEG)
            xhat, _ = row_stats(x_ref[rows, :].astype(jnp.float32))
            xhat_ref[rows, :] = xhat.astype(LOW)
            norm_ref[rows, :] = (xhat * vec_ref[0:1, :] + vec_ref[1:2, :]).astype(LOW)
        fill_natural(place_ref, out_ref, outs)

    fill_natural(place_ref, weight_ref, pieces)
    bias = jnp.concatenate(
        [bias_ref[0:1, :], jnp.zeros((1, 128), jnp.float32), bias_ref[1:2, :]], axis=1
    )
    qkv_ref[...] = (matmul(norm_ref[...], weight_ref[...]) + bias).astype(LOW)
    attend_pair(qkv_ref, att_ref, log_ref, scale)
    joined_ref[:, pl.ds(pl.multiple_of(step * 128, 128), 128)] = att_ref[...]

    @pl.when(step == pl.num_programs(0) - 1)
    def _():
        share_ref[...] = contract_last(joined_ref[...], out_ref[...]).astype(LOW)


def front(place, x, vectors, bias, pieces, pairs, scale):
    length, width = x.shape
    once = pl.Buffered(1)
    square = pl.BlockSpec((length, width), lambda *_: (0, 0), pipeline_mode=once)
    return pl.pallas_call(
        functools.partial(front_kernel, scale=scale, count=len(pieces)),
        grid_spec=pltpu.PrefetchScalarGridSpec(
            num_scalar_prefetch=1,
            grid=(pairs,),
            in_specs=[
                square,
                whole(vectors.shape),
                pl.BlockSpec((8, 128), lambda p, place: (0, place[0] * pairs + p)),
            ]
            + piece_specs(pieces, 384)
            + fixed_specs(pieces, pairs * 128, 3),
            out_specs=[
                square,
                square,
                pl.BlockSpec((length, 384), lambda p, _: (0, p)),
                pl.BlockSpec((length, 128), lambda p, _: (0, p)),
                pl.BlockSpec((1, 8, length), lambda p, _: (p, 0, 0)),
                square,
            ],
            scratch_shapes=[
                pltpu.VMEM((width, 384), LOW),
                pltpu.VMEM((width, pairs * 128), LOW),
                pltpu.VMEM((length, pairs * 128), LOW),
            ],
        ),
        out_shape=[
            jax.ShapeDtypeStruct((length, width), LOW),
            jax.ShapeDtypeStruct((length, width), LOW),
            jax.ShapeDtypeStruct((length, pairs * 384), LOW),
            jax.ShapeDtypeStruct((length, pairs * 128), LOW),
            jax.ShapeDtypeStruct((pairs, 8, length), jnp.float32),
            jax.ShapeDtypeStruct((length, width), LOW),
        ],
        compiler_params=settings(56),
        cost_estimate=cost(2 * length * width * pairs * 384 * 4, 12 * length * width),
        name="front",
    )(place, x, vectors, bias, *pieces, *pieces)


def feed_kernel(
    place_ref,
    x_ref,
    own_ref,
    other_ref,
    vec_ref,
    bias_ref,
    grad_ref,
    up_ref,
    down_ref,
    resid_ref,
    left_ref,
    right_ref,
    mixed_ref,
    dnorm_ref,
    sum_ref,
):
    @pl.when(pl.program_id(0) == 0)
    def _():
        sum_ref[...] = jnp.zeros_like(sum_ref)

    branch = own_ref[...].astype(jnp.float32) + other_ref[...].astype(jnp.float32)
    resid = x_ref[...].astype(jnp.float32) + (branch + vec_ref[2:3, :])
    resid_ref[...] = resid.astype(LOW)
    xhat, _ = row_stats(resid)
    norm = (xhat * vec_ref[3:4, :] + vec_ref[4:5, :]).astype(LOW)
    left_ref[0] = norm
    hidden = up_ref.shape[1]
    for start in range(0, hidden, 512):
        columns = slice(start, start + 512)
        pre = matmul(norm, up_ref[:, columns]) + bias_ref[:, columns]
        square = pre * pre
        bent = jnp.tanh(pre * (square * (0.044715 * gelu_coef) + gelu_coef))
        half = 0.5 * bent + 0.5
        act = pre * half
        right_ref[0, :, columns] = act.astype(LOW)
        slope = half + act * (1.0 - bent) * (square * (3 * 0.044715 * gelu_coef) + gelu_coef)
        dpre = (matmul(grad_ref[0], down_ref[:, columns]) * slope).astype(LOW)
        right_ref[1, :, columns] = dpre
        total = jnp.sum(dpre.astype(jnp.float32), axis=0, keepdims=True)
        sum_ref[:, columns] += jnp.broadcast_to(total, (8, 512))
    dnorm_ref[...] = contract_last(right_ref[1], up_ref[...]).astype(LOW)
    mixed_ref[...] = contract_last(right_ref[0], down_ref[...]).astype(LOW)


def feed_product(place, x, own, other, vectors, bias, lefts, pair, block=SEG):
    length, width = x.shape
    hidden = pair.shape[1] // 2
    once = pl.Buffered(1)
    rows = pl.BlockSpec((block, width), lambda p, _: (p, 0))
    return pl.pallas_call(
        feed_kernel,
        grid_spec=pltpu.PrefetchScalarGridSpec(
            num_scalar_prefetch=1,
            grid=(length // block,),
            in_specs=[rows] * 3
            + [
                whole(vectors.shape),
                pl.BlockSpec((1, hidden), lambda p, place: (0, place[0])),
                pl.BlockSpec((1, block, width), lambda p, _: (0, p, 0)),
                pl.BlockSpec((width, hidden), lambda *_: (0, 0), pipeline_mode=once),
                pl.BlockSpec((width, hidden), lambda *_: (0, 1), pipeline_mode=once),
            ],
            out_specs=[
                rows,
                pl.BlockSpec((1, block, width), lambda p, _: (1, p, 0)),
                pl.BlockSpec((2, block, hidden), lambda p, _: (0, p, 0)),
                rows,
                rows,
                whole((8, hidden)),
            ],
        ),
        out_shape=[
            jax.ShapeDtypeStruct((length, width), LOW),
            jax.ShapeDtypeStruct((2, length, width), LOW),
            jax.ShapeDtypeStruct((2, length, hidden), LOW),
            jax.ShapeDtypeStruct((length, width), LOW),
            jax.ShapeDtypeStruct((length, width), LOW),
            jax.ShapeDtypeStruct((8, hidden), jnp.float32),
        ],
        input_output_aliases={6: 1},
        compiler_params=settings(56),
        cost_estimate=cost(9 * length * width * hidden, 40 * length * width),
        name="feed",
    )(place, x, own, other, vectors, bias, lefts, pair, pair)


def mid_kernel(place_ref, resid_ref, own_ref, other_ref, grad_ref, vec_ref, *refs, count):
    pieces = refs[:count]
    dbranch_ref, datt_ref, sum_ref, weight_ref = refs[count:]

    @pl.when(pl.program_id(0) == 0)
    def _():
        fill_natural(place_ref, weight_ref, pieces)
        sum_ref[...] = jnp.zeros_like(sum_ref)

    dnorm = own_ref[...].astype(jnp.float32) + other_ref[...].astype(jnp.float32)
    grad = grad_ref[0].astype(jnp.float32)
    xhat, inverse = row_stats(resid_ref[...].astype(jnp.float32))
    dresid = grad + norm_back(dnorm, xhat, inverse, vec_ref[3:4, :])
    dbranch = dresid.astype(LOW)
    dbranch_ref[...] = dbranch
    datt_ref[...] = matmul(dbranch, weight_ref[...]).astype(LOW)
    for row, value in enumerate((dnorm * xhat, dnorm, dbranch.astype(jnp.float32), grad)):
        sum_ref[row : row + 1, :] += 0.5 * jnp.sum(value, axis=0, keepdims=True)


def mid_product(place, resid, own, other, grad, vectors, pieces, inner):
    length, width = resid.shape
    rows = pl.BlockSpec((SEG, width), lambda p, _: (p, 0))
    return pl.pallas_call(
        functools.partial(mid_kernel, count=len(pieces)),
        grid_spec=pltpu.PrefetchScalarGridSpec(
            num_scalar_prefetch=1,
            grid=(length // SEG,),
            in_specs=[rows] * 3
            + [pl.BlockSpec((1, SEG, width), lambda p, _: (0, p, 0)), whole(vectors.shape)]
            + fixed_specs(pieces, inner, 3),
            out_specs=[
                rows,
                pl.BlockSpec((SEG, inner), lambda p, _: (p, 0)),
                whole((8, width)),
            ],
            scratch_shapes=[pltpu.VMEM((width, inner), LOW)],
        ),
        out_shape=[
            jax.ShapeDtypeStruct((length, width), LOW),
            jax.ShapeDtypeStruct((length, inner), LOW),
            jax.ShapeDtypeStruct((8, width), jnp.float32),
        ],
        compiler_params=settings(56),
        cost_estimate=cost(2 * length * width * inner * 16, 16 * length * width),
        name="mid",
    )(place, resid, own, other, grad, vectors, *pieces)


def attend_back_pair(qkv_ref, grad_ref, log_ref, out_ref, dkey_ref, dvalue_ref, scale):
    length = qkv_ref.shape[0]
    lane = lax.broadcasted_iota(jnp.int32, (SEG, 128), 1)
    reach = lax.broadcasted_iota(jnp.int32, (SEG, SEG), 0) <= lax.broadcasted_iota(
        jnp.int32, (SEG, SEG), 1
    )
    key_t = jnp.transpose(qkv_ref[:, 128:256])
    for seg in reversed(range(length // SEG)):
        before = seg * SEG
        rows = slice(before, before + SEG)
        spans = [rows] if seg == 0 else [rows, slice(0, before)]
        query = qkv_ref[rows, 0:128] * scale
        grad = grad_ref[rows, :]
        parts = []
        dkeys = [None] * len(spans)
        dvalues = [None] * len(spans)
        for head in range(2):
            here = lane // 64 == head
            lanes = slice(head * 64, head * 64 + 64)
            query_mine = jnp.where(here, query, jnp.zeros_like(query))
            grad_mine = jnp.where(here, grad, jnp.zeros_like(grad))
            log_row = log_ref[0, head : head + 1, rows]
            probs, dprobs = [], []
            mean = None
            for index, span in enumerate(spans):
                scores = contract_last(qkv_ref[span, 128:256], query_mine)
                if index == 0:
                    scores = jnp.where(reach, scores, -1e30)
                prob = jnp.exp(scores - log_row)
                dprob = contract_last(qkv_ref[span, 256:384], grad_mine)
                share = jnp.sum(prob * dprob, axis=0, keepdims=True)
                mean = share if mean is None else mean + share
                probs.append(prob)
                dprobs.append(dprob)
            part = None
            for index, span in enumerate(spans):
                dscores = (probs[index] * (dprobs[index] - mean)).astype(LOW)
                dvalue = matmul(probs[index].astype(LOW), grad_mine)
                dkey = matmul(dscores, query_mine)
                piece = matmul(key_t[lanes, span], dscores)
                part = piece if part is None else part + piece
                dkeys[index] = dkey if head == 0 else dkeys[index] + dkey
                dvalues[index] = dvalue if head == 0 else dvalues[index] + dvalue
            parts.append(part * scale)
        for index, span in enumerate(spans):
            if seg == length // SEG - 1:
                dkey_ref[span, :] = dkeys[index]
                dvalue_ref[span, :] = dvalues[index]
            else:
                dkey_ref[span, :] += dkeys[index]
                dvalue_ref[span, :] += dvalues[index]
        out_ref[rows, 0:128] = jnp.transpose(jnp.concatenate(parts, axis=0)).astype(LOW)
    out_ref[:, 128:256] = dkey_ref[...].astype(LOW)
    out_ref[:, 256:384] = dvalue_ref[...].astype(LOW)


def back_kernel(place_ref, xhat_ref, qkv_ref, grad_ref, log_ref, *refs, scale, count):
    pieces = refs[:count]
    dqkv_ref, dnorm_ref, sum_ref, vec_ref = refs[count : count + 4]
    weight_ref, dkey_ref, dvalue_ref, acc_ref = refs[count + 4 :]
    step = pl.program_id(0)
    fill_natural(place_ref, weight_ref, pieces)
    attend_back_pair(qkv_ref, grad_ref, log_ref, dqkv_ref, dkey_ref, dvalue_ref, scale)
    dnorm = contract_last(dqkv_ref[...], weight_ref[...])
    sum_ref[...] = jnp.broadcast_to(
        jnp.sum(dqkv_ref[...].astype(jnp.float32), axis=0, keepdims=True)[None], sum_ref.shape
    )

    @pl.when(step == 0)
    def _():
        acc_ref[...] = dnorm

    @pl.when((step > 0) & (step < pl.num_programs(0) - 1))
    def _():
        acc_ref[...] += dnorm

    @pl.when(step == pl.num_programs(0) - 1)
    def _():
        total = acc_ref[...] + dnorm
        dnorm_ref[...] = total.astype(LOW)
        vec_ref[0:1, :] = jnp.sum(total * xhat_ref[...].astype(jnp.float32), axis=0, keepdims=True)
        vec_ref[1:8, :] = jnp.broadcast_to(
            jnp.sum(total, axis=0, keepdims=True), (7, total.shape[1])
        )


def back_product(place, xhat, qkv, grad, logs, pieces, scale):
    length, columns = qkv.shape
    width = sum(piece.shape[0] for piece in pieces)
    pairs = columns // 384
    return pl.pallas_call(
        functools.partial(back_kernel, scale=scale, count=len(pieces)),
        grid_spec=pltpu.PrefetchScalarGridSpec(
            num_scalar_prefetch=1,
            grid=(pairs,),
            in_specs=[
                whole((length, width)),
                pl.BlockSpec((length, 384), lambda p, _: (0, p)),
                pl.BlockSpec((length, 128), lambda p, _: (0, p)),
                pl.BlockSpec((1, 8, length), lambda p, _: (p, 0, 0)),
            ]
            + piece_specs(pieces, 384),
            out_specs=[
                pl.BlockSpec((length, 384), lambda p, _: (0, p)),
                whole((length, width)),
                pl.BlockSpec((1, 8, 384), lambda p, _: (p, 0, 0)),
                whole((8, width)),
            ],
            scratch_shapes=[
                pltpu.VMEM((width, 384), LOW),
                pltpu.VMEM((length, 128), jnp.float32),
                pltpu.VMEM((length, 128), jnp.float32),
                pltpu.VMEM((length, width), jnp.float32),
            ],
        ),
        out_shape=[
            jax.ShapeDtypeStruct((length, columns), LOW),
            jax.ShapeDtypeStruct((length, width), LOW),
            jax.ShapeDtypeStruct((pairs, 8, 384), jnp.float32),
            jax.ShapeDtypeStruct((8, width), jnp.float32),
        ],
        compiler_params=settings(56),
        cost_estimate=cost(2 * length * width * columns * 48, 12 * length * width),
        name="back",
    )(place, xhat, qkv, grad, logs, *pieces)


def last_kernel(place_ref, x_ref, dbranch_ref, own_ref, other_ref, vec_ref, out_ref):
    dnorm = own_ref[...].astype(jnp.float32) + other_ref[...].astype(jnp.float32)
    xhat, inverse = row_stats(x_ref[...].astype(jnp.float32))
    back = norm_back(dnorm, xhat, inverse, vec_ref[0:1, :])
    out_ref[...] = dbranch_ref[...].astype(jnp.float32) + back


def last_product(place, x, dbranch, own, other, vectors):
    rows, width = other.shape
    block = 128
    steps = rows // block
    mine = pl.BlockSpec((block, width), lambda p, place: (place[0] * steps + p, 0))
    plain = pl.BlockSpec((block, width), lambda p, _: (p, 0))
    return pl.pallas_call(
        last_kernel,
        grid_spec=pltpu.PrefetchScalarGridSpec(
            num_scalar_prefetch=1,
            grid=(steps,),
            in_specs=[plain, mine, mine, plain, whole(vectors.shape)],
            out_specs=plain,
        ),
        out_shape=jax.ShapeDtypeStruct((rows, width), jnp.float32),
        compiler_params=settings(16),
        cost_estimate=cost(40 * rows * width, 320 * rows * width),
        name="last",
    )(place, x, dbranch, own, other, vectors)


def result_kernel(place_ref, resid_ref, own_ref, other_ref, vec_ref, out_ref):
    mixed = own_ref[...].astype(jnp.float32) + other_ref[...].astype(jnp.float32)
    total = resid_ref[...].astype(jnp.float32) + mixed + vec_ref[5:6, :]
    out_ref[...] = total.astype(LOW)


def result_product(place, resid, own, other, vectors):
    rows, width = other.shape
    block = 128
    steps = rows // block
    mine = pl.BlockSpec((block, width), lambda p, place: (place[0] * steps + p, 0))
    plain = pl.BlockSpec((block, width), lambda p, _: (p, 0))
    return pl.pallas_call(
        result_kernel,
        grid_spec=pltpu.PrefetchScalarGridSpec(
            num_scalar_prefetch=1,
            grid=(steps,),
            in_specs=[mine, mine, plain, whole(vectors.shape)],
            out_specs=plain,
        ),
        out_shape=jax.ShapeDtypeStruct((rows, width), LOW),
        compiler_params=settings(16),
        cost_estimate=cost(10 * rows * width, 320 * rows * width),
        name="result",
    )(place, resid, own, other, vectors)


def pack_kernel(proj_ref, out_ref, up_ref, down_ref, vec_ref, narrow_ref, wide_ref):
    columns = proj_ref.shape[2]
    for pair in range(columns // 128):
        for kind in range(3):
            start = (pair * 3 + kind) * 128
            narrow_ref[:, start : start + 128] = proj_ref[kind, :, pair * 128 : pair * 128 + 128]
    narrow_ref[:, 3 * columns : 4 * columns] = out_ref[...]
    turned = jnp.transpose(vec_ref[...].astype(jnp.float32))
    turned = jnp.concatenate([turned, jnp.zeros((SLOT, 112), jnp.float32)], axis=1)
    narrow_ref[:, 4 * columns :] = turned.astype(LOW)
    hidden = up_ref.shape[1]
    wide_ref[:, :hidden] = up_ref[...]
    wide_ref[:, hidden:] = down_ref[...]


def pack_shards(proj, out, up, down, vec):
    rows, columns = out.shape
    return pl.pallas_call(
        pack_kernel,
        out_shape=[
            jax.ShapeDtypeStruct((rows, 4 * columns + 128), LOW),
            jax.ShapeDtypeStruct((rows, 2 * up.shape[1]), LOW),
        ],
        compiler_params=settings(28),
        cost_estimate=cost(0, 4 * rows * (4 * columns + 2 * up.shape[1])),
        name="pack",
    )(proj, out, up, down, vec)


def vector_kernel(place_ref, *refs):
    pieces = refs[:-4]
    vec_ref, bias_ref, hidden_ref, joined_ref = refs[-4:]
    fill_natural(place_ref, joined_ref, pieces)
    turned = jnp.transpose(joined_ref[...]).astype(jnp.float32)
    vec_ref[...] = turned[0:8]
    bias_ref[...] = turned[8:16]
    lane = lax.broadcasted_iota(jnp.int32, (1, 128), 1)
    for pair in range(bias_ref.shape[1] // 128):
        rows = [turned[10 + q : 11 + q, pair * 128 : pair * 128 + 128] for q in range(4)]
        flipped = [pltpu.roll(row, 64, 1) for row in rows]
        for q in (0, 2):
            start = pair * 512 + q * 64
            hidden_ref[:, start : start + 128] = jnp.where(lane < 64, rows[q], flipped[q + 1])
            hidden_ref[:, start + 256 : start + 384] = jnp.where(
                lane < 64, flipped[q], rows[q + 1]
            )


def spread_vectors(place, pieces, index):
    width = sum(piece.shape[0] for piece in pieces)
    return pl.pallas_call(
        vector_kernel,
        grid_spec=pltpu.PrefetchScalarGridSpec(
            num_scalar_prefetch=1,
            grid=(1,),
            in_specs=fixed_specs(pieces, 128, index),
            out_specs=[whole((8, width)), whole((8, width)), whole((1, 4 * width))],
            scratch_shapes=[pltpu.VMEM((width, 128), LOW)],
        ),
        out_shape=[
            jax.ShapeDtypeStruct((8, width), jnp.float32),
            jax.ShapeDtypeStruct((8, width), jnp.float32),
            jax.ShapeDtypeStruct((1, 4 * width), jnp.float32),
        ],
        compiler_params=settings(28),
        cost_estimate=cost(width * 128, 2 * width * 128),
        name="vectors",
    )(place, *pieces)


def after(value, *events):
    return lax.optimization_barrier((value,) + events)[0]


def dp_shift(value, ranks, dz, dy, dc):
    far, near = 4, ranks // 8

    def goes(rank):
        z, y, c = rank // (near * 2), rank // 2 % near, rank % 2
        return ((z + dz) % far * near + (y + dy) % near) * 2 + (c + dc) % 2

    return lax.ppermute(value, "dp", [(rank, goes(rank)) for rank in range(ranks)])


def dp_gather(shard, ranks):
    far = [shard] + [dp_shift(shard, ranks, k, 0, 0) for k in (1, 2, 3)]
    near = [dp_shift(piece, ranks, 0, 1, 0) for piece in far]
    pieces = far + near
    return pieces + [dp_shift(piece, ranks, 0, 0, 1) for piece in pieces], pieces


def reduce_core(left, right, ranks):
    half = left.shape[1] // 2
    return dp_shift(contract_rows(left[:, half:], right).astype(LOW), ranks, 0, 0, 1)


def reduce_near(left, right, other):
    half = left.shape[1] // 2
    part = half // 2
    sent = contract_rows(left[:, part:half], right) + other[part:].astype(jnp.float32)
    return sent.astype(LOW)


def reduce_sum(left, right, other, arrived):
    part = left.shape[1] // 4
    total = contract_rows(left[:, :part], right) + other[:part].astype(jnp.float32)
    return total + arrived.astype(jnp.float32)


def far_send(total, ranks, wire=LOW):
    rows = total.shape[0] // 4
    low = total.astype(wire)
    return [dp_shift(low[k * rows : (k + 1) * rows], ranks, -k, 0, 0) for k in (2, 3, 1)]


def far_sum(total, sent):
    result = total[: total.shape[0] // 4]
    for value in sent:
        result = result + value.astype(jnp.float32)
    return result


def swap(value):
    return lax.ppermute(value, "tensor", [(0, 1), (1, 0)])


def paired(
    inputs,
    out_grad,
    parents,
    ln1_gain,
    ln1_bias,
    w_qkv,
    qv_bias,
    w_attn_out,
    attn_out_bias,
    ln2_gain,
    ln2_bias,
    w_up,
    up_bias,
    w_down,
    down_bias,
):
    ranks = lax.axis_size("dp")
    near = ranks // 8
    rank = lax.axis_index("dp")
    side = lax.axis_index("tensor")
    rows, width = inputs.shape
    shard = width // ranks
    heads_width = w_qkv.shape[2]
    pairs = heads_width // 128
    hidden = w_up.shape[1]
    scale = 1.0 / math.sqrt(width // HEADS)

    slots = jnp.arange(ranks, dtype=jnp.int32)
    core_step, near_step, far_step = slots // (ranks // 2), slots // 4 % near, slots % 4
    my_z, my_y, my_c = rank // (2 * near), rank // 2 % near, rank % 2
    source = ((my_z - far_step) % 4 * near + (my_y - near_step) % near) * 2 + (
        my_c + core_step
    ) % 2
    place = jnp.concatenate([jnp.stack([side, my_z, my_y, my_c]), source]).astype(jnp.int32)
    feature = jnp.repeat(source * shard, shard) + jnp.tile(
        jnp.arange(shard, dtype=jnp.int32), ranks
    )
    to_local = (jnp.arange(width, dtype=jnp.int32)[:, None] == feature[None, :]).astype(LOW)
    slot_of = (slots[:, None] == source[None, :]).astype(jnp.float32)

    zero = jnp.zeros_like(ln1_gain)
    vec = [ln1_gain, ln1_bias, attn_out_bias, ln2_gain, ln2_bias, down_bias, zero, zero]
    vec = jnp.concatenate(
        [jnp.stack(vec), qv_bias, up_bias.reshape(4, shard), jnp.zeros((2, shard), LOW)], axis=0
    )
    narrow_shard, wide_shard = pack_shards(w_qkv, w_attn_out.T, w_up, w_down.T, vec)
    inputs_other = swap(inputs)
    grad_other = swap(after(out_grad, inputs_other))
    narrow, narrow_far = dp_gather(narrow_shard, ranks)
    wide = lax.all_gather(
        after(wide_shard, inputs_other, *narrow_far[1:7]), "dp", axis=0, tiled=True
    )
    vectors, query_bias, hidden_bias = spread_vectors(place, narrow, 16)

    def in_order(own, other):
        return jnp.where(
            side == 0,
            jnp.concatenate([own, other], axis=0),
            jnp.concatenate([other, own], axis=0),
        )

    def other_rows(value):
        return lax.dynamic_slice_in_dim(value, (1 - side) * rows, rows, 0)

    hidden_in = in_order(inputs, inputs_other)
    xhat, norm_one, qkv, attended, logs, share = front(
        place, after(hidden_in, grad_other), vectors, query_bias, narrow, pairs, scale
    )
    cotangent = after(in_order(out_grad, grad_other), share)
    lefts = jnp.stack([cotangent, jnp.zeros_like(cotangent)])
    norm_slot = matmul(after(norm_one, share), to_local).astype(LOW)
    resid, lefts, rights, mixed_share, dnorm_share, dpre_sum = feed_product(
        place, hidden_in, share, swap(share), vectors, hidden_bias, lefts, wide
    )
    dnorm_other = swap(dnorm_share)
    wide_share = lax.dot_general(
        lefts,
        after(rights, dnorm_share),
        (((1,), (1,)), ((0,), (0,))),
        preferred_element_type=jnp.float32,
    ).astype(LOW)
    wide_grad = lax.psum_scatter(wide_share, "dp", scatter_dimension=1, tiled=True)
    dbranch, dattended, mid_sum = mid_product(
        place,
        after(resid, wide_share, norm_slot),
        dnorm_share,
        dnorm_other,
        lefts,
        vectors,
        narrow,
        heads_width,
    )
    dqkv, dnorm_one, dqkv_sum, front_sum = back_product(
        place, xhat, qkv, dattended, logs, narrow, scale
    )
    proj_core = reduce_core(norm_slot, dqkv, ranks)
    dqkv_sum = dqkv_sum[:, 0].reshape(pairs, 3, 128)
    placed = [
        place_block(value, 2 * value.shape[0], side * value.shape[0]).reshape(ranks, -1)
        for value in (
            dqkv_sum[:, 0].reshape(heads_width),
            dqkv_sum[:, 2].reshape(heads_width),
            dpre_sum[0],
        )
    ]
    pack = jnp.stack([front_sum[0], front_sum[1], mid_sum[2], mid_sum[0], mid_sum[1], mid_sum[3]])
    pack = pack.reshape(6, ranks, shard).transpose(1, 0, 2).reshape(ranks, -1)
    pack = lax.dot_general(
        slot_of,
        jnp.concatenate([pack] + placed, axis=1),
        (((0,), (0,)), ((), ())),
        precision=lax.Precision.HIGHEST,
        preferred_element_type=jnp.float32,
    )
    pack = pack + swap(pack)
    pack = pack[: ranks // 2] + dp_shift(pack[ranks // 2 :], ranks, 0, 0, 1)
    back_other = swap(other_rows(after(dnorm_one, pack)))
    dbranch_slot = matmul(after(dbranch, dattended), to_local).astype(LOW)
    out_core = reduce_core(dbranch_slot, attended, ranks)
    slim_near, pack = lax.optimization_barrier(
        (
            jnp.concatenate(
                [
                    reduce_near(norm_slot, dqkv, proj_core),
                    reduce_near(dbranch_slot, attended, out_core),
                ],
                axis=1,
            ),
            pack,
        )
    )
    pack_arrived = dp_shift(pack[ranks // 4 :], ranks, 0, 1, 0)
    slim_arrived = dp_shift(slim_near, ranks, 0, 1, 0)
    own_other = swap(other_rows(after(mixed_share, back_other)))
    slim_arrived, pack_arrived, back_other = lax.optimization_barrier(
        (slim_arrived, pack_arrived, back_other)
    )
    columns = 3 * heads_width
    slim_total, pack_total = lax.optimization_barrier(
        (
            jnp.concatenate(
                [
                    reduce_sum(norm_slot, dqkv, proj_core, slim_arrived[:, :columns]),
                    reduce_sum(dbranch_slot, attended, out_core, slim_arrived[:, columns:]),
                ],
                axis=1,
            ),
            pack[: ranks // 4] + pack_arrived,
        )
    )
    pack = far_sum(pack_total, far_send(pack_total, ranks, jnp.float32)).reshape(-1)
    grad_back = wide_grad[0].T.astype(jnp.float32)
    grad_hidden = wide_grad[1].astype(jnp.float32)
    slim_grad = far_sum(
        after(slim_total, grad_back, grad_hidden), far_send(slim_total, ranks)
    )
    grad_proj = slim_grad[:, :columns]
    grad_out = slim_grad[:, columns:].T
    result = result_product(
        place, after(resid, slim_total), mixed_share, own_other, vectors
    )
    input_grad = last_product(
        place, inputs, dbranch, dnorm_one, after(back_other, slim_total), vectors
    )
    grad_proj = grad_proj.reshape(shard, pairs, 3, 128).transpose(2, 0, 1, 3)
    grad_proj = grad_proj.reshape(3, shard, heads_width)
    vector_grads = [pack[i * shard : (i + 1) * shard] for i in range(6)]
    return (
        result,
        input_grad,
        vector_grads[0],
        vector_grads[1],
        grad_proj,
        pack[6 * shard : 8 * shard].reshape(2, shard),
        grad_out,
        vector_grads[2],
        vector_grads[3],
        vector_grads[4],
        grad_hidden,
        pack[8 * shard :],
        grad_back,
        vector_grads[5],
    )


def local(*arrays):
    fits = lax.axis_size("tensor") == 2 and lax.axis_size("dp") == 16
    if fits and arrays[2].shape[1] == 3:
        return paired(*arrays)
    return generic(*arrays)


def solution(mesh):
    return jax.shard_map(
        local,
        mesh=mesh,
        in_specs=(
            P(("dp", "tensor"), None),
            P(("dp", "tensor"), None),
            P("dp", None),
            P("dp"),
            P("dp"),
            P(None, "dp", "tensor"),
            P(None, "dp"),
            P("tensor", "dp"),
            P("dp"),
            P("dp"),
            P("dp"),
            P("dp", "tensor"),
            P("dp"),
            P("tensor", "dp"),
            P("dp"),
        ),
        out_specs=(
            P(("dp", "tensor"), None),
            P(("dp", "tensor"), None),
            P("dp"),
            P("dp"),
            P(None, "dp", "tensor"),
            P(None, "dp"),
            P("tensor", "dp"),
            P("dp"),
            P("dp"),
            P("dp"),
            P("dp", "tensor"),
            P("dp"),
            P("tensor", "dp"),
            P("dp"),
        ),
        check_vma=False,
    )
```

```python
import functools
import math

import jax
import jax.numpy as jnp
from jax import lax
from jax.experimental import pallas as pl
from jax.experimental.pallas import tpu as pltpu
from jax.sharding import PartitionSpec as P

HEADS = 16
SEG = 256


epsilon = 1e-05
gelu_coef = 0.7978845608028654


def layer_norm(values, scales, shifts):
    centre = jnp.mean(values, axis=-1, keepdims=True)
    shifted = values - centre
    spread = jnp.mean(shifted * shifted, axis=-1, keepdims=True)
    return shifted * lax.rsqrt(spread + epsilon) * scales + shifts


def gelu_tanh(values):
    return (
        0.5 * values * (1.0 + jnp.tanh(gelu_coef * (values + 0.044715 * values * values * values)))
    )


def matmul(left, right):
    return jnp.dot(left, right, preferred_element_type=jnp.float32)


def contract_rows(left, right):
    return lax.dot_general(
        left, right, (((0,), (0,)), ((), ())), preferred_element_type=jnp.float32
    )


def contract_last(left, right):
    return lax.dot_general(
        left, right, (((1,), (1,)), ((), ())), preferred_element_type=jnp.float32
    )


def ancestors(parent_row, segment_count):
    labels = jnp.arange(segment_count, dtype=jnp.int32)
    links = ((parent_row[:, None] == labels[None, :]) & (labels[:, None] > 0)).astype(jnp.float32)
    identity = jnp.eye(segment_count, dtype=jnp.float32)

    def extend(turn, reached):
        grown = jnp.dot(
            links, reached, precision=lax.Precision.HIGHEST, preferred_element_type=jnp.float32
        )
        return jnp.minimum(identity + grown, 1.0)

    return lax.fori_loop(0, segment_count, extend, identity)


def tree_mask(reached, first_row, block_rows, length):
    query_pos = first_row + jnp.arange(block_rows, dtype=jnp.int32)
    key_pos = jnp.arange(length, dtype=jnp.int32)
    segment_count = reached.shape[0]
    onehot = (
        (query_pos // SEG)[:, None] == jnp.arange(segment_count, dtype=jnp.int32)[None, :]
    ).astype(jnp.float32)
    row_reach = jnp.dot(
        onehot, reached, precision=lax.Precision.HIGHEST, preferred_element_type=jnp.float32
    )
    spread_out = jnp.repeat(row_reach, SEG, axis=1)
    return (spread_out > 0.5) & (key_pos[None, :] <= query_pos[:, None])


def row_block(length):
    pieces = -(-length // 512)
    while length % pieces:
        pieces += 1
    return length // pieces


def place_block(local_vec, full_length, offset):
    empty_vec = jnp.zeros(local_vec.shape[:-1] + (full_length,), jnp.float32)
    return lax.dynamic_update_slice_in_dim(empty_vec, local_vec, offset, local_vec.ndim - 1)


def generic(
    inputs,
    out_grad,
    parents,
    ln1_gain,
    ln1_bias,
    w_qkv,
    qv_bias,
    w_attn_out,
    attn_out_bias,
    ln2_gain,
    ln2_bias,
    w_up,
    up_bias,
    w_down,
    down_bias,
):
    tensor_ranks = lax.axis_size("tensor")
    tensor_rank = lax.axis_index("tensor")
    rows_own = inputs.shape[0]
    length = rows_own * tensor_ranks
    model_width = inputs.shape[1]
    head_dim = model_width // HEADS
    local_width = w_qkv.shape[2]
    local_hidden = w_up.shape[1]
    heads_here = local_width // head_dim
    scale = 1.0 / math.sqrt(head_dim)
    gathered = (
        lax.all_gather(w_qkv, "dp", axis=1, tiled=True),
        lax.all_gather(w_attn_out, "dp", axis=1, tiled=True),
        lax.all_gather(w_up, "dp", axis=0, tiled=True),
        lax.all_gather(w_down, "dp", axis=1, tiled=True),
        lax.all_gather(ln1_gain, "dp", axis=0, tiled=True),
        lax.all_gather(ln1_bias, "dp", axis=0, tiled=True),
        lax.all_gather(qv_bias, "dp", axis=1, tiled=True),
        lax.all_gather(attn_out_bias, "dp", axis=0, tiled=True),
        lax.all_gather(ln2_gain, "dp", axis=0, tiled=True),
        lax.all_gather(ln2_bias, "dp", axis=0, tiled=True),
        lax.all_gather(up_bias, "dp", axis=0, tiled=True),
        lax.all_gather(down_bias, "dp", axis=0, tiled=True),
    )
    proj_full, out_full, hidden_full, back_full = (
        gathered[0],
        gathered[1],
        gathered[2],
        gathered[3],
    )
    gain_one = gathered[4].astype(jnp.float32)
    shift_one = gathered[5].astype(jnp.float32)
    proj_bias = lax.dynamic_slice_in_dim(
        gathered[6].astype(jnp.float32), tensor_rank * local_width, local_width, 1
    )
    out_bias = gathered[7].astype(jnp.float32)
    gain_two = gathered[8].astype(jnp.float32)
    shift_two = gathered[9].astype(jnp.float32)
    hidden_bias_full = gathered[10].astype(jnp.float32)
    back_bias = gathered[11].astype(jnp.float32)
    full_hidden = hidden_bias_full.shape[0]
    hidden_in = inputs.astype(jnp.float32)
    norm_one, ln1_pull = jax.vjp(layer_norm, hidden_in, gain_one, shift_one)
    norm_one_all = lax.all_gather(norm_one.astype(jnp.bfloat16), "tensor", axis=0, tiled=True)
    queries = (matmul(norm_one_all, proj_full[0]) + proj_bias[0]).astype(jnp.bfloat16)
    keys_low = matmul(norm_one_all, proj_full[1]).astype(jnp.bfloat16)
    values_low = (matmul(norm_one_all, proj_full[2]) + proj_bias[1]).astype(jnp.bfloat16)
    reached = ancestors(parents[0], length // SEG)
    block_rows = row_block(length)
    num_blocks = length // block_rows
    starts = jnp.arange(num_blocks, dtype=jnp.int32) * block_rows
    query_blocks = queries.reshape(num_blocks, block_rows, heads_here, head_dim)
    key_heads = keys_low.reshape(length, heads_here, head_dim)
    value_heads = values_low.reshape(length, heads_here, head_dim)

    def block_scores(query_block, first_row):
        scores = (
            jnp.einsum("qhd,khd->hqk", query_block, key_heads, preferred_element_type=jnp.float32)
            * scale
        )
        allowed = tree_mask(reached, first_row, block_rows, length)
        return jnp.where(allowed[None], scores, -1e30)

    def forward_block(element):
        query_block, first_row = element
        scores = block_scores(query_block, first_row)
        top_score = jnp.max(scores, axis=-1, keepdims=True)
        expo = jnp.exp(scores - top_score)
        totals = jnp.sum(expo, axis=-1, keepdims=True)
        probs = (expo / totals).astype(jnp.bfloat16)
        attended_block = jnp.einsum(
            "hqk,khd->qhd", probs, value_heads, preferred_element_type=jnp.float32
        )
        return (attended_block, (top_score + jnp.log(totals))[..., 0])

    attended_blocks, log_totals = lax.map(forward_block, (query_blocks, starts))
    attended = attended_blocks.reshape(length, local_width).astype(jnp.bfloat16)
    branch = (
        lax.psum_scatter(matmul(attended, out_full), "tensor", scatter_dimension=0, tiled=True)
        + out_bias
    )
    resid = hidden_in + branch
    norm_two, ln2_pull = jax.vjp(layer_norm, resid, gain_two, shift_two)
    norm_two_low = norm_two.astype(jnp.bfloat16)
    grad_back_bias = jnp.sum(out_grad.astype(jnp.float32), axis=0)
    norm_two_all = lax.all_gather(norm_two_low, "tensor", axis=0, tiled=True)
    hidden_slice = lax.dynamic_slice_in_dim(
        hidden_bias_full, tensor_rank * local_hidden, local_hidden, 0
    )
    pre = matmul(norm_two_all, hidden_full) + hidden_slice
    act, gelu_pull = jax.vjp(gelu_tanh, pre)
    act_low = act.astype(jnp.bfloat16)
    mixed = (
        lax.psum_scatter(
            matmul(act_low, back_full).astype(jnp.bfloat16),
            "tensor",
            scatter_dimension=0,
            tiled=True,
        ).astype(jnp.float32)
        + back_bias
    )
    cotangent_all = lax.all_gather(out_grad, "tensor", axis=0, tiled=True)
    grad_back = contract_rows(act_low, cotangent_all)
    (dpre,) = gelu_pull(contract_last(cotangent_all, back_full))
    dpre_low = dpre.astype(jnp.bfloat16)
    grad_hidden = contract_rows(norm_two_all, dpre_low)
    grad_hidden_bias = place_block(
        jnp.sum(dpre_low.astype(jnp.float32), axis=0), full_hidden, tensor_rank * local_hidden
    )
    dnorm_two = lax.psum_scatter(
        contract_last(dpre_low, hidden_full), "tensor", scatter_dimension=0, tiled=True
    )
    result = (resid + mixed).astype(jnp.bfloat16)
    dresid_part, grad_gain_two, grad_shift_two = ln2_pull(dnorm_two)
    dresid = out_grad.astype(jnp.float32) + dresid_part
    dbranch = dresid.astype(jnp.bfloat16)
    grad_out_bias = jnp.sum(dbranch.astype(jnp.float32), axis=0)
    dbranch_all = lax.all_gather(dbranch, "tensor", axis=0, tiled=True)
    grad_out = contract_rows(attended, dbranch_all)
    dattended = contract_last(dbranch_all, out_full).astype(jnp.bfloat16)
    dattended_blocks = dattended.reshape(num_blocks, block_rows, heads_here, head_dim)

    def backward_block(carry, element):
        dkey_acc, dvalue_acc = carry
        query_block, dattended_block, log_block, first_row = element
        scores = block_scores(query_block, first_row)
        probs = jnp.exp(scores - log_block[..., None])
        dvalue_acc = dvalue_acc + jnp.einsum(
            "hqk,qhd->khd",
            probs.astype(jnp.bfloat16),
            dattended_block,
            preferred_element_type=jnp.float32,
        )
        dprobs = jnp.einsum(
            "qhd,khd->hqk", dattended_block, value_heads, preferred_element_type=jnp.float32
        )
        dscores = probs * (dprobs - jnp.sum(dprobs * probs, axis=-1, keepdims=True))
        dscores_low = dscores.astype(jnp.bfloat16)
        dquery_block = (
            jnp.einsum("hqk,khd->qhd", dscores_low, key_heads, preferred_element_type=jnp.float32)
            * scale
        )
        dkey_acc = (
            dkey_acc
            + jnp.einsum(
                "hqk,qhd->khd", dscores_low, query_block, preferred_element_type=jnp.float32
            )
            * scale
        )
        return ((dkey_acc, dvalue_acc), dquery_block)

    zero_heads = jnp.zeros((length, heads_here, head_dim), jnp.float32)
    (dkey_acc, dvalue_acc), dquery_blocks = lax.scan(
        backward_block,
        (zero_heads, zero_heads),
        (query_blocks, dattended_blocks, log_totals, starts),
    )
    dqueries = dquery_blocks.reshape(length, local_width).astype(jnp.bfloat16)
    dkeys = dkey_acc.reshape(length, local_width).astype(jnp.bfloat16)
    dvalues = dvalue_acc.reshape(length, local_width).astype(jnp.bfloat16)
    grad_proj = jnp.stack(
        [
            contract_rows(norm_one_all, dqueries),
            contract_rows(norm_one_all, dkeys),
            contract_rows(norm_one_all, dvalues),
        ]
    )
    local_bias_grad = jnp.stack(
        [
            jnp.sum(dqueries.astype(jnp.float32), axis=0),
            jnp.sum(dvalues.astype(jnp.float32), axis=0),
        ]
    )
    grad_proj_bias = place_block(local_bias_grad, model_width, tensor_rank * local_width)
    dnorm_one = lax.psum_scatter(
        (
            contract_last(dqueries, proj_full[0])
            + contract_last(dkeys, proj_full[1])
            + contract_last(dvalues, proj_full[2])
        ).astype(jnp.bfloat16),
        "tensor",
        scatter_dimension=0,
        tiled=True,
    ).astype(jnp.float32)
    dinput_part, grad_gain_one, grad_shift_one = ln1_pull(dnorm_one)
    input_grad = dresid + dinput_part
    summed = (
        lax.psum_scatter(grad_proj, "dp", scatter_dimension=1, tiled=True),
        lax.psum_scatter(grad_out, "dp", scatter_dimension=1, tiled=True),
        lax.psum_scatter(grad_hidden, "dp", scatter_dimension=0, tiled=True),
        lax.psum_scatter(grad_back, "dp", scatter_dimension=1, tiled=True),
        lax.psum_scatter(grad_gain_one, "dp", scatter_dimension=0, tiled=True),
        lax.psum_scatter(grad_shift_one, "dp", scatter_dimension=0, tiled=True),
        lax.psum_scatter(grad_proj_bias, "dp", scatter_dimension=1, tiled=True),
        lax.psum_scatter(grad_out_bias, "dp", scatter_dimension=0, tiled=True),
        lax.psum_scatter(grad_gain_two, "dp", scatter_dimension=0, tiled=True),
        lax.psum_scatter(grad_shift_two, "dp", scatter_dimension=0, tiled=True),
        lax.psum_scatter(grad_hidden_bias, "dp", scatter_dimension=0, tiled=True),
        lax.psum_scatter(grad_back_bias, "dp", scatter_dimension=0, tiled=True),
    )
    vectors = lax.psum(
        (summed[4], summed[5], summed[6], summed[7], summed[8], summed[9], summed[10], summed[11]),
        "tensor",
    )
    return (
        result,
        input_grad,
        vectors[0],
        vectors[1],
        summed[0],
        vectors[2],
        summed[1],
        vectors[3],
        vectors[4],
        vectors[5],
        summed[2],
        vectors[6],
        summed[3],
        vectors[7],
    )


LOW = jnp.bfloat16
SLOT = 64


def settings(mib):
    return pltpu.CompilerParams(vmem_limit_bytes=mib * 2**20)


def cost(flops, moved, exps=0):
    return pl.CostEstimate(
        flops=int(flops), bytes_accessed=int(moved), transcendentals=int(exps)
    )


def whole(shape):
    return pl.BlockSpec(shape, lambda *_: (0,) * len(shape))


def piece_specs(pieces, block, first=0):
    return [
        pl.BlockSpec((piece.shape[0], block), lambda p, *_: (0, first + p)) for piece in pieces
    ]


def fixed_specs(pieces, block, index):
    return [pl.BlockSpec((piece.shape[0], block), lambda *_: (0, index)) for piece in pieces]


def fill_natural(place_ref, scratch, refs):
    for slot, ref in enumerate(refs):
        start = pl.multiple_of(place_ref[4 + slot] * SLOT, SLOT)
        scratch[pl.ds(start, SLOT), :] = ref[...]


def row_stats(rows):
    centre = jnp.mean(rows, axis=-1, keepdims=True)
    shifted = rows - centre
    spread = jnp.mean(shifted * shifted, axis=-1, keepdims=True)
    inverse = lax.rsqrt(spread + epsilon)
    return shifted * inverse, inverse


def norm_back(dnorm, xhat, inverse, gain):
    scaled = dnorm * gain
    return inverse * (
        scaled
        - jnp.mean(scaled, axis=-1, keepdims=True)
        - xhat * jnp.mean(scaled * xhat, axis=-1, keepdims=True)
    )


def attend_pair(qkv_ref, out_ref, log_ref, scale):
    length = qkv_ref.shape[0]
    lane = lax.broadcasted_iota(jnp.int32, (SEG, 128), 1)
    reach = lax.broadcasted_iota(jnp.int32, (SEG, SEG), 0) <= lax.broadcasted_iota(
        jnp.int32, (SEG, SEG), 1
    )
    value_t = jnp.transpose(qkv_ref[:, 256:384])
    for seg in range(length // SEG):
        before = seg * SEG
        rows = slice(before, before + SEG)
        query = qkv_ref[rows, 0:128] * scale
        parts = []
        drawn = []
        for head in range(2):
            mine = jnp.where(lane // 64 == head, query, jnp.zeros_like(query))
            scores = contract_last(qkv_ref[rows, 128:256], mine)
            early = contract_last(qkv_ref[0:before, 128:256], mine) if seg > 0 else None
            drawn.append((jnp.where(reach, scores, -1e30), early))
        for head in range(2):
            lanes = slice(head * 64, head * 64 + 64)
            scores, early = drawn[head]
            top = jnp.max(scores, axis=0, keepdims=True)
            if seg > 0:
                top = jnp.maximum(top, jnp.max(early, axis=0, keepdims=True))
            expo = jnp.exp(scores - top)
            total = jnp.sum(expo, axis=0, keepdims=True)
            mixed = matmul(value_t[lanes, rows], expo.astype(LOW))
            if seg > 0:
                expo = jnp.exp(early - top)
                total = total + jnp.sum(expo, axis=0, keepdims=True)
                mixed = mixed + matmul(value_t[lanes, 0:before], expo.astype(LOW))
            parts.append(mixed / total)
            log_ref[0, head : head + 1, rows] = top + jnp.log(total)
        out_ref[rows, :] = jnp.transpose(jnp.concatenate(parts, axis=0)).astype(LOW)


def front_kernel(place_ref, own_ref, other_ref, vec_ref, bias_ref, *refs, scale, count):
    pieces, outs = refs[:count], refs[count : 2 * count]
    x_ref, xhat_ref, norm_ref, qkv_ref, att_ref, log_ref = refs[2 * count : 2 * count + 6]
    share_ref, weight_ref, out_ref, joined_ref = refs[2 * count + 6 :]
    rows_own = own_ref.shape[0]
    step = pl.program_id(0)

    @pl.when(step == 0)
    def _():
        for half, ref in ((place_ref[0], own_ref), (1 - place_ref[0], other_ref)):
            for start in range(0, rows_own, 128):
                rows = pl.ds(pl.multiple_of(half * rows_own + start, 128), 128)
                x = ref[start : start + 128, :]
                xhat, _ = row_stats(x.astype(jnp.float32))
                x_ref[rows, :] = x
                xhat_ref[rows, :] = xhat.astype(LOW)
                norm_ref[rows, :] = (xhat * vec_ref[0:1, :] + vec_ref[1:2, :]).astype(LOW)
        fill_natural(place_ref, out_ref, outs)

    fill_natural(place_ref, weight_ref, pieces)
    bias = jnp.concatenate(
        [bias_ref[0:1, :], jnp.zeros((1, 128), jnp.float32), bias_ref[1:2, :]], axis=1
    )
    qkv_ref[...] = (matmul(norm_ref[...], weight_ref[...]) + bias).astype(LOW)
    attend_pair(qkv_ref, att_ref, log_ref, scale)
    joined_ref[:, pl.ds(pl.multiple_of(step * 128, 128), 128)] = att_ref[...]

    @pl.when(step == pl.num_programs(0) - 1)
    def _():
        share_ref[...] = contract_last(joined_ref[...], out_ref[...]).astype(LOW)


def front(place, own, other, vectors, bias, pieces, pairs, scale):
    length, width = 2 * own.shape[0], own.shape[1]
    once = pl.Buffered(1)
    square = pl.BlockSpec((length, width), lambda *_: (0, 0), pipeline_mode=once)
    half = pl.BlockSpec(own.shape, lambda *_: (0, 0), pipeline_mode=once)
    return pl.pallas_call(
        functools.partial(front_kernel, scale=scale, count=len(pieces)),
        grid_spec=pltpu.PrefetchScalarGridSpec(
            num_scalar_prefetch=1,
            grid=(pairs,),
            in_specs=[
                half,
                half,
                whole(vectors.shape),
                pl.BlockSpec((8, 128), lambda p, place: (0, place[0] * pairs + p)),
            ]
            + piece_specs(pieces, 384)
            + fixed_specs(pieces, pairs * 128, 3),
            out_specs=[
                square,
                square,
                square,
                pl.BlockSpec((length, 384), lambda p, _: (0, p)),
                pl.BlockSpec((length, 128), lambda p, _: (0, p)),
                pl.BlockSpec((1, 8, length), lambda p, _: (p, 0, 0)),
                square,
                pl.BlockSpec((width, 384), lambda p, _: (0, p)),
                pl.BlockSpec((width, pairs * 128), lambda *_: (0, 0), pipeline_mode=once),
            ],
            scratch_shapes=[pltpu.VMEM((length, pairs * 128), LOW)],
        ),
        out_shape=[
            jax.ShapeDtypeStruct((length, width), LOW),
            jax.ShapeDtypeStruct((length, width), LOW),
            jax.ShapeDtypeStruct((length, width), LOW),
            jax.ShapeDtypeStruct((length, pairs * 384), LOW),
            jax.ShapeDtypeStruct((length, pairs * 128), LOW),
            jax.ShapeDtypeStruct((pairs, 8, length), jnp.float32),
            jax.ShapeDtypeStruct((length, width), LOW),
            jax.ShapeDtypeStruct((width, pairs * 384), LOW),
            jax.ShapeDtypeStruct((width, pairs * 128), LOW),
        ],
        compiler_params=settings(56),
        cost_estimate=cost(2 * length * width * pairs * 384 * 4, 12 * length * width),
        name="front",
    )(place, own, other, vectors, bias, *pieces, *pieces)


def feed_kernel(
    place_ref,
    x_ref,
    own_ref,
    other_ref,
    vec_ref,
    bias_ref,
    grad_ref,
    pair_ref,
    resid_ref,
    left_ref,
    right_ref,
    dnorm_ref,
    sum_ref,
    up_ref,
    down_ref,
    sem,
):
    first = pl.program_id(0) == 0
    hidden = up_ref.shape[1]

    def fetch(start):
        part = pl.ds(start, 512)
        index = start // 512
        return (
            pltpu.make_async_copy(pair_ref.at[:, part], up_ref.at[:, part], sem.at[0, index]),
            pltpu.make_async_copy(
                pair_ref.at[:, pl.ds(hidden + start, 512)], down_ref.at[:, part], sem.at[1, index]
            ),
        )

    @pl.when(first)
    def _():
        for start in range(0, hidden, 512):
            for copy in fetch(start):
                copy.start()
        sum_ref[...] = jnp.zeros_like(sum_ref)

    branch = own_ref[...].astype(jnp.float32) + other_ref[...].astype(jnp.float32)
    resid = x_ref[...].astype(jnp.float32) + (branch + vec_ref[2:3, :])
    resid_ref[...] = resid.astype(LOW)
    xhat, _ = row_stats(resid)
    norm = (xhat * vec_ref[3:4, :] + vec_ref[4:5, :]).astype(LOW)
    left_ref[0] = norm
    for start in range(0, hidden, 512):
        columns = slice(start, start + 512)

        @pl.when(first)
        def _(start=start):
            for copy in fetch(start):
                copy.wait()

        pre = matmul(norm, up_ref[:, columns]) + bias_ref[:, columns]
        square = pre * pre
        bent = jnp.tanh(pre * (square * (0.044715 * gelu_coef) + gelu_coef))
        half = 0.5 * bent + 0.5
        act = pre * half
        right_ref[0, :, columns] = act.astype(LOW)
        slope = half + act * (1.0 - bent) * (square * (3 * 0.044715 * gelu_coef) + gelu_coef)
        dpre = (matmul(grad_ref[0], down_ref[:, columns]) * slope).astype(LOW)
        right_ref[1, :, columns] = dpre
        total = jnp.sum(dpre.astype(jnp.float32), axis=0, keepdims=True)
        sum_ref[:, columns] += jnp.broadcast_to(total, (8, 512))
    dnorm_ref[...] = contract_last(right_ref[1], up_ref[...]).astype(LOW)


def feed_product(place, x, own, other, vectors, bias, lefts, pair, block=SEG):
    length, width = x.shape
    hidden = pair.shape[1] // 2
    rows = pl.BlockSpec((block, width), lambda p, _: (p, 0))
    return pl.pallas_call(
        feed_kernel,
        grid_spec=pltpu.PrefetchScalarGridSpec(
            num_scalar_prefetch=1,
            grid=(length // block,),
            in_specs=[rows] * 3
            + [
                whole(vectors.shape),
                pl.BlockSpec((1, hidden), lambda p, place: (0, place[0])),
                pl.BlockSpec((1, block, width), lambda p, _: (0, p, 0)),
                pl.BlockSpec(memory_space=pl.ANY),
            ],
            out_specs=[
                rows,
                pl.BlockSpec((1, block, width), lambda p, _: (1, p, 0)),
                pl.BlockSpec((2, block, hidden), lambda p, _: (0, p, 0)),
                rows,
                whole((8, hidden)),
            ],
            scratch_shapes=[
                pltpu.VMEM((width, hidden), LOW),
                pltpu.VMEM((width, hidden), LOW),
                pltpu.SemaphoreType.DMA((2, hidden // 512)),
            ],
        ),
        out_shape=[
            jax.ShapeDtypeStruct((length, width), LOW),
            jax.ShapeDtypeStruct((2, length, width), LOW),
            jax.ShapeDtypeStruct((2, length, hidden), LOW),
            jax.ShapeDtypeStruct((length, width), LOW),
            jax.ShapeDtypeStruct((8, hidden), jnp.float32),
        ],
        input_output_aliases={6: 1},
        compiler_params=settings(56),
        cost_estimate=cost(9 * length * width * hidden, 40 * length * width),
        name="feed",
    )(place, x, own, other, vectors, bias, lefts, pair)


def mid_kernel(
    resid_ref, own_ref, other_ref, grad_ref, vec_ref, weight_ref, dbranch_ref, datt_ref, sum_ref
):
    @pl.when(pl.program_id(0) == 0)
    def _():
        sum_ref[...] = jnp.zeros_like(sum_ref)

    dnorm = own_ref[...].astype(jnp.float32) + other_ref[...].astype(jnp.float32)
    grad = grad_ref[0].astype(jnp.float32)
    xhat, inverse = row_stats(resid_ref[...].astype(jnp.float32))
    dresid = grad + norm_back(dnorm, xhat, inverse, vec_ref[3:4, :])
    dbranch = dresid.astype(LOW)
    dbranch_ref[...] = dbranch
    datt_ref[...] = matmul(dbranch, weight_ref[...]).astype(LOW)
    for row, value in enumerate((dnorm * xhat, dnorm, dbranch.astype(jnp.float32), grad)):
        sum_ref[row : row + 1, :] += 0.5 * jnp.sum(value, axis=0, keepdims=True)


def mid_product(resid, own, other, lefts, vectors, weight, block=SEG):
    length, width = resid.shape
    inner = weight.shape[1]
    rows = pl.BlockSpec((block, width), lambda p: (p, 0))
    return pl.pallas_call(
        mid_kernel,
        grid=(length // block,),
        in_specs=[rows] * 3
        + [
            pl.BlockSpec((1, block, width), lambda p: (0, p, 0)),
            whole(vectors.shape),
            whole(weight.shape),
        ],
        out_specs=[rows, pl.BlockSpec((block, inner), lambda p: (p, 0)), whole((8, width))],
        out_shape=[
            jax.ShapeDtypeStruct((length, width), LOW),
            jax.ShapeDtypeStruct((length, inner), LOW),
            jax.ShapeDtypeStruct((8, width), jnp.float32),
        ],
        compiler_params=settings(56),
        cost_estimate=cost(2 * length * width * inner * 16, 16 * length * width),
        name="mid",
    )(resid, own, other, lefts, vectors, weight)


def attend_back_pair(qkv_ref, grad_ref, log_ref, out_ref, dkey_ref, dvalue_ref, scale):
    length = qkv_ref.shape[0]
    lane = lax.broadcasted_iota(jnp.int32, (SEG, 128), 1)
    reach = lax.broadcasted_iota(jnp.int32, (SEG, SEG), 0) <= lax.broadcasted_iota(
        jnp.int32, (SEG, SEG), 1
    )
    key_t = jnp.transpose(qkv_ref[:, 128:256])
    for seg in reversed(range(length // SEG)):
        before = seg * SEG
        rows = slice(before, before + SEG)
        spans = [rows] if seg == 0 else [rows, slice(0, before)]
        query = qkv_ref[rows, 0:128] * scale
        grad = grad_ref[rows, :]
        parts = []
        dkeys = [None] * len(spans)
        dvalues = [None] * len(spans)
        drawn = []
        for head in range(2):
            here = lane // 64 == head
            query_mine = jnp.where(here, query, jnp.zeros_like(query))
            grad_mine = jnp.where(here, grad, jnp.zeros_like(grad))
            scores = [contract_last(qkv_ref[span, 128:256], query_mine) for span in spans]
            scores[0] = jnp.where(reach, scores[0], -1e30)
            dprobs = [contract_last(qkv_ref[span, 256:384], grad_mine) for span in spans]
            drawn.append((query_mine, grad_mine, scores, dprobs))
        for head in range(2):
            lanes = slice(head * 64, head * 64 + 64)
            query_mine, grad_mine, scores, dprobs = drawn[head]
            log_row = log_ref[0, head : head + 1, rows]
            probs = []
            mean = None
            for index in range(len(spans)):
                prob = jnp.exp(scores[index] - log_row)
                share = jnp.sum(prob * dprobs[index], axis=0, keepdims=True)
                mean = share if mean is None else mean + share
                probs.append(prob)
            part = None
            for index, span in enumerate(spans):
                dscores = (probs[index] * (dprobs[index] - mean)).astype(LOW)
                dvalue = matmul(probs[index].astype(LOW), grad_mine)
                dkey = matmul(dscores, query_mine)
                piece = matmul(key_t[lanes, span], dscores)
                part = piece if part is None else part + piece
                dkeys[index] = dkey if head == 0 else dkeys[index] + dkey
                dvalues[index] = dvalue if head == 0 else dvalues[index] + dvalue
            parts.append(part * scale)
        for index, span in enumerate(spans):
            if seg == length // SEG - 1:
                dkey_ref[span, :] = dkeys[index]
                dvalue_ref[span, :] = dvalues[index]
            else:
                dkey_ref[span, :] += dkeys[index]
                dvalue_ref[span, :] += dvalues[index]
        out_ref[rows, 0:128] = jnp.transpose(jnp.concatenate(parts, axis=0)).astype(LOW)
    out_ref[:, 128:256] = dkey_ref[...].astype(LOW)
    out_ref[:, 256:384] = dvalue_ref[...].astype(LOW)


def back_kernel(
    xhat_ref,
    qkv_ref,
    grad_ref,
    log_ref,
    weight_ref,
    dqkv_ref,
    dnorm_ref,
    sum_ref,
    vec_ref,
    dkey_ref,
    dvalue_ref,
    acc_ref,
    *,
    scale,
):
    step = pl.program_id(0)
    attend_back_pair(qkv_ref, grad_ref, log_ref, dqkv_ref, dkey_ref, dvalue_ref, scale)
    dnorm = contract_last(dqkv_ref[...], weight_ref[...])
    sum_ref[...] = jnp.broadcast_to(
        jnp.sum(dqkv_ref[...].astype(jnp.float32), axis=0, keepdims=True)[None], sum_ref.shape
    )

    @pl.when(step == 0)
    def _():
        acc_ref[...] = dnorm

    @pl.when((step > 0) & (step < pl.num_programs(0) - 1))
    def _():
        acc_ref[...] += dnorm

    @pl.when(step == pl.num_programs(0) - 1)
    def _():
        total = acc_ref[...] + dnorm
        dnorm_ref[...] = total.astype(LOW)
        vec_ref[0:1, :] = jnp.sum(total * xhat_ref[...].astype(jnp.float32), axis=0, keepdims=True)
        vec_ref[1:8, :] = jnp.broadcast_to(
            jnp.sum(total, axis=0, keepdims=True), (7, total.shape[1])
        )


def back_product(xhat, qkv, grad, logs, weight, scale):
    length, columns = qkv.shape
    width = weight.shape[0]
    pairs = columns // 384
    once = pl.Buffered(1)
    square = pl.BlockSpec((length, width), lambda p: (0, 0), pipeline_mode=once)
    return pl.pallas_call(
        functools.partial(back_kernel, scale=scale),
        grid=(pairs,),
        in_specs=[
            square,
            pl.BlockSpec((length, 384), lambda p: (0, p)),
            pl.BlockSpec((length, 128), lambda p: (0, p)),
            pl.BlockSpec((1, 8, length), lambda p: (p, 0, 0)),
            pl.BlockSpec((width, 384), lambda p: (0, p)),
        ],
        out_specs=[
            pl.BlockSpec((length, 384), lambda p: (0, p)),
            square,
            pl.BlockSpec((1, 8, 384), lambda p: (p, 0, 0)),
            whole((8, width)),
        ],
        out_shape=[
            jax.ShapeDtypeStruct((length, columns), LOW),
            jax.ShapeDtypeStruct((length, width), LOW),
            jax.ShapeDtypeStruct((pairs, 8, 384), jnp.float32),
            jax.ShapeDtypeStruct((8, width), jnp.float32),
        ],
        scratch_shapes=[
            pltpu.VMEM((length, 128), jnp.float32),
            pltpu.VMEM((length, 128), jnp.float32),
            pltpu.VMEM((length, width), jnp.float32),
        ],
        compiler_params=settings(56),
        cost_estimate=cost(2 * length * width * columns * 48, 12 * length * width),
        name="back",
    )(xhat, qkv, grad, logs, weight)


def last_kernel(place_ref, x_ref, dbranch_ref, own_ref, other_ref, vec_ref, out_ref):
    dnorm = own_ref[...].astype(jnp.float32) + other_ref[...].astype(jnp.float32)
    xhat, inverse = row_stats(x_ref[...].astype(jnp.float32))
    back = norm_back(dnorm, xhat, inverse, vec_ref[0:1, :])
    out_ref[...] = dbranch_ref[...].astype(jnp.float32) + back


def last_product(place, x, dbranch, own, other, vectors):
    rows, width = other.shape
    block = 128
    steps = rows // block
    mine = pl.BlockSpec((block, width), lambda p, place: (place[0] * steps + p, 0))
    plain = pl.BlockSpec((block, width), lambda p, _: (p, 0))
    return pl.pallas_call(
        last_kernel,
        grid_spec=pltpu.PrefetchScalarGridSpec(
            num_scalar_prefetch=1,
            grid=(steps,),
            in_specs=[plain, mine, mine, plain, whole(vectors.shape)],
            out_specs=plain,
        ),
        out_shape=jax.ShapeDtypeStruct((rows, width), jnp.float32),
        compiler_params=settings(16),
        cost_estimate=cost(40 * rows * width, 320 * rows * width),
        name="last",
    )(place, x, dbranch, own, other, vectors)


def result_kernel(place_ref, resid_ref, own_ref, other_ref, vec_ref, out_ref):
    mixed = own_ref[...].astype(jnp.float32) + other_ref[...].astype(jnp.float32)
    total = resid_ref[...].astype(jnp.float32) + mixed + vec_ref[5:6, :]
    out_ref[...] = total.astype(LOW)


def result_product(place, resid, own, other, vectors):
    rows, width = other.shape
    block = 128
    steps = rows // block
    mine = pl.BlockSpec((block, width), lambda p, place: (place[0] * steps + p, 0))
    plain = pl.BlockSpec((block, width), lambda p, _: (p, 0))
    return pl.pallas_call(
        result_kernel,
        grid_spec=pltpu.PrefetchScalarGridSpec(
            num_scalar_prefetch=1,
            grid=(steps,),
            in_specs=[mine, mine, plain, whole(vectors.shape)],
            out_specs=plain,
        ),
        out_shape=jax.ShapeDtypeStruct((rows, width), LOW),
        compiler_params=settings(16),
        cost_estimate=cost(10 * rows * width, 320 * rows * width),
        name="result",
    )(place, resid, own, other, vectors)


def pack_kernel(proj_ref, out_ref, up_ref, down_ref, vec_ref, narrow_ref, wide_ref):
    columns = proj_ref.shape[2]
    for pair in range(columns // 128):
        for kind in range(3):
            start = (pair * 3 + kind) * 128
            narrow_ref[:, start : start + 128] = proj_ref[kind, :, pair * 128 : pair * 128 + 128]
    narrow_ref[:, 3 * columns : 4 * columns] = out_ref[...]
    turned = jnp.transpose(vec_ref[...].astype(jnp.float32))
    turned = jnp.concatenate([turned, jnp.zeros((SLOT, 112), jnp.float32)], axis=1)
    narrow_ref[:, 4 * columns :] = turned.astype(LOW)
    hidden = up_ref.shape[1]
    wide_ref[:, :hidden] = up_ref[...]
    wide_ref[:, hidden:] = down_ref[...]


def pack_shards(proj, out, up, down, vec):
    rows, columns = out.shape
    return pl.pallas_call(
        pack_kernel,
        out_shape=[
            jax.ShapeDtypeStruct((rows, 4 * columns + 128), LOW),
            jax.ShapeDtypeStruct((rows, 2 * up.shape[1]), LOW),
        ],
        compiler_params=settings(56),
        cost_estimate=cost(0, 4 * rows * (4 * columns + 2 * up.shape[1])),
        name="pack",
    )(proj, out, up, down, vec)


def vector_kernel(place_ref, *refs):
    pieces = refs[:-4]
    vec_ref, bias_ref, hidden_ref, joined_ref = refs[-4:]
    fill_natural(place_ref, joined_ref, pieces)
    turned = jnp.transpose(joined_ref[...]).astype(jnp.float32)
    vec_ref[...] = turned[0:8]
    bias_ref[...] = turned[8:16]
    lane = lax.broadcasted_iota(jnp.int32, (1, 128), 1)
    for pair in range(bias_ref.shape[1] // 128):
        rows = [turned[10 + q : 11 + q, pair * 128 : pair * 128 + 128] for q in range(4)]
        flipped = [pltpu.roll(row, 64, 1) for row in rows]
        for q in (0, 2):
            start = pair * 512 + q * 64
            hidden_ref[:, start : start + 128] = jnp.where(lane < 64, rows[q], flipped[q + 1])
            hidden_ref[:, start + 256 : start + 384] = jnp.where(
                lane < 64, flipped[q], rows[q + 1]
            )


def spread_vectors(place, pieces, index):
    width = sum(piece.shape[0] for piece in pieces)
    return pl.pallas_call(
        vector_kernel,
        grid_spec=pltpu.PrefetchScalarGridSpec(
            num_scalar_prefetch=1,
            grid=(1,),
            in_specs=fixed_specs(pieces, 128, index),
            out_specs=[whole((8, width)), whole((8, width)), whole((1, 4 * width))],
            scratch_shapes=[pltpu.VMEM((width, 128), LOW)],
        ),
        out_shape=[
            jax.ShapeDtypeStruct((8, width), jnp.float32),
            jax.ShapeDtypeStruct((8, width), jnp.float32),
            jax.ShapeDtypeStruct((1, 4 * width), jnp.float32),
        ],
        compiler_params=settings(56),
        cost_estimate=cost(width * 128, 2 * width * 128),
        name="vectors",
    )(place, *pieces)


def after(value, *events):
    return lax.optimization_barrier((value,) + events)[0]


def dp_shift(value, ranks, dz, dy, dc):
    far, near = 4, ranks // 8

    def goes(rank):
        z, y, c = rank // (near * 2), rank // 2 % near, rank % 2
        return ((z + dz) % far * near + (y + dy) % near) * 2 + (c + dc) % 2

    return lax.ppermute(value, "dp", [(rank, goes(rank)) for rank in range(ranks)])


def dp_gather(shard, ranks, event):
    far = [shard] + [dp_shift(shard, ranks, k, 0, 0) for k in (1, 2, 3)]
    sent = far[:2] + [after(far[2], event)] + far[3:]
    near = [dp_shift(piece, ranks, 0, 1, 0) for piece in sent]
    pieces = far + near
    return pieces + [dp_shift(piece, ranks, 0, 0, 1) for piece in pieces], pieces


def reduce_core(left, right, ranks):
    half = left.shape[0] // 2
    return dp_shift(matmul(left[half:], right).astype(LOW), ranks, 0, 0, 1)


def reduce_near(left, right, other):
    half = left.shape[0] // 2
    part = half // 2
    sent = matmul(left[part:half], right) + other[part:].astype(jnp.float32)
    return sent.astype(LOW)


def reduce_sum(left, right, other, arrived):
    part = left.shape[0] // 4
    total = matmul(left[:part], right) + other[:part].astype(jnp.float32)
    return total + arrived.astype(jnp.float32)


def far_send(total, ranks, wire=LOW):
    rows = total.shape[0] // 4
    low = total.astype(wire)
    return [dp_shift(low[k * rows : (k + 1) * rows], ranks, -k, 0, 0) for k in (2, 3, 1)]


def far_sum(total, sent):
    result = total[: total.shape[0] // 4]
    for value in sent:
        result = result + value.astype(jnp.float32)
    return result


def swap(value):
    return lax.ppermute(value, "tensor", [(0, 1), (1, 0)])


def paired(
    inputs,
    out_grad,
    parents,
    ln1_gain,
    ln1_bias,
    w_qkv,
    qv_bias,
    w_attn_out,
    attn_out_bias,
    ln2_gain,
    ln2_bias,
    w_up,
    up_bias,
    w_down,
    down_bias,
):
    ranks = lax.axis_size("dp")
    near = ranks // 8
    rank = lax.axis_index("dp")
    side = lax.axis_index("tensor")
    rows, width = inputs.shape
    shard = width // ranks
    heads_width = w_qkv.shape[2]
    pairs = heads_width // 128
    hidden = w_up.shape[1]
    scale = 1.0 / math.sqrt(width // HEADS)

    slots = jnp.arange(ranks, dtype=jnp.int32)
    core_step, near_step, far_step = slots // (ranks // 2), slots // 4 % near, slots % 4
    my_z, my_y, my_c = rank // (2 * near), rank // 2 % near, rank % 2
    source = ((my_z - far_step) % 4 * near + (my_y - near_step) % near) * 2 + (
        my_c + core_step
    ) % 2
    place = jnp.concatenate([jnp.stack([side, my_z, my_y, my_c]), source]).astype(jnp.int32)
    feature = jnp.repeat(source * shard, shard) + jnp.tile(
        jnp.arange(shard, dtype=jnp.int32), ranks
    )
    to_local = (jnp.arange(width, dtype=jnp.int32)[:, None] == feature[None, :]).astype(LOW)
    slot_of = (slots[:, None] == source[None, :]).astype(jnp.float32)

    zero = jnp.zeros_like(ln1_gain)
    vec = [ln1_gain, ln1_bias, attn_out_bias, ln2_gain, ln2_bias, down_bias, zero, zero]
    vec = jnp.concatenate(
        [jnp.stack(vec), qv_bias, up_bias.reshape(4, shard), jnp.zeros((2, shard), LOW)], axis=0
    )
    narrow_shard, wide_shard = pack_shards(w_qkv, w_attn_out.T, w_up, w_down.T, vec)
    narrow, narrow_far = dp_gather(narrow_shard, ranks, place)
    inputs_other = swap(after(inputs, narrow_shard))
    grad_other = swap(after(out_grad, inputs_other))
    wide = lax.all_gather(
        after(wide_shard, inputs_other, *narrow_far[1:6]), "dp", axis=0, tiled=True
    )
    vectors, query_bias, hidden_bias = spread_vectors(place, narrow, 16)

    def in_order(own, other):
        return jnp.where(
            side == 0,
            jnp.concatenate([own, other], axis=0),
            jnp.concatenate([other, own], axis=0),
        )

    def to_slots(value):
        return lax.dot_general(
            to_local, value, (((0,), (1,)), ((), ())), preferred_element_type=jnp.float32
        ).astype(LOW)

    def other_rows(value):
        return lax.dynamic_slice_in_dim(value, (1 - side) * rows, rows, 0)

    hidden_in, xhat, norm_one, qkv, attended, logs, share, proj_full, out_full = front(
        place,
        inputs,
        inputs_other,
        vectors,
        query_bias,
        narrow,
        pairs,
        scale,
    )
    cotangent = after(in_order(out_grad, grad_other), share)
    lefts = jnp.stack([cotangent, jnp.zeros_like(cotangent)])
    norm_slot = to_slots(after(norm_one, share))
    resid, lefts, rights, dnorm_share, dpre_sum = feed_product(
        place, hidden_in, share, swap(after(share, grad_other)), vectors, hidden_bias, lefts, wide
    )
    dnorm_other = swap(dnorm_share)
    wide_share = lax.dot_general(
        lefts,
        after(rights, dnorm_share),
        (((1,), (1,)), ((0,), (0,))),
        preferred_element_type=jnp.float32,
    ).astype(LOW)
    wide_grad = lax.psum_scatter(wide_share, "dp", scatter_dimension=1, tiled=True)
    mixed_share = contract_last(after(rights, wide_share)[0], wide[:, hidden:]).astype(LOW)
    dbranch, dattended, mid_sum = mid_product(
        after(resid, mixed_share, norm_slot), dnorm_share, dnorm_other, lefts, vectors, out_full
    )
    dqkv, dnorm_one, dqkv_sum, front_sum = back_product(
        xhat, qkv, dattended, logs, proj_full, scale
    )
    dqkv_sum = dqkv_sum[:, 0].reshape(pairs, 3, 128)
    placed = [
        place_block(value, 2 * value.shape[0], side * value.shape[0]).reshape(ranks, -1)
        for value in (
            dqkv_sum[:, 0].reshape(heads_width),
            dqkv_sum[:, 2].reshape(heads_width),
            dpre_sum[0],
        )
    ]
    pack = jnp.stack([front_sum[0], front_sum[1], mid_sum[2], mid_sum[0], mid_sum[1], mid_sum[3]])
    pack = pack.reshape(6, ranks, shard).transpose(1, 0, 2).reshape(ranks, -1)
    pack = lax.dot_general(
        slot_of,
        jnp.concatenate([pack] + placed, axis=1),
        (((0,), (0,)), ((), ())),
        precision=lax.Precision.HIGHEST,
        preferred_element_type=jnp.float32,
    )
    proj_core = reduce_core(norm_slot, after(dqkv, pack), ranks)
    pack = pack + swap(pack)
    pack = pack[: ranks // 2] + dp_shift(pack[ranks // 2 :], ranks, 0, 0, 1)
    back_other = swap(other_rows(after(dnorm_one, pack)))
    dbranch_slot = to_slots(after(dbranch, dattended))
    out_core = reduce_core(dbranch_slot, attended, ranks)
    slim_near, pack = lax.optimization_barrier(
        (
            jnp.concatenate(
                [
                    reduce_near(norm_slot, dqkv, proj_core),
                    reduce_near(dbranch_slot, attended, out_core),
                ],
                axis=1,
            ),
            pack,
        )
    )
    pack_arrived = dp_shift(pack[ranks // 4 :], ranks, 0, 1, 0)
    slim_arrived = dp_shift(slim_near, ranks, 0, 1, 0)
    own_other = swap(other_rows(after(mixed_share, back_other)))
    slim_arrived, pack_arrived, back_other = lax.optimization_barrier(
        (slim_arrived, pack_arrived, back_other)
    )
    columns = 3 * heads_width
    slim_total, pack_total = lax.optimization_barrier(
        (
            jnp.concatenate(
                [
                    reduce_sum(norm_slot, dqkv, proj_core, slim_arrived[:, :columns]),
                    reduce_sum(dbranch_slot, attended, out_core, slim_arrived[:, columns:]),
                ],
                axis=1,
            ),
            pack[: ranks // 4] + pack_arrived,
        )
    )
    pack = far_sum(pack_total, far_send(pack_total, ranks, jnp.float32)).reshape(-1)
    grad_back = wide_grad[0].T.astype(jnp.float32)
    grad_hidden = wide_grad[1].astype(jnp.float32)
    slim_grad = far_sum(
        after(slim_total, grad_back, grad_hidden), far_send(slim_total, ranks)
    )
    grad_proj = slim_grad[:, :columns]
    grad_out = slim_grad[:, columns:].T
    result = result_product(
        place, after(resid, slim_total), mixed_share, own_other, vectors
    )
    input_grad = last_product(
        place, inputs, dbranch, dnorm_one, after(back_other, slim_total), vectors
    )
    grad_proj = grad_proj.reshape(shard, pairs, 3, 128).transpose(2, 0, 1, 3)
    grad_proj = grad_proj.reshape(3, shard, heads_width)
    vector_grads = [pack[i * shard : (i + 1) * shard] for i in range(6)]
    return (
        result,
        input_grad,
        vector_grads[0],
        vector_grads[1],
        grad_proj,
        pack[6 * shard : 8 * shard].reshape(2, shard),
        grad_out,
        vector_grads[2],
        vector_grads[3],
        vector_grads[4],
        grad_hidden,
        pack[8 * shard :],
        grad_back,
        vector_grads[5],
    )


def local(*arrays):
    fits = lax.axis_size("tensor") == 2 and lax.axis_size("dp") == 16
    if fits and arrays[2].shape[1] == 3:
        return paired(*arrays)
    return generic(*arrays)


def solution(mesh):
    return jax.shard_map(
        local,
        mesh=mesh,
        in_specs=(
            P(("dp", "tensor"), None),
            P(("dp", "tensor"), None),
            P("dp", None),
            P("dp"),
            P("dp"),
            P(None, "dp", "tensor"),
            P(None, "dp"),
            P("tensor", "dp"),
            P("dp"),
            P("dp"),
            P("dp"),
            P("dp", "tensor"),
            P("dp"),
            P("tensor", "dp"),
            P("dp"),
        ),
        out_specs=(
            P(("dp", "tensor"), None),
            P(("dp", "tensor"), None),
            P("dp"),
            P("dp"),
            P(None, "dp", "tensor"),
            P(None, "dp"),
            P("tensor", "dp"),
            P("dp"),
            P("dp"),
            P("dp"),
            P("dp", "tensor"),
            P("dp"),
            P("tensor", "dp"),
            P("dp"),
        ),
        check_vma=False,
    )
```

```python
import functools
import math

import jax
import jax.numpy as jnp
from jax import lax
from jax.experimental import pallas as pl
from jax.experimental.pallas import tpu as pltpu
from jax.sharding import PartitionSpec as P

HEADS = 16
SEG = 256


epsilon = 1e-05
gelu_coef = 0.7978845608028654


def layer_norm(values, scales, shifts):
    centre = jnp.mean(values, axis=-1, keepdims=True)
    shifted = values - centre
    spread = jnp.mean(shifted * shifted, axis=-1, keepdims=True)
    return shifted * lax.rsqrt(spread + epsilon) * scales + shifts


def gelu_tanh(values):
    return (
        0.5 * values * (1.0 + jnp.tanh(gelu_coef * (values + 0.044715 * values * values * values)))
    )


def matmul(left, right):
    return jnp.dot(left, right, preferred_element_type=jnp.float32)


def contract_rows(left, right):
    return lax.dot_general(
        left, right, (((0,), (0,)), ((), ())), preferred_element_type=jnp.float32
    )


def contract_last(left, right):
    return lax.dot_general(
        left, right, (((1,), (1,)), ((), ())), preferred_element_type=jnp.float32
    )


def ancestors(parent_row, segment_count):
    labels = jnp.arange(segment_count, dtype=jnp.int32)
    links = ((parent_row[:, None] == labels[None, :]) & (labels[:, None] > 0)).astype(jnp.float32)
    identity = jnp.eye(segment_count, dtype=jnp.float32)

    def extend(turn, reached):
        grown = jnp.dot(
            links, reached, precision=lax.Precision.HIGHEST, preferred_element_type=jnp.float32
        )
        return jnp.minimum(identity + grown, 1.0)

    return lax.fori_loop(0, segment_count, extend, identity)


def tree_mask(reached, first_row, block_rows, length):
    query_pos = first_row + jnp.arange(block_rows, dtype=jnp.int32)
    key_pos = jnp.arange(length, dtype=jnp.int32)
    segment_count = reached.shape[0]
    onehot = (
        (query_pos // SEG)[:, None] == jnp.arange(segment_count, dtype=jnp.int32)[None, :]
    ).astype(jnp.float32)
    row_reach = jnp.dot(
        onehot, reached, precision=lax.Precision.HIGHEST, preferred_element_type=jnp.float32
    )
    spread_out = jnp.repeat(row_reach, SEG, axis=1)
    return (spread_out > 0.5) & (key_pos[None, :] <= query_pos[:, None])


def row_block(length):
    pieces = -(-length // 512)
    while length % pieces:
        pieces += 1
    return length // pieces


def place_block(local_vec, full_length, offset):
    empty_vec = jnp.zeros(local_vec.shape[:-1] + (full_length,), jnp.float32)
    return lax.dynamic_update_slice_in_dim(empty_vec, local_vec, offset, local_vec.ndim - 1)


def generic(
    inputs,
    out_grad,
    parents,
    ln1_gain,
    ln1_bias,
    w_qkv,
    qv_bias,
    w_attn_out,
    attn_out_bias,
    ln2_gain,
    ln2_bias,
    w_up,
    up_bias,
    w_down,
    down_bias,
):
    tensor_ranks = lax.axis_size("tensor")
    tensor_rank = lax.axis_index("tensor")
    rows_own = inputs.shape[0]
    length = rows_own * tensor_ranks
    model_width = inputs.shape[1]
    head_dim = model_width // HEADS
    local_width = w_qkv.shape[2]
    local_hidden = w_up.shape[1]
    heads_here = local_width // head_dim
    scale = 1.0 / math.sqrt(head_dim)
    gathered = (
        lax.all_gather(w_qkv, "dp", axis=1, tiled=True),
        lax.all_gather(w_attn_out, "dp", axis=1, tiled=True),
        lax.all_gather(w_up, "dp", axis=0, tiled=True),
        lax.all_gather(w_down, "dp", axis=1, tiled=True),
        lax.all_gather(ln1_gain, "dp", axis=0, tiled=True),
        lax.all_gather(ln1_bias, "dp", axis=0, tiled=True),
        lax.all_gather(qv_bias, "dp", axis=1, tiled=True),
        lax.all_gather(attn_out_bias, "dp", axis=0, tiled=True),
        lax.all_gather(ln2_gain, "dp", axis=0, tiled=True),
        lax.all_gather(ln2_bias, "dp", axis=0, tiled=True),
        lax.all_gather(up_bias, "dp", axis=0, tiled=True),
        lax.all_gather(down_bias, "dp", axis=0, tiled=True),
    )
    proj_full, out_full, hidden_full, back_full = (
        gathered[0],
        gathered[1],
        gathered[2],
        gathered[3],
    )
    gain_one = gathered[4].astype(jnp.float32)
    shift_one = gathered[5].astype(jnp.float32)
    proj_bias = lax.dynamic_slice_in_dim(
        gathered[6].astype(jnp.float32), tensor_rank * local_width, local_width, 1
    )
    out_bias = gathered[7].astype(jnp.float32)
    gain_two = gathered[8].astype(jnp.float32)
    shift_two = gathered[9].astype(jnp.float32)
    hidden_bias_full = gathered[10].astype(jnp.float32)
    back_bias = gathered[11].astype(jnp.float32)
    full_hidden = hidden_bias_full.shape[0]
    hidden_in = inputs.astype(jnp.float32)
    norm_one, ln1_pull = jax.vjp(layer_norm, hidden_in, gain_one, shift_one)
    norm_one_all = lax.all_gather(norm_one.astype(jnp.bfloat16), "tensor", axis=0, tiled=True)
    queries = (matmul(norm_one_all, proj_full[0]) + proj_bias[0]).astype(jnp.bfloat16)
    keys_low = matmul(norm_one_all, proj_full[1]).astype(jnp.bfloat16)
    values_low = (matmul(norm_one_all, proj_full[2]) + proj_bias[1]).astype(jnp.bfloat16)
    reached = ancestors(parents[0], length // SEG)
    block_rows = row_block(length)
    num_blocks = length // block_rows
    starts = jnp.arange(num_blocks, dtype=jnp.int32) * block_rows
    query_blocks = queries.reshape(num_blocks, block_rows, heads_here, head_dim)
    key_heads = keys_low.reshape(length, heads_here, head_dim)
    value_heads = values_low.reshape(length, heads_here, head_dim)

    def block_scores(query_block, first_row):
        scores = (
            jnp.einsum("qhd,khd->hqk", query_block, key_heads, preferred_element_type=jnp.float32)
            * scale
        )
        allowed = tree_mask(reached, first_row, block_rows, length)
        return jnp.where(allowed[None], scores, -1e30)

    def forward_block(element):
        query_block, first_row = element
        scores = block_scores(query_block, first_row)
        top_score = jnp.max(scores, axis=-1, keepdims=True)
        expo = jnp.exp(scores - top_score)
        totals = jnp.sum(expo, axis=-1, keepdims=True)
        probs = (expo / totals).astype(jnp.bfloat16)
        attended_block = jnp.einsum(
            "hqk,khd->qhd", probs, value_heads, preferred_element_type=jnp.float32
        )
        return (attended_block, (top_score + jnp.log(totals))[..., 0])

    attended_blocks, log_totals = lax.map(forward_block, (query_blocks, starts))
    attended = attended_blocks.reshape(length, local_width).astype(jnp.bfloat16)
    branch = (
        lax.psum_scatter(matmul(attended, out_full), "tensor", scatter_dimension=0, tiled=True)
        + out_bias
    )
    resid = hidden_in + branch
    norm_two, ln2_pull = jax.vjp(layer_norm, resid, gain_two, shift_two)
    norm_two_low = norm_two.astype(jnp.bfloat16)
    grad_back_bias = jnp.sum(out_grad.astype(jnp.float32), axis=0)
    norm_two_all = lax.all_gather(norm_two_low, "tensor", axis=0, tiled=True)
    hidden_slice = lax.dynamic_slice_in_dim(
        hidden_bias_full, tensor_rank * local_hidden, local_hidden, 0
    )
    pre = matmul(norm_two_all, hidden_full) + hidden_slice
    act, gelu_pull = jax.vjp(gelu_tanh, pre)
    act_low = act.astype(jnp.bfloat16)
    mixed = (
        lax.psum_scatter(
            matmul(act_low, back_full).astype(jnp.bfloat16),
            "tensor",
            scatter_dimension=0,
            tiled=True,
        ).astype(jnp.float32)
        + back_bias
    )
    cotangent_all = lax.all_gather(out_grad, "tensor", axis=0, tiled=True)
    grad_back = contract_rows(act_low, cotangent_all)
    (dpre,) = gelu_pull(contract_last(cotangent_all, back_full))
    dpre_low = dpre.astype(jnp.bfloat16)
    grad_hidden = contract_rows(norm_two_all, dpre_low)
    grad_hidden_bias = place_block(
        jnp.sum(dpre_low.astype(jnp.float32), axis=0), full_hidden, tensor_rank * local_hidden
    )
    dnorm_two = lax.psum_scatter(
        contract_last(dpre_low, hidden_full), "tensor", scatter_dimension=0, tiled=True
    )
    result = (resid + mixed).astype(jnp.bfloat16)
    dresid_part, grad_gain_two, grad_shift_two = ln2_pull(dnorm_two)
    dresid = out_grad.astype(jnp.float32) + dresid_part
    dbranch = dresid.astype(jnp.bfloat16)
    grad_out_bias = jnp.sum(dbranch.astype(jnp.float32), axis=0)
    dbranch_all = lax.all_gather(dbranch, "tensor", axis=0, tiled=True)
    grad_out = contract_rows(attended, dbranch_all)
    dattended = contract_last(dbranch_all, out_full).astype(jnp.bfloat16)
    dattended_blocks = dattended.reshape(num_blocks, block_rows, heads_here, head_dim)

    def backward_block(carry, element):
        dkey_acc, dvalue_acc = carry
        query_block, dattended_block, log_block, first_row = element
        scores = block_scores(query_block, first_row)
        probs = jnp.exp(scores - log_block[..., None])
        dvalue_acc = dvalue_acc + jnp.einsum(
            "hqk,qhd->khd",
            probs.astype(jnp.bfloat16),
            dattended_block,
            preferred_element_type=jnp.float32,
        )
        dprobs = jnp.einsum(
            "qhd,khd->hqk", dattended_block, value_heads, preferred_element_type=jnp.float32
        )
        dscores = probs * (dprobs - jnp.sum(dprobs * probs, axis=-1, keepdims=True))
        dscores_low = dscores.astype(jnp.bfloat16)
        dquery_block = (
            jnp.einsum("hqk,khd->qhd", dscores_low, key_heads, preferred_element_type=jnp.float32)
            * scale
        )
        dkey_acc = (
            dkey_acc
            + jnp.einsum(
                "hqk,qhd->khd", dscores_low, query_block, preferred_element_type=jnp.float32
            )
            * scale
        )
        return ((dkey_acc, dvalue_acc), dquery_block)

    zero_heads = jnp.zeros((length, heads_here, head_dim), jnp.float32)
    (dkey_acc, dvalue_acc), dquery_blocks = lax.scan(
        backward_block,
        (zero_heads, zero_heads),
        (query_blocks, dattended_blocks, log_totals, starts),
    )
    dqueries = dquery_blocks.reshape(length, local_width).astype(jnp.bfloat16)
    dkeys = dkey_acc.reshape(length, local_width).astype(jnp.bfloat16)
    dvalues = dvalue_acc.reshape(length, local_width).astype(jnp.bfloat16)
    grad_proj = jnp.stack(
        [
            contract_rows(norm_one_all, dqueries),
            contract_rows(norm_one_all, dkeys),
            contract_rows(norm_one_all, dvalues),
        ]
    )
    local_bias_grad = jnp.stack(
        [
            jnp.sum(dqueries.astype(jnp.float32), axis=0),
            jnp.sum(dvalues.astype(jnp.float32), axis=0),
        ]
    )
    grad_proj_bias = place_block(local_bias_grad, model_width, tensor_rank * local_width)
    dnorm_one = lax.psum_scatter(
        (
            contract_last(dqueries, proj_full[0])
            + contract_last(dkeys, proj_full[1])
            + contract_last(dvalues, proj_full[2])
        ).astype(jnp.bfloat16),
        "tensor",
        scatter_dimension=0,
        tiled=True,
    ).astype(jnp.float32)
    dinput_part, grad_gain_one, grad_shift_one = ln1_pull(dnorm_one)
    input_grad = dresid + dinput_part
    summed = (
        lax.psum_scatter(grad_proj, "dp", scatter_dimension=1, tiled=True),
        lax.psum_scatter(grad_out, "dp", scatter_dimension=1, tiled=True),
        lax.psum_scatter(grad_hidden, "dp", scatter_dimension=0, tiled=True),
        lax.psum_scatter(grad_back, "dp", scatter_dimension=1, tiled=True),
        lax.psum_scatter(grad_gain_one, "dp", scatter_dimension=0, tiled=True),
        lax.psum_scatter(grad_shift_one, "dp", scatter_dimension=0, tiled=True),
        lax.psum_scatter(grad_proj_bias, "dp", scatter_dimension=1, tiled=True),
        lax.psum_scatter(grad_out_bias, "dp", scatter_dimension=0, tiled=True),
        lax.psum_scatter(grad_gain_two, "dp", scatter_dimension=0, tiled=True),
        lax.psum_scatter(grad_shift_two, "dp", scatter_dimension=0, tiled=True),
        lax.psum_scatter(grad_hidden_bias, "dp", scatter_dimension=0, tiled=True),
        lax.psum_scatter(grad_back_bias, "dp", scatter_dimension=0, tiled=True),
    )
    vectors = lax.psum(
        (summed[4], summed[5], summed[6], summed[7], summed[8], summed[9], summed[10], summed[11]),
        "tensor",
    )
    return (
        result,
        input_grad,
        vectors[0],
        vectors[1],
        summed[0],
        vectors[2],
        summed[1],
        vectors[3],
        vectors[4],
        vectors[5],
        summed[2],
        vectors[6],
        summed[3],
        vectors[7],
    )


LOW = jnp.bfloat16
SLOT = 64


def settings(mib):
    return pltpu.CompilerParams(vmem_limit_bytes=mib * 2**20)


def cost(flops, moved, exps=0):
    return pl.CostEstimate(
        flops=int(flops), bytes_accessed=int(moved), transcendentals=int(exps)
    )


def whole(shape):
    return pl.BlockSpec(shape, lambda *_: (0,) * len(shape))


def piece_specs(pieces, block, first=0):
    return [
        pl.BlockSpec((piece.shape[0], block), lambda p, *_: (0, first + p)) for piece in pieces
    ]


def fixed_specs(pieces, block, index):
    return [pl.BlockSpec((piece.shape[0], block), lambda *_: (0, index)) for piece in pieces]


def fill_natural(place_ref, scratch, refs):
    for slot, ref in enumerate(refs):
        start = pl.multiple_of(place_ref[4 + slot] * SLOT, SLOT)
        scratch[pl.ds(start, SLOT), :] = ref[...]


def row_stats(rows):
    centre = jnp.mean(rows, axis=-1, keepdims=True)
    shifted = rows - centre
    spread = jnp.mean(shifted * shifted, axis=-1, keepdims=True)
    inverse = lax.rsqrt(spread + epsilon)
    return shifted * inverse, inverse


def norm_back(dnorm, xhat, inverse, gain):
    scaled = dnorm * gain
    return inverse * (
        scaled
        - jnp.mean(scaled, axis=-1, keepdims=True)
        - xhat * jnp.mean(scaled * xhat, axis=-1, keepdims=True)
    )


def attend_pair(qkv_ref, out_ref, log_ref, scale):
    length = qkv_ref.shape[0]
    lane = lax.broadcasted_iota(jnp.int32, (SEG, 128), 1)
    reach = lax.broadcasted_iota(jnp.int32, (SEG, SEG), 0) <= lax.broadcasted_iota(
        jnp.int32, (SEG, SEG), 1
    )
    value_t = jnp.transpose(qkv_ref[:, 256:384])
    for seg in range(length // SEG):
        before = seg * SEG
        rows = slice(before, before + SEG)
        query = qkv_ref[rows, 0:128] * scale
        parts = []
        drawn = []
        for head in range(2):
            mine = jnp.where(lane // 64 == head, query, jnp.zeros_like(query))
            scores = contract_last(qkv_ref[rows, 128:256], mine)
            early = contract_last(qkv_ref[0:before, 128:256], mine) if seg > 0 else None
            drawn.append((jnp.where(reach, scores, -1e30), early))
        for head in range(2):
            lanes = slice(head * 64, head * 64 + 64)
            scores, early = drawn[head]
            top = jnp.max(scores, axis=0, keepdims=True)
            if seg > 0:
                top = jnp.maximum(top, jnp.max(early, axis=0, keepdims=True))
            expo = jnp.exp(scores - top)
            total = jnp.sum(expo, axis=0, keepdims=True)
            mixed = matmul(value_t[lanes, rows], expo.astype(LOW))
            if seg > 0:
                expo = jnp.exp(early - top)
                total = total + jnp.sum(expo, axis=0, keepdims=True)
                mixed = mixed + matmul(value_t[lanes, 0:before], expo.astype(LOW))
            parts.append(mixed / total)
            log_ref[0, head : head + 1, rows] = top + jnp.log(total)
        out_ref[rows, :] = jnp.transpose(jnp.concatenate(parts, axis=0)).astype(LOW)


def read_vectors(vec_ref, bias_ref, hidden_ref, joined_ref):
    turned = jnp.transpose(joined_ref[...]).astype(jnp.float32)
    vec_ref[...] = turned[0:8]
    bias_ref[...] = turned[8:16]
    lane = lax.broadcasted_iota(jnp.int32, (1, 128), 1)
    for pair in range(bias_ref.shape[1] // 128):
        rows = [turned[10 + q : 11 + q, pair * 128 : pair * 128 + 128] for q in range(4)]
        flipped = [pltpu.roll(row, 64, 1) for row in rows]
        for q in (0, 2):
            start = pair * 512 + q * 64
            hidden_ref[:, start : start + 128] = jnp.where(lane < 64, rows[q], flipped[q + 1])
            hidden_ref[:, start + 256 : start + 384] = jnp.where(
                lane < 64, flipped[q], rows[q + 1]
            )


def front_kernel(place_ref, own_ref, other_ref, *refs, scale, count):
    pieces, outs, vecs = (refs[i * count : (i + 1) * count] for i in range(3))
    kept, refs = refs[3 * count : 3 * count + 4], refs[3 * count + 4 :]
    qkv_ref, att_ref, log_ref, share_ref, weight_ref, vec_ref, hidden_ref = refs[:7]
    x_ref, xhat_ref, norm_ref, out_ref, joined_ref, bias_ref, lines_ref, sem = refs[7:]
    pairs = pl.num_programs(0)
    copies = [
        pltpu.make_async_copy(source, target, sem.at[index])
        for index, (source, target) in enumerate(zip((x_ref, xhat_ref, norm_ref, out_ref), kept))
    ]
    rows_own = own_ref.shape[0]
    step = pl.program_id(0)

    @pl.when(step == 0)
    def _():
        fill_natural(place_ref, lines_ref, vecs)
        read_vectors(vec_ref, bias_ref, hidden_ref, lines_ref)
        for half, ref in ((place_ref[0], own_ref), (1 - place_ref[0], other_ref)):
            for start in range(0, rows_own, 128):
                rows = pl.ds(pl.multiple_of(half * rows_own + start, 128), 128)
                x = ref[start : start + 128, :]
                xhat, _ = row_stats(x.astype(jnp.float32))
                x_ref[rows, :] = x
                xhat_ref[rows, :] = xhat.astype(LOW)
                norm_ref[rows, :] = (xhat * vec_ref[0:1, :] + vec_ref[1:2, :]).astype(LOW)
        fill_natural(place_ref, out_ref, outs)
        for copy in copies:
            copy.start()

    fill_natural(place_ref, weight_ref, pieces)
    mine = pl.ds(pl.multiple_of((place_ref[0] * pairs + step) * 128, 128), 128)
    bias = jnp.concatenate(
        [bias_ref[0:1, mine], jnp.zeros((1, 128), jnp.float32), bias_ref[1:2, mine]], axis=1
    )
    qkv_ref[...] = (matmul(norm_ref[...], weight_ref[...]) + bias).astype(LOW)
    attend_pair(qkv_ref, att_ref, log_ref, scale)
    joined_ref[:, pl.ds(pl.multiple_of(step * 128, 128), 128)] = att_ref[...]

    @pl.when(step == pl.num_programs(0) - 1)
    def _():
        share_ref[...] = contract_last(joined_ref[...], out_ref[...]).astype(LOW)
        for copy in copies:
            copy.wait()


def front(place, own, other, pieces, pairs, scale):
    length, width = 2 * own.shape[0], own.shape[1]
    once = pl.Buffered(1)
    square = pl.BlockSpec((length, width), lambda *_: (0, 0), pipeline_mode=once)
    half = pl.BlockSpec(own.shape, lambda *_: (0, 0), pipeline_mode=once)
    return pl.pallas_call(
        functools.partial(front_kernel, scale=scale, count=len(pieces)),
        grid_spec=pltpu.PrefetchScalarGridSpec(
            num_scalar_prefetch=1,
            grid=(pairs,),
            in_specs=[
                half,
                half,
            ]
            + piece_specs(pieces, 384)
            + fixed_specs(pieces, pairs * 128, 3)
            + fixed_specs(pieces, 128, pairs * 4),
            out_specs=[pl.BlockSpec(memory_space=pl.ANY)] * 4
            + [
                pl.BlockSpec((length, 384), lambda p, _: (0, p)),
                pl.BlockSpec((length, 128), lambda p, _: (0, p)),
                pl.BlockSpec((1, 8, length), lambda p, _: (p, 0, 0)),
                square,
                pl.BlockSpec((width, 384), lambda p, _: (0, p)),
                whole((8, width)),
                whole((1, 4 * width)),
            ],
            scratch_shapes=[
                pltpu.VMEM((length, width), LOW),
                pltpu.VMEM((length, width), LOW),
                pltpu.VMEM((length, width), LOW),
                pltpu.VMEM((width, pairs * 128), LOW),
                pltpu.VMEM((length, pairs * 128), LOW),
                pltpu.VMEM((8, width), jnp.float32),
                pltpu.VMEM((width, 128), LOW),
                pltpu.SemaphoreType.DMA((4,)),
            ],
        ),
        out_shape=[
            jax.ShapeDtypeStruct((length, width), LOW),
            jax.ShapeDtypeStruct((length, width), LOW),
            jax.ShapeDtypeStruct((length, width), LOW),
            jax.ShapeDtypeStruct((width, pairs * 128), LOW),
            jax.ShapeDtypeStruct((length, pairs * 384), LOW),
            jax.ShapeDtypeStruct((length, pairs * 128), LOW),
            jax.ShapeDtypeStruct((pairs, 8, length), jnp.float32),
            jax.ShapeDtypeStruct((length, width), LOW),
            jax.ShapeDtypeStruct((width, pairs * 384), LOW),
            jax.ShapeDtypeStruct((8, width), jnp.float32),
            jax.ShapeDtypeStruct((1, 4 * width), jnp.float32),
        ],
        compiler_params=settings(56),
        cost_estimate=cost(2 * length * width * pairs * 384 * 4, 12 * length * width),
        name="front",
    )(place, own, other, *pieces, *pieces, *pieces)


def feed_kernel(
    place_ref,
    x_ref,
    own_ref,
    other_ref,
    vec_ref,
    bias_ref,
    grad_ref,
    pair_ref,
    resid_ref,
    left_ref,
    right_ref,
    dnorm_ref,
    sum_ref,
    up_ref,
    down_ref,
    sem,
):
    first = pl.program_id(0) == 0
    hidden = up_ref.shape[1]

    def fetch(start):
        part = pl.ds(start, 512)
        index = start // 512
        return (
            pltpu.make_async_copy(pair_ref.at[:, part], up_ref.at[:, part], sem.at[0, index]),
            pltpu.make_async_copy(
                pair_ref.at[:, pl.ds(hidden + start, 512)], down_ref.at[:, part], sem.at[1, index]
            ),
        )

    @pl.when(first)
    def _():
        for start in range(0, hidden, 512):
            for copy in fetch(start):
                copy.start()
        sum_ref[...] = jnp.zeros_like(sum_ref)

    branch = own_ref[...].astype(jnp.float32) + other_ref[...].astype(jnp.float32)
    resid = x_ref[...].astype(jnp.float32) + (branch + vec_ref[2:3, :])
    resid_ref[...] = resid.astype(LOW)
    xhat, _ = row_stats(resid)
    norm = (xhat * vec_ref[3:4, :] + vec_ref[4:5, :]).astype(LOW)
    left_ref[0] = norm
    for start in range(0, hidden, 512):
        columns = slice(start, start + 512)

        @pl.when(first)
        def _(start=start):
            for copy in fetch(start):
                copy.wait()

        pre = matmul(norm, up_ref[:, columns]) + bias_ref[:, columns]
        square = pre * pre
        bent = jnp.tanh(pre * (square * (0.044715 * gelu_coef) + gelu_coef))
        half = 0.5 * bent + 0.5
        act = pre * half
        right_ref[0, :, columns] = act.astype(LOW)
        slope = half + act * (1.0 - bent) * (square * (3 * 0.044715 * gelu_coef) + gelu_coef)
        dpre = (matmul(grad_ref[0], down_ref[:, columns]) * slope).astype(LOW)
        right_ref[1, :, columns] = dpre
        total = jnp.sum(dpre.astype(jnp.float32), axis=0, keepdims=True)
        sum_ref[:, columns] += jnp.broadcast_to(total, (8, 512))
    dnorm_ref[...] = contract_last(right_ref[1], up_ref[...]).astype(LOW)


def feed_product(place, x, own, other, vectors, bias, lefts, pair, block=SEG):
    length, width = x.shape
    hidden = pair.shape[1] // 2
    rows = pl.BlockSpec((block, width), lambda p, _: (p, 0))
    return pl.pallas_call(
        feed_kernel,
        grid_spec=pltpu.PrefetchScalarGridSpec(
            num_scalar_prefetch=1,
            grid=(length // block,),
            in_specs=[rows] * 3
            + [
                whole(vectors.shape),
                pl.BlockSpec((1, hidden), lambda p, place: (0, place[0])),
                pl.BlockSpec((1, block, width), lambda p, _: (0, p, 0)),
                pl.BlockSpec(memory_space=pl.ANY),
            ],
            out_specs=[
                rows,
                pl.BlockSpec((1, block, width), lambda p, _: (1, p, 0)),
                pl.BlockSpec((2, block, hidden), lambda p, _: (0, p, 0)),
                rows,
                whole((8, hidden)),
            ],
            scratch_shapes=[
                pltpu.VMEM((width, hidden), LOW),
                pltpu.VMEM((width, hidden), LOW),
                pltpu.SemaphoreType.DMA((2, hidden // 512)),
            ],
        ),
        out_shape=[
            jax.ShapeDtypeStruct((length, width), LOW),
            jax.ShapeDtypeStruct((2, length, width), LOW),
            jax.ShapeDtypeStruct((2, length, hidden), LOW),
            jax.ShapeDtypeStruct((length, width), LOW),
            jax.ShapeDtypeStruct((8, hidden), jnp.float32),
        ],
        input_output_aliases={6: 1},
        compiler_params=settings(56),
        cost_estimate=cost(9 * length * width * hidden, 40 * length * width),
        name="feed",
    )(place, x, own, other, vectors, bias, lefts, pair)


def mid_kernel(
    resid_ref, own_ref, other_ref, grad_ref, vec_ref, weight_ref, dbranch_ref, datt_ref, sum_ref
):
    @pl.when(pl.program_id(0) == 0)
    def _():
        sum_ref[...] = jnp.zeros_like(sum_ref)

    dnorm = own_ref[...].astype(jnp.float32) + other_ref[...].astype(jnp.float32)
    grad = grad_ref[0].astype(jnp.float32)
    xhat, inverse = row_stats(resid_ref[...].astype(jnp.float32))
    dresid = grad + norm_back(dnorm, xhat, inverse, vec_ref[3:4, :])
    dbranch = dresid.astype(LOW)
    dbranch_ref[...] = dbranch
    datt_ref[...] = matmul(dbranch, weight_ref[...]).astype(LOW)
    for row, value in enumerate((dnorm * xhat, dnorm, dbranch.astype(jnp.float32), grad)):
        sum_ref[row : row + 1, :] += 0.5 * jnp.sum(value, axis=0, keepdims=True)


def mid_product(resid, own, other, lefts, vectors, weight, block=SEG):
    length, width = resid.shape
    inner = weight.shape[1]
    rows = pl.BlockSpec((block, width), lambda p: (p, 0))
    return pl.pallas_call(
        mid_kernel,
        grid=(length // block,),
        in_specs=[rows] * 3
        + [
            pl.BlockSpec((1, block, width), lambda p: (0, p, 0)),
            whole(vectors.shape),
            whole(weight.shape),
        ],
        out_specs=[rows, pl.BlockSpec((block, inner), lambda p: (p, 0)), whole((8, width))],
        out_shape=[
            jax.ShapeDtypeStruct((length, width), LOW),
            jax.ShapeDtypeStruct((length, inner), LOW),
            jax.ShapeDtypeStruct((8, width), jnp.float32),
        ],
        compiler_params=settings(56),
        cost_estimate=cost(2 * length * width * inner * 16, 16 * length * width),
        name="mid",
    )(resid, own, other, lefts, vectors, weight)


def attend_back_pair(qkv_ref, grad_ref, log_ref, out_ref, dkey_ref, dvalue_ref, scale):
    length = qkv_ref.shape[0]
    lane = lax.broadcasted_iota(jnp.int32, (SEG, 128), 1)
    reach = lax.broadcasted_iota(jnp.int32, (SEG, SEG), 0) <= lax.broadcasted_iota(
        jnp.int32, (SEG, SEG), 1
    )
    key_t = jnp.transpose(qkv_ref[:, 128:256])
    for seg in reversed(range(length // SEG)):
        before = seg * SEG
        rows = slice(before, before + SEG)
        spans = [rows] if seg == 0 else [rows, slice(0, before)]
        query = qkv_ref[rows, 0:128] * scale
        grad = grad_ref[rows, :]
        parts = []
        dkeys = [None] * len(spans)
        dvalues = [None] * len(spans)
        drawn = []
        for head in range(2):
            here = lane // 64 == head
            query_mine = jnp.where(here, query, jnp.zeros_like(query))
            grad_mine = jnp.where(here, grad, jnp.zeros_like(grad))
            scores = [contract_last(qkv_ref[span, 128:256], query_mine) for span in spans]
            scores[0] = jnp.where(reach, scores[0], -1e30)
            dprobs = [contract_last(qkv_ref[span, 256:384], grad_mine) for span in spans]
            drawn.append((query_mine, grad_mine, scores, dprobs))
        for head in range(2):
            lanes = slice(head * 64, head * 64 + 64)
            query_mine, grad_mine, scores, dprobs = drawn[head]
            log_row = log_ref[0, head : head + 1, rows]
            probs = []
            mean = None
            for index in range(len(spans)):
                prob = jnp.exp(scores[index] - log_row)
                share = jnp.sum(prob * dprobs[index], axis=0, keepdims=True)
                mean = share if mean is None else mean + share
                probs.append(prob)
            part = None
            for index, span in enumerate(spans):
                dscores = (probs[index] * (dprobs[index] - mean)).astype(LOW)
                dvalue = matmul(probs[index].astype(LOW), grad_mine)
                dkey = matmul(dscores, query_mine)
                piece = matmul(key_t[lanes, span], dscores)
                part = piece if part is None else part + piece
                dkeys[index] = dkey if head == 0 else dkeys[index] + dkey
                dvalues[index] = dvalue if head == 0 else dvalues[index] + dvalue
            parts.append(part * scale)
        for index, span in enumerate(spans):
            if seg == length // SEG - 1:
                dkey_ref[span, :] = dkeys[index]
                dvalue_ref[span, :] = dvalues[index]
            else:
                dkey_ref[span, :] += dkeys[index]
                dvalue_ref[span, :] += dvalues[index]
        out_ref[rows, 0:128] = jnp.transpose(jnp.concatenate(parts, axis=0)).astype(LOW)
    out_ref[:, 128:256] = dkey_ref[...].astype(LOW)
    out_ref[:, 256:384] = dvalue_ref[...].astype(LOW)


def back_kernel(
    xhat_ref,
    qkv_ref,
    grad_ref,
    log_ref,
    weight_ref,
    dqkv_ref,
    dnorm_ref,
    sum_ref,
    vec_ref,
    dkey_ref,
    dvalue_ref,
    acc_ref,
    *,
    scale,
):
    step = pl.program_id(0)
    attend_back_pair(qkv_ref, grad_ref, log_ref, dqkv_ref, dkey_ref, dvalue_ref, scale)
    dnorm = contract_last(dqkv_ref[...], weight_ref[...])
    sum_ref[...] = jnp.broadcast_to(
        jnp.sum(dqkv_ref[...].astype(jnp.float32), axis=0, keepdims=True)[None], sum_ref.shape
    )

    @pl.when(step == 0)
    def _():
        acc_ref[...] = dnorm

    @pl.when((step > 0) & (step < pl.num_programs(0) - 1))
    def _():
        acc_ref[...] += dnorm

    @pl.when(step == pl.num_programs(0) - 1)
    def _():
        total = acc_ref[...] + dnorm
        dnorm_ref[...] = total.astype(LOW)
        vec_ref[0:1, :] = jnp.sum(total * xhat_ref[...].astype(jnp.float32), axis=0, keepdims=True)
        vec_ref[1:8, :] = jnp.broadcast_to(
            jnp.sum(total, axis=0, keepdims=True), (7, total.shape[1])
        )


def back_product(xhat, qkv, grad, logs, weight, scale):
    length, columns = qkv.shape
    width = weight.shape[0]
    pairs = columns // 384
    once = pl.Buffered(1)
    square = pl.BlockSpec((length, width), lambda p: (0, 0), pipeline_mode=once)
    return pl.pallas_call(
        functools.partial(back_kernel, scale=scale),
        grid=(pairs,),
        in_specs=[
            square,
            pl.BlockSpec((length, 384), lambda p: (0, p)),
            pl.BlockSpec((length, 128), lambda p: (0, p)),
            pl.BlockSpec((1, 8, length), lambda p: (p, 0, 0)),
            pl.BlockSpec((width, 384), lambda p: (0, p)),
        ],
        out_specs=[
            pl.BlockSpec((length, 384), lambda p: (0, p)),
            square,
            pl.BlockSpec((1, 8, 384), lambda p: (p, 0, 0)),
            whole((8, width)),
        ],
        out_shape=[
            jax.ShapeDtypeStruct((length, columns), LOW),
            jax.ShapeDtypeStruct((length, width), LOW),
            jax.ShapeDtypeStruct((pairs, 8, 384), jnp.float32),
            jax.ShapeDtypeStruct((8, width), jnp.float32),
        ],
        scratch_shapes=[
            pltpu.VMEM((length, 128), jnp.float32),
            pltpu.VMEM((length, 128), jnp.float32),
            pltpu.VMEM((length, width), jnp.float32),
        ],
        compiler_params=settings(56),
        cost_estimate=cost(2 * length * width * columns * 48, 12 * length * width),
        name="back",
    )(xhat, qkv, grad, logs, weight)


def last_kernel(place_ref, x_ref, dbranch_ref, own_ref, other_ref, vec_ref, out_ref):
    dnorm = own_ref[...].astype(jnp.float32) + other_ref[...].astype(jnp.float32)
    xhat, inverse = row_stats(x_ref[...].astype(jnp.float32))
    back = norm_back(dnorm, xhat, inverse, vec_ref[0:1, :])
    out_ref[...] = dbranch_ref[...].astype(jnp.float32) + back


def last_product(place, x, dbranch, own, other, vectors):
    rows, width = other.shape
    block = 128
    steps = rows // block
    mine = pl.BlockSpec((block, width), lambda p, place: (place[0] * steps + p, 0))
    plain = pl.BlockSpec((block, width), lambda p, _: (p, 0))
    return pl.pallas_call(
        last_kernel,
        grid_spec=pltpu.PrefetchScalarGridSpec(
            num_scalar_prefetch=1,
            grid=(steps,),
            in_specs=[plain, mine, mine, plain, whole(vectors.shape)],
            out_specs=plain,
        ),
        out_shape=jax.ShapeDtypeStruct((rows, width), jnp.float32),
        compiler_params=settings(16),
        cost_estimate=cost(40 * rows * width, 320 * rows * width),
        name="last",
    )(place, x, dbranch, own, other, vectors)


def result_kernel(place_ref, resid_ref, own_ref, other_ref, vec_ref, out_ref):
    mixed = own_ref[...].astype(jnp.float32) + other_ref[...].astype(jnp.float32)
    total = resid_ref[...].astype(jnp.float32) + mixed + vec_ref[5:6, :]
    out_ref[...] = total.astype(LOW)


def result_product(place, resid, own, other, vectors):
    rows, width = other.shape
    block = 128
    steps = rows // block
    mine = pl.BlockSpec((block, width), lambda p, place: (place[0] * steps + p, 0))
    plain = pl.BlockSpec((block, width), lambda p, _: (p, 0))
    return pl.pallas_call(
        result_kernel,
        grid_spec=pltpu.PrefetchScalarGridSpec(
            num_scalar_prefetch=1,
            grid=(steps,),
            in_specs=[mine, mine, plain, whole(vectors.shape)],
            out_specs=plain,
        ),
        out_shape=jax.ShapeDtypeStruct((rows, width), LOW),
        compiler_params=settings(16),
        cost_estimate=cost(10 * rows * width, 320 * rows * width),
        name="result",
    )(place, resid, own, other, vectors)


def pack_kernel(proj_ref, out_ref, up_ref, down_ref, vec_ref, narrow_ref, wide_ref):
    columns = proj_ref.shape[2]
    for pair in range(columns // 128):
        for kind in range(3):
            start = (pair * 3 + kind) * 128
            narrow_ref[:, start : start + 128] = proj_ref[kind, :, pair * 128 : pair * 128 + 128]
    narrow_ref[:, 3 * columns : 4 * columns] = out_ref[...]
    turned = jnp.transpose(vec_ref[...].astype(jnp.float32))
    turned = jnp.concatenate([turned, jnp.zeros((SLOT, 112), jnp.float32)], axis=1)
    narrow_ref[:, 4 * columns :] = turned.astype(LOW)
    hidden = up_ref.shape[1]
    wide_ref[:, :hidden] = up_ref[...]
    wide_ref[:, hidden:] = down_ref[...]


def pack_shards(proj, out, up, down, vec):
    rows, columns = out.shape
    return pl.pallas_call(
        pack_kernel,
        out_shape=[
            jax.ShapeDtypeStruct((rows, 4 * columns + 128), LOW),
            jax.ShapeDtypeStruct((rows, 2 * up.shape[1]), LOW),
        ],
        compiler_params=settings(56),
        cost_estimate=cost(0, 4 * rows * (4 * columns + 2 * up.shape[1])),
        name="pack",
    )(proj, out, up, down, vec)


def after(value, *events):
    return lax.optimization_barrier((value,) + events)[0]


def dp_shift(value, ranks, dz, dy, dc):
    far, near = 4, ranks // 8

    def goes(rank):
        z, y, c = rank // (near * 2), rank // 2 % near, rank % 2
        return ((z + dz) % far * near + (y + dy) % near) * 2 + (c + dc) % 2

    return lax.ppermute(value, "dp", [(rank, goes(rank)) for rank in range(ranks)])


def dp_gather(shard, ranks, event):
    far = [shard] + [dp_shift(shard, ranks, k, 0, 0) for k in (1, 2, 3)]
    sent = far[:2] + [after(far[2], event)] + far[3:]
    near = [dp_shift(piece, ranks, 0, 1, 0) for piece in sent]
    pieces = far + near
    return pieces + [dp_shift(piece, ranks, 0, 0, 1) for piece in pieces], pieces


def reduce_core(left, right, ranks):
    half = left.shape[0] // 2
    return dp_shift(matmul(left[half:], right).astype(LOW), ranks, 0, 0, 1)


def reduce_near(left, right, other):
    half = left.shape[0] // 2
    part = half // 2
    sent = matmul(left[part:half], right) + other[part:].astype(jnp.float32)
    return sent.astype(LOW)


def reduce_sum(left, right, other, arrived):
    part = left.shape[0] // 4
    total = matmul(left[:part], right) + other[:part].astype(jnp.float32)
    return total + arrived.astype(jnp.float32)


def far_send(total, ranks, wire=LOW):
    rows = total.shape[0] // 4
    low = total.astype(wire)
    return [dp_shift(low[k * rows : (k + 1) * rows], ranks, -k, 0, 0) for k in (2, 3, 1)]


def far_sum(total, sent):
    result = total[: total.shape[0] // 4]
    for value in sent:
        result = result + value.astype(jnp.float32)
    return result


def swap(value):
    return lax.ppermute(value, "tensor", [(0, 1), (1, 0)])


def paired(
    inputs,
    out_grad,
    parents,
    ln1_gain,
    ln1_bias,
    w_qkv,
    qv_bias,
    w_attn_out,
    attn_out_bias,
    ln2_gain,
    ln2_bias,
    w_up,
    up_bias,
    w_down,
    down_bias,
):
    ranks = lax.axis_size("dp")
    near = ranks // 8
    rank = lax.axis_index("dp")
    side = lax.axis_index("tensor")
    rows, width = inputs.shape
    shard = width // ranks
    heads_width = w_qkv.shape[2]
    pairs = heads_width // 128
    hidden = w_up.shape[1]
    scale = 1.0 / math.sqrt(width // HEADS)

    slots = jnp.arange(ranks, dtype=jnp.int32)
    core_step, near_step, far_step = slots // (ranks // 2), slots // 4 % near, slots % 4
    my_z, my_y, my_c = rank // (2 * near), rank // 2 % near, rank % 2
    source = ((my_z - far_step) % 4 * near + (my_y - near_step) % near) * 2 + (
        my_c + core_step
    ) % 2
    place = jnp.concatenate([jnp.stack([side, my_z, my_y, my_c]), source]).astype(jnp.int32)
    feature = jnp.repeat(source * shard, shard) + jnp.tile(
        jnp.arange(shard, dtype=jnp.int32), ranks
    )
    to_local = (jnp.arange(width, dtype=jnp.int32)[:, None] == feature[None, :]).astype(LOW)
    slot_of = (slots[:, None] == source[None, :]).astype(jnp.float32)

    zero = jnp.zeros_like(ln1_gain)
    vec = [ln1_gain, ln1_bias, attn_out_bias, ln2_gain, ln2_bias, down_bias, zero, zero]
    vec = jnp.concatenate(
        [jnp.stack(vec), qv_bias, up_bias.reshape(4, shard), jnp.zeros((2, shard), LOW)], axis=0
    )
    narrow_shard, wide_shard = pack_shards(w_qkv, w_attn_out.T, w_up, w_down.T, vec)
    narrow, narrow_far = dp_gather(narrow_shard, ranks, place)
    inputs_other = swap(after(inputs, narrow_shard))
    grad_other = swap(after(out_grad, inputs_other))
    wide = lax.all_gather(
        after(wide_shard, inputs_other, *narrow_far[1:6]), "dp", axis=0, tiled=True
    )

    def in_order(own, other):
        return jnp.where(
            side == 0,
            jnp.concatenate([own, other], axis=0),
            jnp.concatenate([other, own], axis=0),
        )

    def to_slots(value):
        return lax.dot_general(
            to_local, value, (((0,), (1,)), ((), ())), preferred_element_type=jnp.float32
        ).astype(LOW)

    def other_rows(value):
        return lax.dynamic_slice_in_dim(value, (1 - side) * rows, rows, 0)

    early = front(place, inputs, inputs_other, narrow, pairs, scale)
    hidden_in, xhat, norm_one, out_full, qkv, attended, logs, share, proj_full = early[:9]
    vectors, hidden_bias = early[9:]
    cotangent = after(in_order(out_grad, grad_other), share)
    lefts = jnp.stack([cotangent, jnp.zeros_like(cotangent)])
    norm_slot = to_slots(after(norm_one, share))
    resid, lefts, rights, dnorm_share, dpre_sum = feed_product(
        place, hidden_in, share, swap(after(share, grad_other)), vectors, hidden_bias, lefts, wide
    )
    dnorm_other = swap(dnorm_share)
    wide_share = lax.dot_general(
        lefts,
        after(rights, dnorm_share),
        (((1,), (1,)), ((0,), (0,))),
        preferred_element_type=jnp.float32,
    ).astype(LOW)
    wide_grad = lax.psum_scatter(wide_share, "dp", scatter_dimension=1, tiled=True)
    mixed_share = contract_last(after(rights, wide_share)[0], wide[:, hidden:]).astype(LOW)
    dbranch, dattended, mid_sum = mid_product(
        after(resid, mixed_share, norm_slot), dnorm_share, dnorm_other, lefts, vectors, out_full
    )
    dqkv, dnorm_one, dqkv_sum, front_sum = back_product(
        xhat, qkv, dattended, logs, proj_full, scale
    )
    dqkv_sum = dqkv_sum[:, 0].reshape(pairs, 3, 128)
    placed = [
        place_block(value, 2 * value.shape[0], side * value.shape[0]).reshape(ranks, -1)
        for value in (
            dqkv_sum[:, 0].reshape(heads_width),
            dqkv_sum[:, 2].reshape(heads_width),
            dpre_sum[0],
        )
    ]
    pack = jnp.stack([front_sum[0], front_sum[1], mid_sum[2], mid_sum[0], mid_sum[1], mid_sum[3]])
    pack = pack.reshape(6, ranks, shard).transpose(1, 0, 2).reshape(ranks, -1)
    pack = lax.dot_general(
        slot_of,
        jnp.concatenate([pack] + placed, axis=1),
        (((0,), (0,)), ((), ())),
        precision=lax.Precision.HIGHEST,
        preferred_element_type=jnp.float32,
    )
    proj_core = reduce_core(norm_slot, dqkv, ranks)
    dbranch_slot = to_slots(after(dbranch, pack))
    pack = pack + swap(pack)
    out_core = reduce_core(dbranch_slot, attended, ranks)
    slim_near = jnp.concatenate(
        [
            reduce_near(norm_slot, dqkv, proj_core),
            reduce_near(dbranch_slot, attended, out_core),
        ],
        axis=1,
    )
    pack = pack[: ranks // 2] + dp_shift(after(pack[ranks // 2 :], slim_near), ranks, 0, 0, 1)
    slim_near, pack = lax.optimization_barrier((slim_near, pack))
    back_other = swap(other_rows(after(dnorm_one, pack)))
    pack_arrived = dp_shift(pack[ranks // 4 :], ranks, 0, 1, 0)
    slim_arrived = dp_shift(slim_near, ranks, 0, 1, 0)
    own_other = swap(other_rows(after(mixed_share, back_other)))
    slim_arrived, pack_arrived, back_other = lax.optimization_barrier(
        (slim_arrived, pack_arrived, back_other)
    )
    columns = 3 * heads_width
    slim_total, pack_total = lax.optimization_barrier(
        (
            jnp.concatenate(
                [
                    reduce_sum(norm_slot, dqkv, proj_core, slim_arrived[:, :columns]),
                    reduce_sum(dbranch_slot, attended, out_core, slim_arrived[:, columns:]),
                ],
                axis=1,
            ),
            pack[: ranks // 4] + pack_arrived,
        )
    )
    grad_back = wide_grad[0].T.astype(jnp.float32)
    grad_hidden = wide_grad[1].astype(jnp.float32)
    pack = far_sum(pack_total, far_send(pack_total, ranks, jnp.float32)).reshape(-1)
    slim_sent = far_send(slim_total, ranks)
    slim_grad = far_sum(after(slim_total, grad_back, grad_hidden), slim_sent)
    grad_proj = slim_grad[:, :columns]
    grad_out = slim_grad[:, columns:].T
    result = result_product(
        place, after(resid, slim_total), mixed_share, own_other, vectors
    )
    input_grad = last_product(
        place, inputs, dbranch, dnorm_one, after(back_other, slim_total), vectors
    )
    grad_proj = grad_proj.reshape(shard, pairs, 3, 128).transpose(2, 0, 1, 3)
    grad_proj = grad_proj.reshape(3, shard, heads_width)
    vector_grads = [pack[i * shard : (i + 1) * shard] for i in range(6)]
    return (
        result,
        input_grad,
        vector_grads[0],
        vector_grads[1],
        grad_proj,
        pack[6 * shard : 8 * shard].reshape(2, shard),
        grad_out,
        vector_grads[2],
        vector_grads[3],
        vector_grads[4],
        grad_hidden,
        pack[8 * shard :],
        grad_back,
        vector_grads[5],
    )


def local(*arrays):
    fits = lax.axis_size("tensor") == 2 and lax.axis_size("dp") == 16
    if fits and arrays[2].shape[1] == 3:
        return paired(*arrays)
    return generic(*arrays)


def solution(mesh):
    return jax.shard_map(
        local,
        mesh=mesh,
        in_specs=(
            P(("dp", "tensor"), None),
            P(("dp", "tensor"), None),
            P("dp", None),
            P("dp"),
            P("dp"),
            P(None, "dp", "tensor"),
            P(None, "dp"),
            P("tensor", "dp"),
            P("dp"),
            P("dp"),
            P("dp"),
            P("dp", "tensor"),
            P("dp"),
            P("tensor", "dp"),
            P("dp"),
        ),
        out_specs=(
            P(("dp", "tensor"), None),
            P(("dp", "tensor"), None),
            P("dp"),
            P("dp"),
            P(None, "dp", "tensor"),
            P(None, "dp"),
            P("tensor", "dp"),
            P("dp"),
            P("dp"),
            P("dp"),
            P("dp", "tensor"),
            P("dp"),
            P("tensor", "dp"),
            P("dp"),
        ),
        check_vma=False,
    )
```

```python
import functools
import math

import jax
import jax.numpy as jnp
from jax import lax
from jax.experimental import pallas as pl
from jax.experimental.pallas import tpu as pltpu
from jax.sharding import PartitionSpec as P

HEADS = 16
SEG = 256


epsilon = 1e-05
gelu_coef = 0.7978845608028654


def layer_norm(values, scales, shifts):
    centre = jnp.mean(values, axis=-1, keepdims=True)
    shifted = values - centre
    spread = jnp.mean(shifted * shifted, axis=-1, keepdims=True)
    return shifted * lax.rsqrt(spread + epsilon) * scales + shifts


def gelu_tanh(values):
    return (
        0.5 * values * (1.0 + jnp.tanh(gelu_coef * (values + 0.044715 * values * values * values)))
    )


def matmul(left, right):
    return jnp.dot(left, right, preferred_element_type=jnp.float32)


def contract_rows(left, right):
    return lax.dot_general(
        left, right, (((0,), (0,)), ((), ())), preferred_element_type=jnp.float32
    )


def contract_last(left, right):
    return lax.dot_general(
        left, right, (((1,), (1,)), ((), ())), preferred_element_type=jnp.float32
    )


def ancestors(parent_row, segment_count):
    labels = jnp.arange(segment_count, dtype=jnp.int32)
    links = ((parent_row[:, None] == labels[None, :]) & (labels[:, None] > 0)).astype(jnp.float32)
    identity = jnp.eye(segment_count, dtype=jnp.float32)

    def extend(turn, reached):
        grown = jnp.dot(
            links, reached, precision=lax.Precision.HIGHEST, preferred_element_type=jnp.float32
        )
        return jnp.minimum(identity + grown, 1.0)

    return lax.fori_loop(0, segment_count, extend, identity)


def tree_mask(reached, first_row, block_rows, length):
    query_pos = first_row + jnp.arange(block_rows, dtype=jnp.int32)
    key_pos = jnp.arange(length, dtype=jnp.int32)
    segment_count = reached.shape[0]
    onehot = (
        (query_pos // SEG)[:, None] == jnp.arange(segment_count, dtype=jnp.int32)[None, :]
    ).astype(jnp.float32)
    row_reach = jnp.dot(
        onehot, reached, precision=lax.Precision.HIGHEST, preferred_element_type=jnp.float32
    )
    spread_out = jnp.repeat(row_reach, SEG, axis=1)
    return (spread_out > 0.5) & (key_pos[None, :] <= query_pos[:, None])


def row_block(length):
    pieces = -(-length // 512)
    while length % pieces:
        pieces += 1
    return length // pieces


def place_block(local_vec, full_length, offset):
    empty_vec = jnp.zeros(local_vec.shape[:-1] + (full_length,), jnp.float32)
    return lax.dynamic_update_slice_in_dim(empty_vec, local_vec, offset, local_vec.ndim - 1)


def generic(
    inputs,
    out_grad,
    parents,
    ln1_gain,
    ln1_bias,
    w_qkv,
    qv_bias,
    w_attn_out,
    attn_out_bias,
    ln2_gain,
    ln2_bias,
    w_up,
    up_bias,
    w_down,
    down_bias,
):
    tensor_ranks = lax.axis_size("tensor")
    tensor_rank = lax.axis_index("tensor")
    rows_own = inputs.shape[0]
    length = rows_own * tensor_ranks
    model_width = inputs.shape[1]
    head_dim = model_width // HEADS
    local_width = w_qkv.shape[2]
    local_hidden = w_up.shape[1]
    heads_here = local_width // head_dim
    scale = 1.0 / math.sqrt(head_dim)
    gathered = (
        lax.all_gather(w_qkv, "dp", axis=1, tiled=True),
        lax.all_gather(w_attn_out, "dp", axis=1, tiled=True),
        lax.all_gather(w_up, "dp", axis=0, tiled=True),
        lax.all_gather(w_down, "dp", axis=1, tiled=True),
        lax.all_gather(ln1_gain, "dp", axis=0, tiled=True),
        lax.all_gather(ln1_bias, "dp", axis=0, tiled=True),
        lax.all_gather(qv_bias, "dp", axis=1, tiled=True),
        lax.all_gather(attn_out_bias, "dp", axis=0, tiled=True),
        lax.all_gather(ln2_gain, "dp", axis=0, tiled=True),
        lax.all_gather(ln2_bias, "dp", axis=0, tiled=True),
        lax.all_gather(up_bias, "dp", axis=0, tiled=True),
        lax.all_gather(down_bias, "dp", axis=0, tiled=True),
    )
    proj_full, out_full, hidden_full, back_full = (
        gathered[0],
        gathered[1],
        gathered[2],
        gathered[3],
    )
    gain_one = gathered[4].astype(jnp.float32)
    shift_one = gathered[5].astype(jnp.float32)
    proj_bias = lax.dynamic_slice_in_dim(
        gathered[6].astype(jnp.float32), tensor_rank * local_width, local_width, 1
    )
    out_bias = gathered[7].astype(jnp.float32)
    gain_two = gathered[8].astype(jnp.float32)
    shift_two = gathered[9].astype(jnp.float32)
    hidden_bias_full = gathered[10].astype(jnp.float32)
    back_bias = gathered[11].astype(jnp.float32)
    full_hidden = hidden_bias_full.shape[0]
    hidden_in = inputs.astype(jnp.float32)
    norm_one, ln1_pull = jax.vjp(layer_norm, hidden_in, gain_one, shift_one)
    norm_one_all = lax.all_gather(norm_one.astype(jnp.bfloat16), "tensor", axis=0, tiled=True)
    queries = (matmul(norm_one_all, proj_full[0]) + proj_bias[0]).astype(jnp.bfloat16)
    keys_low = matmul(norm_one_all, proj_full[1]).astype(jnp.bfloat16)
    values_low = (matmul(norm_one_all, proj_full[2]) + proj_bias[1]).astype(jnp.bfloat16)
    reached = ancestors(parents[0], length // SEG)
    block_rows = row_block(length)
    num_blocks = length // block_rows
    starts = jnp.arange(num_blocks, dtype=jnp.int32) * block_rows
    query_blocks = queries.reshape(num_blocks, block_rows, heads_here, head_dim)
    key_heads = keys_low.reshape(length, heads_here, head_dim)
    value_heads = values_low.reshape(length, heads_here, head_dim)

    def block_scores(query_block, first_row):
        scores = (
            jnp.einsum("qhd,khd->hqk", query_block, key_heads, preferred_element_type=jnp.float32)
            * scale
        )
        allowed = tree_mask(reached, first_row, block_rows, length)
        return jnp.where(allowed[None], scores, -1e30)

    def forward_block(element):
        query_block, first_row = element
        scores = block_scores(query_block, first_row)
        top_score = jnp.max(scores, axis=-1, keepdims=True)
        expo = jnp.exp(scores - top_score)
        totals = jnp.sum(expo, axis=-1, keepdims=True)
        probs = (expo / totals).astype(jnp.bfloat16)
        attended_block = jnp.einsum(
            "hqk,khd->qhd", probs, value_heads, preferred_element_type=jnp.float32
        )
        return (attended_block, (top_score + jnp.log(totals))[..., 0])

    attended_blocks, log_totals = lax.map(forward_block, (query_blocks, starts))
    attended = attended_blocks.reshape(length, local_width).astype(jnp.bfloat16)
    branch = (
        lax.psum_scatter(matmul(attended, out_full), "tensor", scatter_dimension=0, tiled=True)
        + out_bias
    )
    resid = hidden_in + branch
    norm_two, ln2_pull = jax.vjp(layer_norm, resid, gain_two, shift_two)
    norm_two_low = norm_two.astype(jnp.bfloat16)
    grad_back_bias = jnp.sum(out_grad.astype(jnp.float32), axis=0)
    norm_two_all = lax.all_gather(norm_two_low, "tensor", axis=0, tiled=True)
    hidden_slice = lax.dynamic_slice_in_dim(
        hidden_bias_full, tensor_rank * local_hidden, local_hidden, 0
    )
    pre = matmul(norm_two_all, hidden_full) + hidden_slice
    act, gelu_pull = jax.vjp(gelu_tanh, pre)
    act_low = act.astype(jnp.bfloat16)
    mixed = (
        lax.psum_scatter(
            matmul(act_low, back_full).astype(jnp.bfloat16),
            "tensor",
            scatter_dimension=0,
            tiled=True,
        ).astype(jnp.float32)
        + back_bias
    )
    cotangent_all = lax.all_gather(out_grad, "tensor", axis=0, tiled=True)
    grad_back = contract_rows(act_low, cotangent_all)
    (dpre,) = gelu_pull(contract_last(cotangent_all, back_full))
    dpre_low = dpre.astype(jnp.bfloat16)
    grad_hidden = contract_rows(norm_two_all, dpre_low)
    grad_hidden_bias = place_block(
        jnp.sum(dpre_low.astype(jnp.float32), axis=0), full_hidden, tensor_rank * local_hidden
    )
    dnorm_two = lax.psum_scatter(
        contract_last(dpre_low, hidden_full), "tensor", scatter_dimension=0, tiled=True
    )
    result = (resid + mixed).astype(jnp.bfloat16)
    dresid_part, grad_gain_two, grad_shift_two = ln2_pull(dnorm_two)
    dresid = out_grad.astype(jnp.float32) + dresid_part
    dbranch = dresid.astype(jnp.bfloat16)
    grad_out_bias = jnp.sum(dbranch.astype(jnp.float32), axis=0)
    dbranch_all = lax.all_gather(dbranch, "tensor", axis=0, tiled=True)
    grad_out = contract_rows(attended, dbranch_all)
    dattended = contract_last(dbranch_all, out_full).astype(jnp.bfloat16)
    dattended_blocks = dattended.reshape(num_blocks, block_rows, heads_here, head_dim)

    def backward_block(carry, element):
        dkey_acc, dvalue_acc = carry
        query_block, dattended_block, log_block, first_row = element
        scores = block_scores(query_block, first_row)
        probs = jnp.exp(scores - log_block[..., None])
        dvalue_acc = dvalue_acc + jnp.einsum(
            "hqk,qhd->khd",
            probs.astype(jnp.bfloat16),
            dattended_block,
            preferred_element_type=jnp.float32,
        )
        dprobs = jnp.einsum(
            "qhd,khd->hqk", dattended_block, value_heads, preferred_element_type=jnp.float32
        )
        dscores = probs * (dprobs - jnp.sum(dprobs * probs, axis=-1, keepdims=True))
        dscores_low = dscores.astype(jnp.bfloat16)
        dquery_block = (
            jnp.einsum("hqk,khd->qhd", dscores_low, key_heads, preferred_element_type=jnp.float32)
            * scale
        )
        dkey_acc = (
            dkey_acc
            + jnp.einsum(
                "hqk,qhd->khd", dscores_low, query_block, preferred_element_type=jnp.float32
            )
            * scale
        )
        return ((dkey_acc, dvalue_acc), dquery_block)

    zero_heads = jnp.zeros((length, heads_here, head_dim), jnp.float32)
    (dkey_acc, dvalue_acc), dquery_blocks = lax.scan(
        backward_block,
        (zero_heads, zero_heads),
        (query_blocks, dattended_blocks, log_totals, starts),
    )
    dqueries = dquery_blocks.reshape(length, local_width).astype(jnp.bfloat16)
    dkeys = dkey_acc.reshape(length, local_width).astype(jnp.bfloat16)
    dvalues = dvalue_acc.reshape(length, local_width).astype(jnp.bfloat16)
    grad_proj = jnp.stack(
        [
            contract_rows(norm_one_all, dqueries),
            contract_rows(norm_one_all, dkeys),
            contract_rows(norm_one_all, dvalues),
        ]
    )
    local_bias_grad = jnp.stack(
        [
            jnp.sum(dqueries.astype(jnp.float32), axis=0),
            jnp.sum(dvalues.astype(jnp.float32), axis=0),
        ]
    )
    grad_proj_bias = place_block(local_bias_grad, model_width, tensor_rank * local_width)
    dnorm_one = lax.psum_scatter(
        (
            contract_last(dqueries, proj_full[0])
            + contract_last(dkeys, proj_full[1])
            + contract_last(dvalues, proj_full[2])
        ).astype(jnp.bfloat16),
        "tensor",
        scatter_dimension=0,
        tiled=True,
    ).astype(jnp.float32)
    dinput_part, grad_gain_one, grad_shift_one = ln1_pull(dnorm_one)
    input_grad = dresid + dinput_part
    summed = (
        lax.psum_scatter(grad_proj, "dp", scatter_dimension=1, tiled=True),
        lax.psum_scatter(grad_out, "dp", scatter_dimension=1, tiled=True),
        lax.psum_scatter(grad_hidden, "dp", scatter_dimension=0, tiled=True),
        lax.psum_scatter(grad_back, "dp", scatter_dimension=1, tiled=True),
        lax.psum_scatter(grad_gain_one, "dp", scatter_dimension=0, tiled=True),
        lax.psum_scatter(grad_shift_one, "dp", scatter_dimension=0, tiled=True),
        lax.psum_scatter(grad_proj_bias, "dp", scatter_dimension=1, tiled=True),
        lax.psum_scatter(grad_out_bias, "dp", scatter_dimension=0, tiled=True),
        lax.psum_scatter(grad_gain_two, "dp", scatter_dimension=0, tiled=True),
        lax.psum_scatter(grad_shift_two, "dp", scatter_dimension=0, tiled=True),
        lax.psum_scatter(grad_hidden_bias, "dp", scatter_dimension=0, tiled=True),
        lax.psum_scatter(grad_back_bias, "dp", scatter_dimension=0, tiled=True),
    )
    vectors = lax.psum(
        (summed[4], summed[5], summed[6], summed[7], summed[8], summed[9], summed[10], summed[11]),
        "tensor",
    )
    return (
        result,
        input_grad,
        vectors[0],
        vectors[1],
        summed[0],
        vectors[2],
        summed[1],
        vectors[3],
        vectors[4],
        vectors[5],
        summed[2],
        vectors[6],
        summed[3],
        vectors[7],
    )


LOW = jnp.bfloat16
SLOT = 64


def settings(mib):
    return pltpu.CompilerParams(vmem_limit_bytes=mib * 2**20)


def cost(flops, moved, exps=0):
    return pl.CostEstimate(
        flops=int(flops), bytes_accessed=int(moved), transcendentals=int(exps)
    )


def whole(shape):
    return pl.BlockSpec(shape, lambda *_: (0,) * len(shape))


def piece_specs(pieces, block, first=0):
    return [
        pl.BlockSpec((piece.shape[0], block), lambda p, *_: (0, first + p)) for piece in pieces
    ]


def fixed_specs(pieces, block, index):
    return [pl.BlockSpec((piece.shape[0], block), lambda *_: (0, index)) for piece in pieces]


def fill_natural(place_ref, scratch, refs):
    for slot, ref in enumerate(refs):
        start = pl.multiple_of(place_ref[4 + slot] * SLOT, SLOT)
        scratch[pl.ds(start, SLOT), :] = ref[...]


def row_stats(rows):
    centre = jnp.mean(rows, axis=-1, keepdims=True)
    shifted = rows - centre
    spread = jnp.mean(shifted * shifted, axis=-1, keepdims=True)
    inverse = lax.rsqrt(spread + epsilon)
    return shifted * inverse, inverse


def norm_back(dnorm, xhat, inverse, gain):
    scaled = dnorm * gain
    return inverse * (
        scaled
        - jnp.mean(scaled, axis=-1, keepdims=True)
        - xhat * jnp.mean(scaled * xhat, axis=-1, keepdims=True)
    )


def attend_pair(qkv_ref, out_ref, log_ref, scale):
    length = qkv_ref.shape[0]
    lane = lax.broadcasted_iota(jnp.int32, (SEG, 128), 1)
    reach = lax.broadcasted_iota(jnp.int32, (SEG, SEG), 0) <= lax.broadcasted_iota(
        jnp.int32, (SEG, SEG), 1
    )
    value_t = jnp.transpose(qkv_ref[:, 256:384])
    for seg in range(length // SEG):
        before = seg * SEG
        rows = slice(before, before + SEG)
        query = qkv_ref[rows, 0:128] * scale
        parts = []
        drawn = []
        for head in range(2):
            mine = jnp.where(lane // 64 == head, query, jnp.zeros_like(query))
            scores = contract_last(qkv_ref[rows, 128:256], mine)
            early = contract_last(qkv_ref[0:before, 128:256], mine) if seg > 0 else None
            drawn.append((jnp.where(reach, scores, -1e30), early))
        for head in range(2):
            lanes = slice(head * 64, head * 64 + 64)
            scores, early = drawn[head]
            top = jnp.max(scores, axis=0, keepdims=True)
            if seg > 0:
                top = jnp.maximum(top, jnp.max(early, axis=0, keepdims=True))
            expo = jnp.exp(scores - top)
            total = jnp.sum(expo, axis=0, keepdims=True)
            mixed = matmul(value_t[lanes, rows], expo.astype(LOW))
            if seg > 0:
                expo = jnp.exp(early - top)
                total = total + jnp.sum(expo, axis=0, keepdims=True)
                mixed = mixed + matmul(value_t[lanes, 0:before], expo.astype(LOW))
            parts.append(mixed / total)
            log_ref[0, head : head + 1, rows] = top + jnp.log(total)
        out_ref[rows, :] = jnp.transpose(jnp.concatenate(parts, axis=0)).astype(LOW)


def read_vectors(vec_ref, bias_ref, hidden_ref, joined_ref):
    turned = jnp.transpose(joined_ref[...]).astype(jnp.float32)
    vec_ref[...] = turned[0:8]
    bias_ref[...] = turned[8:16]
    lane = lax.broadcasted_iota(jnp.int32, (1, 128), 1)
    for pair in range(bias_ref.shape[1] // 128):
        rows = [turned[10 + q : 11 + q, pair * 128 : pair * 128 + 128] for q in range(4)]
        flipped = [pltpu.roll(row, 64, 1) for row in rows]
        for q in (0, 2):
            start = pair * 512 + q * 64
            hidden_ref[:, start : start + 128] = jnp.where(lane < 64, rows[q], flipped[q + 1])
            hidden_ref[:, start + 256 : start + 384] = jnp.where(
                lane < 64, flipped[q], rows[q + 1]
            )


def front_kernel(place_ref, own_ref, other_ref, *refs, scale, count):
    pieces, outs, vecs = (refs[i * count : (i + 1) * count] for i in range(3))
    kept, refs = refs[3 * count : 3 * count + 4], refs[3 * count + 4 :]
    qkv_ref, att_ref, log_ref, share_ref, weight_ref, vec_ref, hidden_ref = refs[:7]
    x_ref, xhat_ref, norm_ref, out_ref, joined_ref, bias_ref, lines_ref, sem = refs[7:]
    pairs = pl.num_programs(0)
    copies = [
        pltpu.make_async_copy(source, target, sem.at[index])
        for index, (source, target) in enumerate(zip((x_ref, xhat_ref, norm_ref, out_ref), kept))
    ]
    rows_own = own_ref.shape[0]
    step = pl.program_id(0)

    @pl.when(step == 0)
    def _():
        fill_natural(place_ref, lines_ref, vecs)
        read_vectors(vec_ref, bias_ref, hidden_ref, lines_ref)
        for half, ref in ((place_ref[0], own_ref), (1 - place_ref[0], other_ref)):
            for start in range(0, rows_own, 128):
                rows = pl.ds(pl.multiple_of(half * rows_own + start, 128), 128)
                x = ref[start : start + 128, :]
                xhat, _ = row_stats(x.astype(jnp.float32))
                x_ref[rows, :] = x
                xhat_ref[rows, :] = xhat.astype(LOW)
                norm_ref[rows, :] = (xhat * vec_ref[0:1, :] + vec_ref[1:2, :]).astype(LOW)
        fill_natural(place_ref, out_ref, outs)
        for copy in copies:
            copy.start()

    fill_natural(place_ref, weight_ref, pieces)
    mine = pl.ds(pl.multiple_of((place_ref[0] * pairs + step) * 128, 128), 128)
    bias = jnp.concatenate(
        [bias_ref[0:1, mine], jnp.zeros((1, 128), jnp.float32), bias_ref[1:2, mine]], axis=1
    )
    qkv_ref[...] = (matmul(norm_ref[...], weight_ref[...]) + bias).astype(LOW)
    attend_pair(qkv_ref, att_ref, log_ref, scale)
    joined_ref[:, pl.ds(pl.multiple_of(step * 128, 128), 128)] = att_ref[...]

    @pl.when(step == pl.num_programs(0) - 1)
    def _():
        share_ref[...] = contract_last(joined_ref[...], out_ref[...]).astype(LOW)
        for copy in copies:
            copy.wait()


def front(place, own, other, pieces, pairs, scale):
    length, width = 2 * own.shape[0], own.shape[1]
    once = pl.Buffered(1)
    square = pl.BlockSpec((length, width), lambda *_: (0, 0), pipeline_mode=once)
    half = pl.BlockSpec(own.shape, lambda *_: (0, 0), pipeline_mode=once)
    return pl.pallas_call(
        functools.partial(front_kernel, scale=scale, count=len(pieces)),
        grid_spec=pltpu.PrefetchScalarGridSpec(
            num_scalar_prefetch=1,
            grid=(pairs,),
            in_specs=[
                half,
                half,
            ]
            + piece_specs(pieces, 384)
            + fixed_specs(pieces, pairs * 128, 3)
            + fixed_specs(pieces, 128, pairs * 4),
            out_specs=[pl.BlockSpec(memory_space=pl.ANY)] * 4
            + [
                pl.BlockSpec((length, 384), lambda p, _: (0, p)),
                pl.BlockSpec((length, 128), lambda p, _: (0, p)),
                pl.BlockSpec((1, 8, length), lambda p, _: (p, 0, 0)),
                square,
                pl.BlockSpec((width, 384), lambda p, _: (0, p)),
                whole((8, width)),
                whole((1, 4 * width)),
            ],
            scratch_shapes=[
                pltpu.VMEM((length, width), LOW),
                pltpu.VMEM((length, width), LOW),
                pltpu.VMEM((length, width), LOW),
                pltpu.VMEM((width, pairs * 128), LOW),
                pltpu.VMEM((length, pairs * 128), LOW),
                pltpu.VMEM((8, width), jnp.float32),
                pltpu.VMEM((width, 128), LOW),
                pltpu.SemaphoreType.DMA((4,)),
            ],
        ),
        out_shape=[
            jax.ShapeDtypeStruct((length, width), LOW),
            jax.ShapeDtypeStruct((length, width), LOW),
            jax.ShapeDtypeStruct((length, width), LOW),
            jax.ShapeDtypeStruct((width, pairs * 128), LOW),
            jax.ShapeDtypeStruct((length, pairs * 384), LOW),
            jax.ShapeDtypeStruct((length, pairs * 128), LOW),
            jax.ShapeDtypeStruct((pairs, 8, length), jnp.float32),
            jax.ShapeDtypeStruct((length, width), LOW),
            jax.ShapeDtypeStruct((width, pairs * 384), LOW),
            jax.ShapeDtypeStruct((8, width), jnp.float32),
            jax.ShapeDtypeStruct((1, 4 * width), jnp.float32),
        ],
        compiler_params=settings(56),
        cost_estimate=cost(2 * length * width * pairs * 384 * 4, 12 * length * width),
        name="front",
    )(place, own, other, *pieces, *pieces, *pieces)


def feed_kernel(
    place_ref,
    x_ref,
    own_ref,
    other_ref,
    vec_ref,
    bias_ref,
    grad_ref,
    pair_ref,
    resid_ref,
    left_ref,
    right_ref,
    dnorm_ref,
    sum_ref,
    up_ref,
    down_ref,
    sem,
):
    first = pl.program_id(0) == 0
    hidden = up_ref.shape[1]

    def fetch(start):
        part = pl.ds(start, 512)
        index = start // 512
        return (
            pltpu.make_async_copy(pair_ref.at[:, part], up_ref.at[:, part], sem.at[0, index]),
            pltpu.make_async_copy(
                pair_ref.at[:, pl.ds(hidden + start, 512)], down_ref.at[:, part], sem.at[1, index]
            ),
        )

    @pl.when(first)
    def _():
        for start in range(0, hidden, 512):
            for copy in fetch(start):
                copy.start()
        sum_ref[...] = jnp.zeros_like(sum_ref)

    branch = own_ref[...].astype(jnp.float32) + other_ref[...].astype(jnp.float32)
    resid = x_ref[...].astype(jnp.float32) + (branch + vec_ref[2:3, :])
    resid_ref[...] = resid.astype(LOW)
    xhat, _ = row_stats(resid)
    norm = (xhat * vec_ref[3:4, :] + vec_ref[4:5, :]).astype(LOW)
    left_ref[0] = norm
    for start in range(0, hidden, 512):
        columns = slice(start, start + 512)

        @pl.when(first)
        def _(start=start):
            for copy in fetch(start):
                copy.wait()

        pre = matmul(norm, up_ref[:, columns]) + bias_ref[:, columns]
        square = pre * pre
        bent = jnp.tanh(pre * (square * (0.044715 * gelu_coef) + gelu_coef))
        half = 0.5 * bent + 0.5
        act = pre * half
        right_ref[0, :, columns] = act.astype(LOW)
        slope = half + act * (1.0 - bent) * (square * (3 * 0.044715 * gelu_coef) + gelu_coef)
        dpre = (matmul(grad_ref[0], down_ref[:, columns]) * slope).astype(LOW)
        right_ref[1, :, columns] = dpre
        total = jnp.sum(dpre.astype(jnp.float32), axis=0, keepdims=True)
        sum_ref[:, columns] += jnp.broadcast_to(total, (8, 512))
    dnorm_ref[...] = contract_last(right_ref[1], up_ref[...]).astype(LOW)


def feed_product(place, x, own, other, vectors, bias, lefts, pair, block=SEG):
    length, width = x.shape
    hidden = pair.shape[1] // 2
    rows = pl.BlockSpec((block, width), lambda p, _: (p, 0))
    return pl.pallas_call(
        feed_kernel,
        grid_spec=pltpu.PrefetchScalarGridSpec(
            num_scalar_prefetch=1,
            grid=(length // block,),
            in_specs=[rows] * 3
            + [
                whole(vectors.shape),
                pl.BlockSpec((1, hidden), lambda p, place: (0, place[0])),
                pl.BlockSpec((1, block, width), lambda p, _: (0, p, 0)),
                pl.BlockSpec(memory_space=pl.ANY),
            ],
            out_specs=[
                rows,
                pl.BlockSpec((1, block, width), lambda p, _: (1, p, 0)),
                pl.BlockSpec((2, block, hidden), lambda p, _: (0, p, 0)),
                rows,
                whole((8, hidden)),
            ],
            scratch_shapes=[
                pltpu.VMEM((width, hidden), LOW),
                pltpu.VMEM((width, hidden), LOW),
                pltpu.SemaphoreType.DMA((2, hidden // 512)),
            ],
        ),
        out_shape=[
            jax.ShapeDtypeStruct((length, width), LOW),
            jax.ShapeDtypeStruct((2, length, width), LOW),
            jax.ShapeDtypeStruct((2, length, hidden), LOW),
            jax.ShapeDtypeStruct((length, width), LOW),
            jax.ShapeDtypeStruct((8, hidden), jnp.float32),
        ],
        input_output_aliases={6: 1},
        compiler_params=settings(56),
        cost_estimate=cost(9 * length * width * hidden, 40 * length * width),
        name="feed",
    )(place, x, own, other, vectors, bias, lefts, pair)


def mid_kernel(
    resid_ref, own_ref, other_ref, grad_ref, vec_ref, weight_ref, dbranch_ref, datt_ref, sum_ref
):
    @pl.when(pl.program_id(0) == 0)
    def _():
        sum_ref[...] = jnp.zeros_like(sum_ref)

    dnorm = own_ref[...].astype(jnp.float32) + other_ref[...].astype(jnp.float32)
    grad = grad_ref[0].astype(jnp.float32)
    xhat, inverse = row_stats(resid_ref[...].astype(jnp.float32))
    dresid = grad + norm_back(dnorm, xhat, inverse, vec_ref[3:4, :])
    dbranch = dresid.astype(LOW)
    dbranch_ref[...] = dbranch
    datt_ref[...] = matmul(dbranch, weight_ref[...]).astype(LOW)
    for row, value in enumerate((dbranch.astype(jnp.float32), dnorm * xhat, dnorm, grad)):
        sum_ref[row : row + 1, :] += 0.5 * jnp.sum(value, axis=0, keepdims=True)


def mid_product(resid, own, other, lefts, vectors, weight, block=SEG):
    length, width = resid.shape
    inner = weight.shape[1]
    rows = pl.BlockSpec((block, width), lambda p: (p, 0))
    return pl.pallas_call(
        mid_kernel,
        grid=(length // block,),
        in_specs=[rows] * 3
        + [
            pl.BlockSpec((1, block, width), lambda p: (0, p, 0)),
            whole(vectors.shape),
            whole(weight.shape),
        ],
        out_specs=[rows, pl.BlockSpec((block, inner), lambda p: (p, 0)), whole((8, width))],
        out_shape=[
            jax.ShapeDtypeStruct((length, width), LOW),
            jax.ShapeDtypeStruct((length, inner), LOW),
            jax.ShapeDtypeStruct((8, width), jnp.float32),
        ],
        compiler_params=settings(56),
        cost_estimate=cost(2 * length * width * inner * 16, 16 * length * width),
        name="mid",
    )(resid, own, other, lefts, vectors, weight)


def attend_back_pair(qkv_ref, grad_ref, log_ref, out_ref, dkey_ref, dvalue_ref, scale):
    length = qkv_ref.shape[0]
    lane = lax.broadcasted_iota(jnp.int32, (SEG, 128), 1)
    reach = lax.broadcasted_iota(jnp.int32, (SEG, SEG), 0) <= lax.broadcasted_iota(
        jnp.int32, (SEG, SEG), 1
    )
    key_t = jnp.transpose(qkv_ref[:, 128:256])
    for seg in reversed(range(length // SEG)):
        before = seg * SEG
        rows = slice(before, before + SEG)
        spans = [rows] if seg == 0 else [rows, slice(0, before)]
        query = qkv_ref[rows, 0:128] * scale
        grad = grad_ref[rows, :]
        parts = []
        dkeys = [None] * len(spans)
        dvalues = [None] * len(spans)
        drawn = []
        for head in range(2):
            here = lane // 64 == head
            query_mine = jnp.where(here, query, jnp.zeros_like(query))
            grad_mine = jnp.where(here, grad, jnp.zeros_like(grad))
            scores = [contract_last(qkv_ref[span, 128:256], query_mine) for span in spans]
            scores[0] = jnp.where(reach, scores[0], -1e30)
            dprobs = [contract_last(qkv_ref[span, 256:384], grad_mine) for span in spans]
            drawn.append((query_mine, grad_mine, scores, dprobs))
        for head in range(2):
            lanes = slice(head * 64, head * 64 + 64)
            query_mine, grad_mine, scores, dprobs = drawn[head]
            log_row = log_ref[0, head : head + 1, rows]
            probs = []
            mean = None
            for index in range(len(spans)):
                prob = jnp.exp(scores[index] - log_row)
                share = jnp.sum(prob * dprobs[index], axis=0, keepdims=True)
                mean = share if mean is None else mean + share
                probs.append(prob)
            part = None
            for index, span in enumerate(spans):
                dscores = (probs[index] * (dprobs[index] - mean)).astype(LOW)
                dvalue = matmul(probs[index].astype(LOW), grad_mine)
                dkey = matmul(dscores, query_mine)
                piece = matmul(key_t[lanes, span], dscores)
                part = piece if part is None else part + piece
                dkeys[index] = dkey if head == 0 else dkeys[index] + dkey
                dvalues[index] = dvalue if head == 0 else dvalues[index] + dvalue
            parts.append(part * scale)
        for index, span in enumerate(spans):
            if seg == length // SEG - 1:
                dkey_ref[span, :] = dkeys[index]
                dvalue_ref[span, :] = dvalues[index]
            else:
                dkey_ref[span, :] += dkeys[index]
                dvalue_ref[span, :] += dvalues[index]
        out_ref[rows, 0:128] = jnp.transpose(jnp.concatenate(parts, axis=0)).astype(LOW)
    out_ref[:, 128:256] = dkey_ref[...].astype(LOW)
    out_ref[:, 256:384] = dvalue_ref[...].astype(LOW)


def back_kernel(
    xhat_all_ref,
    qkv_ref,
    grad_ref,
    log_ref,
    weight_ref,
    dqkv_ref,
    dnorm_ref,
    sum_ref,
    vec_ref,
    dkey_ref,
    dvalue_ref,
    acc_ref,
    xhat_ref,
    sem,
    *,
    scale,
):
    step = pl.program_id(0)
    fetch = pltpu.make_async_copy(xhat_all_ref, xhat_ref, sem.at[0])

    @pl.when(step == 0)
    def _():
        fetch.start()

    attend_back_pair(qkv_ref, grad_ref, log_ref, dqkv_ref, dkey_ref, dvalue_ref, scale)
    dnorm = contract_last(dqkv_ref[...], weight_ref[...])
    sum_ref[0] = jnp.sum(dqkv_ref[...].astype(jnp.float32), axis=0, keepdims=True)

    @pl.when(step == 0)
    def _():
        acc_ref[...] = dnorm

    @pl.when((step > 0) & (step < pl.num_programs(0) - 1))
    def _():
        acc_ref[...] += dnorm

    @pl.when(step == pl.num_programs(0) - 1)
    def _():
        fetch.wait()
        total = acc_ref[...] + dnorm
        dnorm_ref[...] = total.astype(LOW)
        vec_ref[0:1, :] = jnp.sum(total * xhat_ref[...].astype(jnp.float32), axis=0, keepdims=True)
        vec_ref[1:2, :] = jnp.sum(total, axis=0, keepdims=True)


def back_product(xhat, qkv, grad, logs, weight, scale):
    length, columns = qkv.shape
    width = weight.shape[0]
    pairs = columns // 384
    once = pl.Buffered(1)
    square = pl.BlockSpec((length, width), lambda p: (0, 0), pipeline_mode=once)
    return pl.pallas_call(
        functools.partial(back_kernel, scale=scale),
        grid=(pairs,),
        in_specs=[
            pl.BlockSpec(memory_space=pl.ANY),
            pl.BlockSpec((length, 384), lambda p: (0, p)),
            pl.BlockSpec((length, 128), lambda p: (0, p)),
            pl.BlockSpec((1, 8, length), lambda p: (p, 0, 0)),
            pl.BlockSpec((width, 384), lambda p: (0, p)),
        ],
        out_specs=[
            pl.BlockSpec((length, 384), lambda p: (0, p)),
            square,
            pl.BlockSpec((1, 1, 384), lambda p: (p, 0, 0)),
            whole((2, width)),
        ],
        out_shape=[
            jax.ShapeDtypeStruct((length, columns), LOW),
            jax.ShapeDtypeStruct((length, width), LOW),
            jax.ShapeDtypeStruct((pairs, 1, 384), jnp.float32),
            jax.ShapeDtypeStruct((2, width), jnp.float32),
        ],
        scratch_shapes=[
            pltpu.VMEM((length, 128), jnp.float32),
            pltpu.VMEM((length, 128), jnp.float32),
            pltpu.VMEM((length, width), jnp.float32),
            pltpu.VMEM((length, width), LOW),
            pltpu.SemaphoreType.DMA((1,)),
        ],
        compiler_params=settings(56),
        cost_estimate=cost(2 * length * width * columns * 48, 12 * length * width),
        name="back",
    )(xhat, qkv, grad, logs, weight)


def last_kernel(place_ref, x_ref, dbranch_ref, own_ref, other_ref, vec_ref, out_ref):
    dnorm = own_ref[...].astype(jnp.float32) + other_ref[...].astype(jnp.float32)
    xhat, inverse = row_stats(x_ref[...].astype(jnp.float32))
    back = norm_back(dnorm, xhat, inverse, vec_ref[0:1, :])
    out_ref[...] = dbranch_ref[...].astype(jnp.float32) + back


def last_product(place, x, dbranch, own, other, vectors):
    rows, width = other.shape
    block = 128
    steps = rows // block
    mine = pl.BlockSpec((block, width), lambda p, place: (place[0] * steps + p, 0))
    plain = pl.BlockSpec((block, width), lambda p, _: (p, 0))
    return pl.pallas_call(
        last_kernel,
        grid_spec=pltpu.PrefetchScalarGridSpec(
            num_scalar_prefetch=1,
            grid=(steps,),
            in_specs=[plain, mine, mine, plain, whole(vectors.shape)],
            out_specs=plain,
        ),
        out_shape=jax.ShapeDtypeStruct((rows, width), jnp.float32),
        compiler_params=settings(16),
        cost_estimate=cost(40 * rows * width, 320 * rows * width),
        name="last",
    )(place, x, dbranch, own, other, vectors)


def result_kernel(place_ref, resid_ref, own_ref, other_ref, vec_ref, out_ref):
    mixed = own_ref[...].astype(jnp.float32) + other_ref[...].astype(jnp.float32)
    total = resid_ref[...].astype(jnp.float32) + mixed + vec_ref[5:6, :]
    out_ref[...] = total.astype(LOW)


def result_product(place, resid, own, other, vectors):
    rows, width = other.shape
    block = 128
    steps = rows // block
    mine = pl.BlockSpec((block, width), lambda p, place: (place[0] * steps + p, 0))
    plain = pl.BlockSpec((block, width), lambda p, _: (p, 0))
    return pl.pallas_call(
        result_kernel,
        grid_spec=pltpu.PrefetchScalarGridSpec(
            num_scalar_prefetch=1,
            grid=(steps,),
            in_specs=[mine, mine, plain, whole(vectors.shape)],
            out_specs=plain,
        ),
        out_shape=jax.ShapeDtypeStruct((rows, width), LOW),
        compiler_params=settings(16),
        cost_estimate=cost(10 * rows * width, 320 * rows * width),
        name="result",
    )(place, resid, own, other, vectors)


def finish_kernel(own_ref, one_ref, two_ref, three_ref, proj_ref, out_ref):
    total = own_ref[...]
    for ref in (one_ref, two_ref, three_ref):
        total = total + ref[...].astype(jnp.float32)
    columns = out_ref.shape[1]
    for pair in range(columns // 128):
        for kind in range(3):
            start = (pair * 3 + kind) * 128
            proj_ref[kind, :, pair * 128 : pair * 128 + 128] = total[:, start : start + 128]
    out_ref[...] = total[:, 3 * columns :]


def finish(total, sent):
    rows, columns = sent[0].shape
    return pl.pallas_call(
        finish_kernel,
        grid=(1,),
        in_specs=[whole((rows, columns))] * 4,
        out_specs=[whole((3, rows, columns // 4)), whole((rows, columns // 4))],
        out_shape=[
            jax.ShapeDtypeStruct((3, rows, columns // 4), jnp.float32),
            jax.ShapeDtypeStruct((rows, columns // 4), jnp.float32),
        ],
        compiler_params=settings(16),
        cost_estimate=cost(4 * rows * columns, 14 * rows * columns),
        name="finish",
    )(total, *sent)


def pack_kernel(proj_ref, out_ref, up_ref, down_ref, *refs):
    singles, pair_ref, ups_ref = refs[:6], refs[6], refs[7]
    narrow_ref, wide_ref, rows_ref = refs[8:]
    columns = proj_ref.shape[2]
    for pair in range(columns // 128):
        for kind in range(3):
            start = (pair * 3 + kind) * 128
            narrow_ref[:, start : start + 128] = proj_ref[kind, :, pair * 128 : pair * 128 + 128]
    narrow_ref[:, 3 * columns : 4 * columns] = out_ref[...]
    rows_ref[...] = jnp.zeros_like(rows_ref)
    for index, ref in enumerate(singles):
        rows_ref[index : index + 1, 0:SLOT] = ref[...].astype(jnp.float32).reshape(1, SLOT)
    rows_ref[8:10, 0:SLOT] = pair_ref[...].astype(jnp.float32)
    ups = ups_ref[...].astype(jnp.float32).reshape(2, 128)
    for half in range(2):
        rows_ref[10 + 2 * half : 11 + 2 * half, :] = ups[half : half + 1, :]
        rows_ref[11 + 2 * half : 12 + 2 * half, :] = pltpu.roll(ups[half : half + 1, :], SLOT, 1)
    turned = jnp.transpose(rows_ref[...])[0:SLOT]
    narrow_ref[:, 4 * columns :] = jnp.concatenate(
        [turned, jnp.zeros((SLOT, 112), jnp.float32)], axis=1
    ).astype(LOW)
    hidden = up_ref.shape[1]
    wide_ref[:, :hidden] = up_ref[...]
    wide_ref[:, hidden:] = down_ref[...]


def pack_shards(proj, out, up, down, singles, pair, ups):
    rows, columns = out.shape
    return pl.pallas_call(
        pack_kernel,
        out_shape=[
            jax.ShapeDtypeStruct((rows, 4 * columns + 128), LOW),
            jax.ShapeDtypeStruct((rows, 2 * up.shape[1]), LOW),
        ],
        scratch_shapes=[pltpu.VMEM((16, 128), jnp.float32)],
        compiler_params=settings(56),
        cost_estimate=cost(0, 4 * rows * (4 * columns + 2 * up.shape[1])),
        name="pack",
    )(proj, out, up, down, *singles, pair, ups)


def after(value, *events):
    return lax.optimization_barrier((value,) + events)[0]


def dp_shift(value, ranks, dz, dy, dc):
    far, near = 4, ranks // 8

    def goes(rank):
        z, y, c = rank // (near * 2), rank // 2 % near, rank % 2
        return ((z + dz) % far * near + (y + dy) % near) * 2 + (c + dc) % 2

    return lax.ppermute(value, "dp", [(rank, goes(rank)) for rank in range(ranks)])


def dp_gather(shard, ranks, event):
    far = [shard] + [dp_shift(shard, ranks, k, 0, 0) for k in (1, 2, 3)]
    near = [dp_shift(piece, ranks, 0, 1, 0) for piece in (far[0], far[1], far[3])]
    second = dp_shift(after(far[2], event, near[2]), ranks, 0, 1, 0)
    pieces = far + [near[0], near[1], second, near[2]]
    return pieces + [dp_shift(piece, ranks, 0, 0, 1) for piece in pieces], pieces


def reduce_core(left, right, ranks):
    half = left.shape[0] // 2
    return dp_shift(matmul(left[half:], right).astype(LOW), ranks, 0, 0, 1)


def reduce_near(left, right, other):
    half = left.shape[0] // 2
    part = half // 2
    sent = matmul(left[part:half], right) + other[part:].astype(jnp.float32)
    return sent.astype(LOW)


def reduce_sum(left, right, other, arrived):
    part = left.shape[0] // 4
    total = matmul(left[:part], right) + other[:part].astype(jnp.float32)
    return total + arrived.astype(jnp.float32)


def far_send(total, ranks, wire=LOW):
    rows = total.shape[0] // 4
    low = total.astype(wire)
    return [dp_shift(low[k * rows : (k + 1) * rows], ranks, -k, 0, 0) for k in (1, 3, 2)]


def far_sum(total, sent):
    result = total[: total.shape[0] // 4]
    for value in sent:
        result = result + value.astype(jnp.float32)
    return result


def swap(value):
    return lax.ppermute(value, "tensor", [(0, 1), (1, 0)])


def paired(
    inputs,
    out_grad,
    parents,
    ln1_gain,
    ln1_bias,
    w_qkv,
    qv_bias,
    w_attn_out,
    attn_out_bias,
    ln2_gain,
    ln2_bias,
    w_up,
    up_bias,
    w_down,
    down_bias,
):
    ranks = lax.axis_size("dp")
    near = ranks // 8
    rank = lax.axis_index("dp")
    side = lax.axis_index("tensor")
    rows, width = inputs.shape
    shard = width // ranks
    heads_width = w_qkv.shape[2]
    pairs = heads_width // 128
    hidden = w_up.shape[1]
    scale = 1.0 / math.sqrt(width // HEADS)

    slots = jnp.arange(ranks, dtype=jnp.int32)
    core_step, near_step, far_step = slots // (ranks // 2), slots // 4 % near, slots % 4
    my_z, my_y, my_c = rank // (2 * near), rank // 2 % near, rank % 2
    source = ((my_z - far_step) % 4 * near + (my_y - near_step) % near) * 2 + (
        my_c + core_step
    ) % 2
    place = jnp.concatenate([jnp.stack([side, my_z, my_y, my_c]), source]).astype(jnp.int32)
    feature = jnp.repeat(source * shard, shard) + jnp.tile(
        jnp.arange(shard, dtype=jnp.int32), ranks
    )
    to_local = (jnp.arange(width, dtype=jnp.int32)[:, None] == feature[None, :]).astype(LOW)
    slot_of = (slots[:, None] == source[None, :]).astype(jnp.float32)

    singles = [ln1_gain, ln1_bias, attn_out_bias, ln2_gain, ln2_bias, down_bias]
    narrow_shard, wide_shard = pack_shards(
        w_qkv, w_attn_out.T, w_up, w_down.T, singles, qv_bias, up_bias
    )
    narrow, narrow_far = dp_gather(narrow_shard, ranks, place)
    inputs_other = swap(after(inputs, narrow_shard))
    grad_other = swap(after(out_grad, inputs_other))
    wide = lax.all_gather(
        after(wide_shard, inputs_other, *narrow_far[1:6], narrow_far[7]), "dp", axis=0, tiled=True
    )

    def in_order(own, other):
        return jnp.where(
            side == 0,
            jnp.concatenate([own, other], axis=0),
            jnp.concatenate([other, own], axis=0),
        )

    def to_slots(value):
        return lax.dot_general(
            to_local, value, (((0,), (1,)), ((), ())), preferred_element_type=jnp.float32
        ).astype(LOW)

    def other_rows(value):
        return lax.dynamic_slice_in_dim(value, (1 - side) * rows, rows, 0)

    early = front(place, inputs, inputs_other, narrow, pairs, scale)
    hidden_in, xhat, norm_one, out_full, qkv, attended, logs, share, proj_full = early[:9]
    vectors, hidden_bias = early[9:]
    cotangent = after(in_order(out_grad, grad_other), share)
    lefts = jnp.stack([cotangent, jnp.zeros_like(cotangent)])
    norm_slot = to_slots(after(norm_one, share))
    resid, lefts, rights, dnorm_share, dpre_sum = feed_product(
        place, hidden_in, share, swap(after(share, grad_other)), vectors, hidden_bias, lefts, wide
    )
    dnorm_other = swap(dnorm_share)
    wide_share = lax.dot_general(
        lefts,
        after(rights, dnorm_share),
        (((1,), (1,)), ((0,), (0,))),
        preferred_element_type=jnp.float32,
    ).astype(LOW)
    wide_grad = lax.psum_scatter(wide_share, "dp", scatter_dimension=1, tiled=True)
    mixed_share = contract_last(after(rights, wide_share)[0], wide[:, hidden:]).astype(LOW)
    dbranch, dattended, mid_sum = mid_product(
        after(resid, mixed_share, norm_slot), dnorm_share, dnorm_other, lefts, vectors, out_full
    )
    dqkv, dnorm_one, dqkv_sum, front_sum = back_product(
        xhat, qkv, dattended, logs, proj_full, scale
    )
    dqkv_sum = dqkv_sum.reshape(pairs, 3, 128)
    placed = [
        place_block(value, 2 * value.shape[0], side * value.shape[0]).reshape(ranks, -1)
        for value in (
            dqkv_sum[:, 0].reshape(heads_width),
            dqkv_sum[:, 2].reshape(heads_width),
            dpre_sum[0],
        )
    ]
    pack = jnp.concatenate([front_sum, mid_sum[:4]], axis=0)
    pack = pack.reshape(6, ranks, shard).transpose(1, 0, 2).reshape(ranks, -1)
    pack = lax.dot_general(
        slot_of,
        jnp.concatenate([pack] + placed, axis=1),
        (((0,), (0,)), ((), ())),
        precision=lax.Precision.HIGHEST,
        preferred_element_type=jnp.float32,
    )
    proj_core = reduce_core(norm_slot, dqkv, ranks)
    dbranch_slot = to_slots(after(dbranch, pack))
    pack_other = swap(pack)
    out_core = reduce_core(dbranch_slot, attended, ranks)
    slim_near = jnp.concatenate(
        [
            reduce_near(norm_slot, dqkv, proj_core),
            reduce_near(dbranch_slot, attended, out_core),
        ],
        axis=1,
    )
    pack = pack + after(pack_other, slim_near)
    pack = pack[: ranks // 2] + dp_shift(pack[ranks // 2 :], ranks, 0, 0, 1)
    slim_near, pack = lax.optimization_barrier((slim_near, pack))
    back_other = swap(other_rows(after(dnorm_one, pack)))
    pack_arrived = dp_shift(pack[ranks // 4 :], ranks, 0, 1, 0)
    slim_arrived = dp_shift(slim_near, ranks, 0, 1, 0)
    own_other = swap(other_rows(after(mixed_share, back_other)))
    slim_arrived, pack_arrived, back_other = lax.optimization_barrier(
        (slim_arrived, pack_arrived, back_other)
    )
    columns = 3 * heads_width
    slim_total, pack_total = lax.optimization_barrier(
        (
            jnp.concatenate(
                [
                    reduce_sum(norm_slot, dqkv, proj_core, slim_arrived[:, :columns]),
                    reduce_sum(dbranch_slot, attended, out_core, slim_arrived[:, columns:]),
                ],
                axis=1,
            ),
            pack[: ranks // 4] + pack_arrived,
        )
    )
    grad_back = wide_grad[0].T.astype(jnp.float32)
    grad_hidden = wide_grad[1].astype(jnp.float32)
    slim_sent = far_send(slim_total, ranks)
    pack = far_sum(pack_total, far_send(pack_total, ranks, jnp.float32)).reshape(-1)
    grad_proj, grad_out = finish(after(slim_total, grad_back, grad_hidden), slim_sent)
    grad_out = grad_out.T
    result = result_product(
        place, after(resid, slim_total), mixed_share, own_other, vectors
    )
    input_grad = last_product(
        place, inputs, dbranch, dnorm_one, after(back_other, slim_total), vectors
    )
    vector_grads = [pack[i * shard : (i + 1) * shard] for i in range(6)]
    return (
        result,
        input_grad,
        vector_grads[0],
        vector_grads[1],
        grad_proj,
        pack[6 * shard : 8 * shard].reshape(2, shard),
        grad_out,
        vector_grads[2],
        vector_grads[3],
        vector_grads[4],
        grad_hidden,
        pack[8 * shard :],
        grad_back,
        vector_grads[5],
    )


def local(*arrays):
    fits = lax.axis_size("tensor") == 2 and lax.axis_size("dp") == 16
    if fits and arrays[2].shape[1] == 3:
        return paired(*arrays)
    return generic(*arrays)


def solution(mesh):
    return jax.shard_map(
        local,
        mesh=mesh,
        in_specs=(
            P(("dp", "tensor"), None),
            P(("dp", "tensor"), None),
            P("dp", None),
            P("dp"),
            P("dp"),
            P(None, "dp", "tensor"),
            P(None, "dp"),
            P("tensor", "dp"),
            P("dp"),
            P("dp"),
            P("dp"),
            P("dp", "tensor"),
            P("dp"),
            P("tensor", "dp"),
            P("dp"),
        ),
        out_specs=(
            P(("dp", "tensor"), None),
            P(("dp", "tensor"), None),
            P("dp"),
            P("dp"),
            P(None, "dp", "tensor"),
            P(None, "dp"),
            P("tensor", "dp"),
            P("dp"),
            P("dp"),
            P("dp"),
            P("dp", "tensor"),
            P("dp"),
            P("tensor", "dp"),
            P("dp"),
        ),
        check_vma=False,
    )
```

```python
import functools
import math

import jax
import jax.numpy as jnp
from jax import lax
from jax.experimental import pallas as pl
from jax.experimental.pallas import tpu as pltpu
from jax.sharding import PartitionSpec as P

HEADS = 16
SEG = 256


epsilon = 1e-05
gelu_coef = 0.7978845608028654


def layer_norm(values, scales, shifts):
    centre = jnp.mean(values, axis=-1, keepdims=True)
    shifted = values - centre
    spread = jnp.mean(shifted * shifted, axis=-1, keepdims=True)
    return shifted * lax.rsqrt(spread + epsilon) * scales + shifts


def gelu_tanh(values):
    return (
        0.5 * values * (1.0 + jnp.tanh(gelu_coef * (values + 0.044715 * values * values * values)))
    )


def matmul(left, right):
    return jnp.dot(left, right, preferred_element_type=jnp.float32)


def contract_rows(left, right):
    return lax.dot_general(
        left, right, (((0,), (0,)), ((), ())), preferred_element_type=jnp.float32
    )


def contract_last(left, right):
    return lax.dot_general(
        left, right, (((1,), (1,)), ((), ())), preferred_element_type=jnp.float32
    )


def ancestors(parent_row, segment_count):
    labels = jnp.arange(segment_count, dtype=jnp.int32)
    links = ((parent_row[:, None] == labels[None, :]) & (labels[:, None] > 0)).astype(jnp.float32)
    identity = jnp.eye(segment_count, dtype=jnp.float32)

    def extend(turn, reached):
        grown = jnp.dot(
            links, reached, precision=lax.Precision.HIGHEST, preferred_element_type=jnp.float32
        )
        return jnp.minimum(identity + grown, 1.0)

    return lax.fori_loop(0, segment_count, extend, identity)


def tree_mask(reached, first_row, block_rows, length):
    query_pos = first_row + jnp.arange(block_rows, dtype=jnp.int32)
    key_pos = jnp.arange(length, dtype=jnp.int32)
    segment_count = reached.shape[0]
    onehot = (
        (query_pos // SEG)[:, None] == jnp.arange(segment_count, dtype=jnp.int32)[None, :]
    ).astype(jnp.float32)
    row_reach = jnp.dot(
        onehot, reached, precision=lax.Precision.HIGHEST, preferred_element_type=jnp.float32
    )
    spread_out = jnp.repeat(row_reach, SEG, axis=1)
    return (spread_out > 0.5) & (key_pos[None, :] <= query_pos[:, None])


def row_block(length):
    pieces = -(-length // 512)
    while length % pieces:
        pieces += 1
    return length // pieces


def place_block(local_vec, full_length, offset):
    empty_vec = jnp.zeros(local_vec.shape[:-1] + (full_length,), jnp.float32)
    return lax.dynamic_update_slice_in_dim(empty_vec, local_vec, offset, local_vec.ndim - 1)


def generic(
    inputs,
    out_grad,
    parents,
    ln1_gain,
    ln1_bias,
    w_qkv,
    qv_bias,
    w_attn_out,
    attn_out_bias,
    ln2_gain,
    ln2_bias,
    w_up,
    up_bias,
    w_down,
    down_bias,
):
    tensor_ranks = lax.axis_size("tensor")
    tensor_rank = lax.axis_index("tensor")
    rows_own = inputs.shape[0]
    length = rows_own * tensor_ranks
    model_width = inputs.shape[1]
    head_dim = model_width // HEADS
    local_width = w_qkv.shape[2]
    local_hidden = w_up.shape[1]
    heads_here = local_width // head_dim
    scale = 1.0 / math.sqrt(head_dim)
    gathered = (
        lax.all_gather(w_qkv, "dp", axis=1, tiled=True),
        lax.all_gather(w_attn_out, "dp", axis=1, tiled=True),
        lax.all_gather(w_up, "dp", axis=0, tiled=True),
        lax.all_gather(w_down, "dp", axis=1, tiled=True),
        lax.all_gather(ln1_gain, "dp", axis=0, tiled=True),
        lax.all_gather(ln1_bias, "dp", axis=0, tiled=True),
        lax.all_gather(qv_bias, "dp", axis=1, tiled=True),
        lax.all_gather(attn_out_bias, "dp", axis=0, tiled=True),
        lax.all_gather(ln2_gain, "dp", axis=0, tiled=True),
        lax.all_gather(ln2_bias, "dp", axis=0, tiled=True),
        lax.all_gather(up_bias, "dp", axis=0, tiled=True),
        lax.all_gather(down_bias, "dp", axis=0, tiled=True),
    )
    proj_full, out_full, hidden_full, back_full = (
        gathered[0],
        gathered[1],
        gathered[2],
        gathered[3],
    )
    gain_one = gathered[4].astype(jnp.float32)
    shift_one = gathered[5].astype(jnp.float32)
    proj_bias = lax.dynamic_slice_in_dim(
        gathered[6].astype(jnp.float32), tensor_rank * local_width, local_width, 1
    )
    out_bias = gathered[7].astype(jnp.float32)
    gain_two = gathered[8].astype(jnp.float32)
    shift_two = gathered[9].astype(jnp.float32)
    hidden_bias_full = gathered[10].astype(jnp.float32)
    back_bias = gathered[11].astype(jnp.float32)
    full_hidden = hidden_bias_full.shape[0]
    hidden_in = inputs.astype(jnp.float32)
    norm_one, ln1_pull = jax.vjp(layer_norm, hidden_in, gain_one, shift_one)
    norm_one_all = lax.all_gather(norm_one.astype(jnp.bfloat16), "tensor", axis=0, tiled=True)
    queries = (matmul(norm_one_all, proj_full[0]) + proj_bias[0]).astype(jnp.bfloat16)
    keys_low = matmul(norm_one_all, proj_full[1]).astype(jnp.bfloat16)
    values_low = (matmul(norm_one_all, proj_full[2]) + proj_bias[1]).astype(jnp.bfloat16)
    reached = ancestors(parents[0], length // SEG)
    block_rows = row_block(length)
    num_blocks = length // block_rows
    starts = jnp.arange(num_blocks, dtype=jnp.int32) * block_rows
    query_blocks = queries.reshape(num_blocks, block_rows, heads_here, head_dim)
    key_heads = keys_low.reshape(length, heads_here, head_dim)
    value_heads = values_low.reshape(length, heads_here, head_dim)

    def block_scores(query_block, first_row):
        scores = (
            jnp.einsum("qhd,khd->hqk", query_block, key_heads, preferred_element_type=jnp.float32)
            * scale
        )
        allowed = tree_mask(reached, first_row, block_rows, length)
        return jnp.where(allowed[None], scores, -1e30)

    def forward_block(element):
        query_block, first_row = element
        scores = block_scores(query_block, first_row)
        top_score = jnp.max(scores, axis=-1, keepdims=True)
        expo = jnp.exp(scores - top_score)
        totals = jnp.sum(expo, axis=-1, keepdims=True)
        probs = (expo / totals).astype(jnp.bfloat16)
        attended_block = jnp.einsum(
            "hqk,khd->qhd", probs, value_heads, preferred_element_type=jnp.float32
        )
        return (attended_block, (top_score + jnp.log(totals))[..., 0])

    attended_blocks, log_totals = lax.map(forward_block, (query_blocks, starts))
    attended = attended_blocks.reshape(length, local_width).astype(jnp.bfloat16)
    branch = (
        lax.psum_scatter(matmul(attended, out_full), "tensor", scatter_dimension=0, tiled=True)
        + out_bias
    )
    resid = hidden_in + branch
    norm_two, ln2_pull = jax.vjp(layer_norm, resid, gain_two, shift_two)
    norm_two_low = norm_two.astype(jnp.bfloat16)
    grad_back_bias = jnp.sum(out_grad.astype(jnp.float32), axis=0)
    norm_two_all = lax.all_gather(norm_two_low, "tensor", axis=0, tiled=True)
    hidden_slice = lax.dynamic_slice_in_dim(
        hidden_bias_full, tensor_rank * local_hidden, local_hidden, 0
    )
    pre = matmul(norm_two_all, hidden_full) + hidden_slice
    act, gelu_pull = jax.vjp(gelu_tanh, pre)
    act_low = act.astype(jnp.bfloat16)
    mixed = (
        lax.psum_scatter(
            matmul(act_low, back_full).astype(jnp.bfloat16),
            "tensor",
            scatter_dimension=0,
            tiled=True,
        ).astype(jnp.float32)
        + back_bias
    )
    cotangent_all = lax.all_gather(out_grad, "tensor", axis=0, tiled=True)
    grad_back = contract_rows(act_low, cotangent_all)
    (dpre,) = gelu_pull(contract_last(cotangent_all, back_full))
    dpre_low = dpre.astype(jnp.bfloat16)
    grad_hidden = contract_rows(norm_two_all, dpre_low)
    grad_hidden_bias = place_block(
        jnp.sum(dpre_low.astype(jnp.float32), axis=0), full_hidden, tensor_rank * local_hidden
    )
    dnorm_two = lax.psum_scatter(
        contract_last(dpre_low, hidden_full), "tensor", scatter_dimension=0, tiled=True
    )
    result = (resid + mixed).astype(jnp.bfloat16)
    dresid_part, grad_gain_two, grad_shift_two = ln2_pull(dnorm_two)
    dresid = out_grad.astype(jnp.float32) + dresid_part
    dbranch = dresid.astype(jnp.bfloat16)
    grad_out_bias = jnp.sum(dbranch.astype(jnp.float32), axis=0)
    dbranch_all = lax.all_gather(dbranch, "tensor", axis=0, tiled=True)
    grad_out = contract_rows(attended, dbranch_all)
    dattended = contract_last(dbranch_all, out_full).astype(jnp.bfloat16)
    dattended_blocks = dattended.reshape(num_blocks, block_rows, heads_here, head_dim)

    def backward_block(carry, element):
        dkey_acc, dvalue_acc = carry
        query_block, dattended_block, log_block, first_row = element
        scores = block_scores(query_block, first_row)
        probs = jnp.exp(scores - log_block[..., None])
        dvalue_acc = dvalue_acc + jnp.einsum(
            "hqk,qhd->khd",
            probs.astype(jnp.bfloat16),
            dattended_block,
            preferred_element_type=jnp.float32,
        )
        dprobs = jnp.einsum(
            "qhd,khd->hqk", dattended_block, value_heads, preferred_element_type=jnp.float32
        )
        dscores = probs * (dprobs - jnp.sum(dprobs * probs, axis=-1, keepdims=True))
        dscores_low = dscores.astype(jnp.bfloat16)
        dquery_block = (
            jnp.einsum("hqk,khd->qhd", dscores_low, key_heads, preferred_element_type=jnp.float32)
            * scale
        )
        dkey_acc = (
            dkey_acc
            + jnp.einsum(
                "hqk,qhd->khd", dscores_low, query_block, preferred_element_type=jnp.float32
            )
            * scale
        )
        return ((dkey_acc, dvalue_acc), dquery_block)

    zero_heads = jnp.zeros((length, heads_here, head_dim), jnp.float32)
    (dkey_acc, dvalue_acc), dquery_blocks = lax.scan(
        backward_block,
        (zero_heads, zero_heads),
        (query_blocks, dattended_blocks, log_totals, starts),
    )
    dqueries = dquery_blocks.reshape(length, local_width).astype(jnp.bfloat16)
    dkeys = dkey_acc.reshape(length, local_width).astype(jnp.bfloat16)
    dvalues = dvalue_acc.reshape(length, local_width).astype(jnp.bfloat16)
    grad_proj = jnp.stack(
        [
            contract_rows(norm_one_all, dqueries),
            contract_rows(norm_one_all, dkeys),
            contract_rows(norm_one_all, dvalues),
        ]
    )
    local_bias_grad = jnp.stack(
        [
            jnp.sum(dqueries.astype(jnp.float32), axis=0),
            jnp.sum(dvalues.astype(jnp.float32), axis=0),
        ]
    )
    grad_proj_bias = place_block(local_bias_grad, model_width, tensor_rank * local_width)
    dnorm_one = lax.psum_scatter(
        (
            contract_last(dqueries, proj_full[0])
            + contract_last(dkeys, proj_full[1])
            + contract_last(dvalues, proj_full[2])
        ).astype(jnp.bfloat16),
        "tensor",
        scatter_dimension=0,
        tiled=True,
    ).astype(jnp.float32)
    dinput_part, grad_gain_one, grad_shift_one = ln1_pull(dnorm_one)
    input_grad = dresid + dinput_part
    summed = (
        lax.psum_scatter(grad_proj, "dp", scatter_dimension=1, tiled=True),
        lax.psum_scatter(grad_out, "dp", scatter_dimension=1, tiled=True),
        lax.psum_scatter(grad_hidden, "dp", scatter_dimension=0, tiled=True),
        lax.psum_scatter(grad_back, "dp", scatter_dimension=1, tiled=True),
        lax.psum_scatter(grad_gain_one, "dp", scatter_dimension=0, tiled=True),
        lax.psum_scatter(grad_shift_one, "dp", scatter_dimension=0, tiled=True),
        lax.psum_scatter(grad_proj_bias, "dp", scatter_dimension=1, tiled=True),
        lax.psum_scatter(grad_out_bias, "dp", scatter_dimension=0, tiled=True),
        lax.psum_scatter(grad_gain_two, "dp", scatter_dimension=0, tiled=True),
        lax.psum_scatter(grad_shift_two, "dp", scatter_dimension=0, tiled=True),
        lax.psum_scatter(grad_hidden_bias, "dp", scatter_dimension=0, tiled=True),
        lax.psum_scatter(grad_back_bias, "dp", scatter_dimension=0, tiled=True),
    )
    vectors = lax.psum(
        (summed[4], summed[5], summed[6], summed[7], summed[8], summed[9], summed[10], summed[11]),
        "tensor",
    )
    return (
        result,
        input_grad,
        vectors[0],
        vectors[1],
        summed[0],
        vectors[2],
        summed[1],
        vectors[3],
        vectors[4],
        vectors[5],
        summed[2],
        vectors[6],
        summed[3],
        vectors[7],
    )


LOW = jnp.bfloat16
SLOT = 64


def settings(mib):
    return pltpu.CompilerParams(vmem_limit_bytes=mib * 2**20)


def cost(flops, moved, exps=0):
    return pl.CostEstimate(
        flops=int(flops), bytes_accessed=int(moved), transcendentals=int(exps)
    )


def whole(shape):
    return pl.BlockSpec(shape, lambda *_: (0,) * len(shape))


def piece_specs(pieces, block, first=0):
    return [
        pl.BlockSpec((piece.shape[0], block), lambda p, *_: (0, first + p)) for piece in pieces
    ]


def fixed_specs(pieces, block, index):
    return [pl.BlockSpec((piece.shape[0], block), lambda *_: (0, index)) for piece in pieces]


def fill_natural(place_ref, scratch, refs):
    for slot, ref in enumerate(refs):
        start = pl.multiple_of(place_ref[4 + slot] * SLOT, SLOT)
        scratch[pl.ds(start, SLOT), :] = ref[...]


def row_stats(rows):
    centre = jnp.mean(rows, axis=-1, keepdims=True)
    shifted = rows - centre
    spread = jnp.mean(shifted * shifted, axis=-1, keepdims=True)
    inverse = lax.rsqrt(spread + epsilon)
    return shifted * inverse, inverse


def norm_back(dnorm, xhat, inverse, gain):
    scaled = dnorm * gain
    return inverse * (
        scaled
        - jnp.mean(scaled, axis=-1, keepdims=True)
        - xhat * jnp.mean(scaled * xhat, axis=-1, keepdims=True)
    )


def attend_pair(qkv_ref, out_ref, log_ref, scale):
    length = qkv_ref.shape[0]
    lane = lax.broadcasted_iota(jnp.int32, (SEG, 128), 1)
    reach = lax.broadcasted_iota(jnp.int32, (SEG, SEG), 0) <= lax.broadcasted_iota(
        jnp.int32, (SEG, SEG), 1
    )
    value_t = jnp.transpose(qkv_ref[:, 256:384])
    for seg in range(length // SEG):
        before = seg * SEG
        rows = slice(before, before + SEG)
        query = qkv_ref[rows, 0:128] * scale
        parts = []
        drawn = []
        for head in range(2):
            mine = jnp.where(lane // 64 == head, query, jnp.zeros_like(query))
            scores = contract_last(qkv_ref[rows, 128:256], mine)
            early = contract_last(qkv_ref[0:before, 128:256], mine) if seg > 0 else None
            drawn.append((jnp.where(reach, scores, -1e30), early))
        for head in range(2):
            lanes = slice(head * 64, head * 64 + 64)
            scores, early = drawn[head]
            top = jnp.max(scores, axis=0, keepdims=True)
            if seg > 0:
                top = jnp.maximum(top, jnp.max(early, axis=0, keepdims=True))
            expo = jnp.exp(scores - top)
            total = jnp.sum(expo, axis=0, keepdims=True)
            mixed = matmul(value_t[lanes, rows], expo.astype(LOW))
            if seg > 0:
                expo = jnp.exp(early - top)
                total = total + jnp.sum(expo, axis=0, keepdims=True)
                mixed = mixed + matmul(value_t[lanes, 0:before], expo.astype(LOW))
            parts.append(mixed / total)
            log_ref[0, head : head + 1, rows] = top + jnp.log(total)
        out_ref[rows, :] = jnp.transpose(jnp.concatenate(parts, axis=0)).astype(LOW)


def read_vectors(vec_ref, bias_ref, hidden_ref, joined_ref):
    turned = jnp.transpose(joined_ref[...]).astype(jnp.float32)
    vec_ref[...] = turned[0:8]
    bias_ref[...] = turned[8:16]
    lane = lax.broadcasted_iota(jnp.int32, (1, 128), 1)
    for pair in range(bias_ref.shape[1] // 128):
        rows = [turned[10 + q : 11 + q, pair * 128 : pair * 128 + 128] for q in range(4)]
        flipped = [pltpu.roll(row, 64, 1) for row in rows]
        for q in (0, 2):
            start = pair * 512 + q * 64
            hidden_ref[:, start : start + 128] = jnp.where(lane < 64, rows[q], flipped[q + 1])
            hidden_ref[:, start + 256 : start + 384] = jnp.where(
                lane < 64, flipped[q], rows[q + 1]
            )


def front_kernel(place_ref, own_ref, other_ref, *refs, scale, count):
    pieces, outs, vecs = (refs[i * count : (i + 1) * count] for i in range(3))
    kept, refs = refs[3 * count : 3 * count + 4], refs[3 * count + 4 :]
    qkv_ref, att_ref, log_ref, share_ref, weight_ref, vec_ref, hidden_ref = refs[:7]
    x_ref, xhat_ref, norm_ref, out_ref, joined_ref, bias_ref, lines_ref, sem = refs[7:]
    pairs = pl.num_programs(0)
    copies = [
        pltpu.make_async_copy(source, target, sem.at[index])
        for index, (source, target) in enumerate(zip((x_ref, xhat_ref, norm_ref, out_ref), kept))
    ]
    rows_own = own_ref.shape[0]
    step = pl.program_id(0)

    @pl.when(step == 0)
    def _():
        fill_natural(place_ref, lines_ref, vecs)
        read_vectors(vec_ref, bias_ref, hidden_ref, lines_ref)
        for half, ref in ((place_ref[0], own_ref), (1 - place_ref[0], other_ref)):
            for start in range(0, rows_own, 128):
                rows = pl.ds(pl.multiple_of(half * rows_own + start, 128), 128)
                x = ref[start : start + 128, :]
                xhat, _ = row_stats(x.astype(jnp.float32))
                x_ref[rows, :] = x
                xhat_ref[rows, :] = xhat.astype(LOW)
                norm_ref[rows, :] = (xhat * vec_ref[0:1, :] + vec_ref[1:2, :]).astype(LOW)
        fill_natural(place_ref, out_ref, outs)
        for copy in copies:
            copy.start()

    fill_natural(place_ref, weight_ref, pieces)
    mine = pl.ds(pl.multiple_of((place_ref[0] * pairs + step) * 128, 128), 128)
    bias = jnp.concatenate(
        [bias_ref[0:1, mine], jnp.zeros((1, 128), jnp.float32), bias_ref[1:2, mine]], axis=1
    )
    qkv_ref[...] = (matmul(norm_ref[...], weight_ref[...]) + bias).astype(LOW)
    attend_pair(qkv_ref, att_ref, log_ref, scale)
    joined_ref[:, pl.ds(pl.multiple_of(step * 128, 128), 128)] = att_ref[...]

    @pl.when(step == pl.num_programs(0) - 1)
    def _():
        share_ref[...] = contract_last(joined_ref[...], out_ref[...]).astype(LOW)
        for copy in copies:
            copy.wait()


def front(place, own, other, pieces, pairs, scale):
    length, width = 2 * own.shape[0], own.shape[1]
    once = pl.Buffered(1)
    square = pl.BlockSpec((length, width), lambda *_: (0, 0), pipeline_mode=once)
    half = pl.BlockSpec(own.shape, lambda *_: (0, 0), pipeline_mode=once)
    return pl.pallas_call(
        functools.partial(front_kernel, scale=scale, count=len(pieces)),
        grid_spec=pltpu.PrefetchScalarGridSpec(
            num_scalar_prefetch=1,
            grid=(pairs,),
            in_specs=[
                half,
                half,
            ]
            + piece_specs(pieces, 384)
            + fixed_specs(pieces, pairs * 128, 3)
            + fixed_specs(pieces, 128, pairs * 4),
            out_specs=[pl.BlockSpec(memory_space=pl.ANY)] * 4
            + [
                pl.BlockSpec((length, 384), lambda p, _: (0, p)),
                pl.BlockSpec((length, 128), lambda p, _: (0, p)),
                pl.BlockSpec((1, 8, length), lambda p, _: (p, 0, 0)),
                square,
                pl.BlockSpec((width, 384), lambda p, _: (0, p)),
                whole((8, width)),
                whole((1, 4 * width)),
            ],
            scratch_shapes=[
                pltpu.VMEM((length, width), LOW),
                pltpu.VMEM((length, width), LOW),
                pltpu.VMEM((length, width), LOW),
                pltpu.VMEM((width, pairs * 128), LOW),
                pltpu.VMEM((length, pairs * 128), LOW),
                pltpu.VMEM((8, width), jnp.float32),
                pltpu.VMEM((width, 128), LOW),
                pltpu.SemaphoreType.DMA((4,)),
            ],
        ),
        out_shape=[
            jax.ShapeDtypeStruct((length, width), LOW),
            jax.ShapeDtypeStruct((length, width), LOW),
            jax.ShapeDtypeStruct((length, width), LOW),
            jax.ShapeDtypeStruct((width, pairs * 128), LOW),
            jax.ShapeDtypeStruct((length, pairs * 384), LOW),
            jax.ShapeDtypeStruct((length, pairs * 128), LOW),
            jax.ShapeDtypeStruct((pairs, 8, length), jnp.float32),
            jax.ShapeDtypeStruct((length, width), LOW),
            jax.ShapeDtypeStruct((width, pairs * 384), LOW),
            jax.ShapeDtypeStruct((8, width), jnp.float32),
            jax.ShapeDtypeStruct((1, 4 * width), jnp.float32),
        ],
        compiler_params=settings(56),
        cost_estimate=cost(2 * length * width * pairs * 384 * 4, 12 * length * width),
        name="front",
    )(place, own, other, *pieces, *pieces, *pieces)


def feed_kernel(
    place_ref,
    x_ref,
    own_ref,
    other_ref,
    vec_ref,
    bias_ref,
    grad_ref,
    pair_ref,
    resid_ref,
    left_ref,
    right_ref,
    dnorm_ref,
    sum_ref,
    up_ref,
    down_ref,
    sem,
):
    first = pl.program_id(0) == 0
    hidden = up_ref.shape[1]

    def fetch(start):
        part = pl.ds(start, 512)
        index = start // 512
        return (
            pltpu.make_async_copy(pair_ref.at[:, part], up_ref.at[:, part], sem.at[0, index]),
            pltpu.make_async_copy(
                pair_ref.at[:, pl.ds(hidden + start, 512)], down_ref.at[:, part], sem.at[1, index]
            ),
        )

    @pl.when(first)
    def _():
        for start in range(0, hidden, 512):
            for copy in fetch(start):
                copy.start()
        sum_ref[...] = jnp.zeros_like(sum_ref)

    branch = own_ref[...].astype(jnp.float32) + other_ref[...].astype(jnp.float32)
    resid = x_ref[...].astype(jnp.float32) + (branch + vec_ref[2:3, :])
    resid_ref[...] = resid.astype(LOW)
    xhat, _ = row_stats(resid)
    norm = (xhat * vec_ref[3:4, :] + vec_ref[4:5, :]).astype(LOW)
    left_ref[0] = norm
    for start in range(0, hidden, 512):
        columns = slice(start, start + 512)

        @pl.when(first)
        def _(start=start):
            for copy in fetch(start):
                copy.wait()

        pre = matmul(norm, up_ref[:, columns]) + bias_ref[:, columns]
        square = pre * pre
        bent = jnp.tanh(pre * (square * (0.044715 * gelu_coef) + gelu_coef))
        half = 0.5 * bent + 0.5
        act = pre * half
        right_ref[0, :, columns] = act.astype(LOW)
        slope = half + act * (1.0 - bent) * (square * (3 * 0.044715 * gelu_coef) + gelu_coef)
        dpre = (matmul(grad_ref[0], down_ref[:, columns]) * slope).astype(LOW)
        right_ref[1, :, columns] = dpre
        total = jnp.sum(dpre.astype(jnp.float32), axis=0, keepdims=True)
        sum_ref[:, columns] += jnp.broadcast_to(total, (8, 512))
    dnorm_ref[...] = contract_last(right_ref[1], up_ref[...]).astype(LOW)


def feed_product(place, x, own, other, vectors, bias, lefts, pair, block=SEG):
    length, width = x.shape
    hidden = pair.shape[1] // 2
    rows = pl.BlockSpec((block, width), lambda p, _: (p, 0))
    return pl.pallas_call(
        feed_kernel,
        grid_spec=pltpu.PrefetchScalarGridSpec(
            num_scalar_prefetch=1,
            grid=(length // block,),
            in_specs=[rows] * 3
            + [
                whole(vectors.shape),
                pl.BlockSpec((1, hidden), lambda p, place: (0, place[0])),
                pl.BlockSpec((1, block, width), lambda p, _: (0, p, 0)),
                pl.BlockSpec(memory_space=pl.ANY),
            ],
            out_specs=[
                rows,
                pl.BlockSpec((1, block, width), lambda p, _: (1, p, 0)),
                pl.BlockSpec((2, block, hidden), lambda p, _: (0, p, 0)),
                rows,
                whole((8, hidden)),
            ],
            scratch_shapes=[
                pltpu.VMEM((width, hidden), LOW),
                pltpu.VMEM((width, hidden), LOW),
                pltpu.SemaphoreType.DMA((2, hidden // 512)),
            ],
        ),
        out_shape=[
            jax.ShapeDtypeStruct((length, width), LOW),
            jax.ShapeDtypeStruct((2, length, width), LOW),
            jax.ShapeDtypeStruct((2, length, hidden), LOW),
            jax.ShapeDtypeStruct((length, width), LOW),
            jax.ShapeDtypeStruct((8, hidden), jnp.float32),
        ],
        input_output_aliases={6: 1},
        compiler_params=settings(56),
        cost_estimate=cost(9 * length * width * hidden, 40 * length * width),
        name="feed",
    )(place, x, own, other, vectors, bias, lefts, pair)


def mid_kernel(
    resid_ref, own_ref, other_ref, grad_ref, vec_ref, weight_ref, dbranch_ref, datt_ref, sum_ref
):
    @pl.when(pl.program_id(0) == 0)
    def _():
        sum_ref[...] = jnp.zeros_like(sum_ref)

    dnorm = own_ref[...].astype(jnp.float32) + other_ref[...].astype(jnp.float32)
    grad = grad_ref[0].astype(jnp.float32)
    xhat, inverse = row_stats(resid_ref[...].astype(jnp.float32))
    dresid = grad + norm_back(dnorm, xhat, inverse, vec_ref[3:4, :])
    dbranch = dresid.astype(LOW)
    dbranch_ref[...] = dbranch
    datt_ref[...] = matmul(dbranch, weight_ref[...]).astype(LOW)
    for row, value in enumerate((dbranch.astype(jnp.float32), dnorm * xhat, dnorm, grad)):
        sum_ref[row : row + 1, :] += 0.5 * jnp.sum(value, axis=0, keepdims=True)


def mid_product(resid, own, other, lefts, vectors, weight, block=SEG):
    length, width = resid.shape
    inner = weight.shape[1]
    rows = pl.BlockSpec((block, width), lambda p: (p, 0))
    return pl.pallas_call(
        mid_kernel,
        grid=(length // block,),
        in_specs=[rows] * 3
        + [
            pl.BlockSpec((1, block, width), lambda p: (0, p, 0)),
            whole(vectors.shape),
            whole(weight.shape),
        ],
        out_specs=[rows, pl.BlockSpec((block, inner), lambda p: (p, 0)), whole((8, width))],
        out_shape=[
            jax.ShapeDtypeStruct((length, width), LOW),
            jax.ShapeDtypeStruct((length, inner), LOW),
            jax.ShapeDtypeStruct((8, width), jnp.float32),
        ],
        compiler_params=settings(56),
        cost_estimate=cost(2 * length * width * inner * 16, 16 * length * width),
        name="mid",
    )(resid, own, other, lefts, vectors, weight)


def attend_back_pair(qkv_ref, grad_ref, log_ref, out_ref, dkey_ref, dvalue_ref, scale):
    length = qkv_ref.shape[0]
    lane = lax.broadcasted_iota(jnp.int32, (SEG, 128), 1)
    reach = lax.broadcasted_iota(jnp.int32, (SEG, SEG), 0) <= lax.broadcasted_iota(
        jnp.int32, (SEG, SEG), 1
    )
    key_t = jnp.transpose(qkv_ref[:, 128:256])
    for seg in reversed(range(length // SEG)):
        before = seg * SEG
        rows = slice(before, before + SEG)
        spans = [rows] if seg == 0 else [rows, slice(0, before)]
        query = qkv_ref[rows, 0:128] * scale
        grad = grad_ref[rows, :]
        parts = []
        dkeys = [None] * len(spans)
        dvalues = [None] * len(spans)
        drawn = []
        for head in range(2):
            here = lane // 64 == head
            query_mine = jnp.where(here, query, jnp.zeros_like(query))
            grad_mine = jnp.where(here, grad, jnp.zeros_like(grad))
            scores = [contract_last(qkv_ref[span, 128:256], query_mine) for span in spans]
            scores[0] = jnp.where(reach, scores[0], -1e30)
            dprobs = [contract_last(qkv_ref[span, 256:384], grad_mine) for span in spans]
            drawn.append((query_mine, grad_mine, scores, dprobs))
        for head in range(2):
            lanes = slice(head * 64, head * 64 + 64)
            query_mine, grad_mine, scores, dprobs = drawn[head]
            log_row = log_ref[0, head : head + 1, rows]
            probs = []
            mean = None
            for index in range(len(spans)):
                prob = jnp.exp(scores[index] - log_row)
                share = jnp.sum(prob * dprobs[index], axis=0, keepdims=True)
                mean = share if mean is None else mean + share
                probs.append(prob)
            part = None
            for index, span in enumerate(spans):
                dscores = (probs[index] * (dprobs[index] - mean)).astype(LOW)
                dvalue = matmul(probs[index].astype(LOW), grad_mine)
                dkey = matmul(dscores, query_mine)
                piece = matmul(key_t[lanes, span], dscores)
                part = piece if part is None else part + piece
                dkeys[index] = dkey if head == 0 else dkeys[index] + dkey
                dvalues[index] = dvalue if head == 0 else dvalues[index] + dvalue
            parts.append(part * scale)
        for index, span in enumerate(spans):
            if seg == length // SEG - 1:
                dkey_ref[span, :] = dkeys[index]
                dvalue_ref[span, :] = dvalues[index]
            else:
                dkey_ref[span, :] += dkeys[index]
                dvalue_ref[span, :] += dvalues[index]
        out_ref[rows, 0:128] = jnp.transpose(jnp.concatenate(parts, axis=0)).astype(LOW)
    out_ref[:, 128:256] = dkey_ref[...].astype(LOW)
    out_ref[:, 256:384] = dvalue_ref[...].astype(LOW)


def back_kernel(
    xhat_all_ref,
    qkv_ref,
    grad_ref,
    log_ref,
    weight_ref,
    dqkv_ref,
    dnorm_ref,
    sum_ref,
    vec_ref,
    dkey_ref,
    dvalue_ref,
    acc_ref,
    xhat_ref,
    sem,
    *,
    scale,
):
    step = pl.program_id(0)
    fetch = pltpu.make_async_copy(xhat_all_ref, xhat_ref, sem.at[0])

    @pl.when(step == 0)
    def _():
        fetch.start()

    attend_back_pair(qkv_ref, grad_ref, log_ref, dqkv_ref, dkey_ref, dvalue_ref, scale)
    dnorm = contract_last(dqkv_ref[...], weight_ref[...])
    sum_ref[0] = jnp.sum(dqkv_ref[...].astype(jnp.float32), axis=0, keepdims=True)

    @pl.when(step == 0)
    def _():
        acc_ref[...] = dnorm

    @pl.when((step > 0) & (step < pl.num_programs(0) - 1))
    def _():
        acc_ref[...] += dnorm

    @pl.when(step == pl.num_programs(0) - 1)
    def _():
        fetch.wait()
        total = acc_ref[...] + dnorm
        dnorm_ref[...] = total.astype(LOW)
        vec_ref[0:1, :] = jnp.sum(total * xhat_ref[...].astype(jnp.float32), axis=0, keepdims=True)
        vec_ref[1:2, :] = jnp.sum(total, axis=0, keepdims=True)


def back_product(xhat, qkv, grad, logs, weight, scale):
    length, columns = qkv.shape
    width = weight.shape[0]
    pairs = columns // 384
    once = pl.Buffered(1)
    square = pl.BlockSpec((length, width), lambda p: (0, 0), pipeline_mode=once)
    return pl.pallas_call(
        functools.partial(back_kernel, scale=scale),
        grid=(pairs,),
        in_specs=[
            pl.BlockSpec(memory_space=pl.ANY),
            pl.BlockSpec((length, 384), lambda p: (0, p)),
            pl.BlockSpec((length, 128), lambda p: (0, p)),
            pl.BlockSpec((1, 8, length), lambda p: (p, 0, 0)),
            pl.BlockSpec((width, 384), lambda p: (0, p)),
        ],
        out_specs=[
            pl.BlockSpec((length, 384), lambda p: (0, p)),
            square,
            pl.BlockSpec((1, 1, 384), lambda p: (p, 0, 0)),
            whole((2, width)),
        ],
        out_shape=[
            jax.ShapeDtypeStruct((length, columns), LOW),
            jax.ShapeDtypeStruct((length, width), LOW),
            jax.ShapeDtypeStruct((pairs, 1, 384), jnp.float32),
            jax.ShapeDtypeStruct((2, width), jnp.float32),
        ],
        scratch_shapes=[
            pltpu.VMEM((length, 128), jnp.float32),
            pltpu.VMEM((length, 128), jnp.float32),
            pltpu.VMEM((length, width), jnp.float32),
            pltpu.VMEM((length, width), LOW),
            pltpu.SemaphoreType.DMA((1,)),
        ],
        compiler_params=settings(56),
        cost_estimate=cost(2 * length * width * columns * 48, 12 * length * width),
        name="back",
    )(xhat, qkv, grad, logs, weight)


def last_kernel(place_ref, x_ref, dbranch_ref, own_ref, other_ref, vec_ref, out_ref):
    dnorm = own_ref[...].astype(jnp.float32) + other_ref[...].astype(jnp.float32)
    xhat, inverse = row_stats(x_ref[...].astype(jnp.float32))
    back = norm_back(dnorm, xhat, inverse, vec_ref[0:1, :])
    out_ref[...] = dbranch_ref[...].astype(jnp.float32) + back


def last_product(place, x, dbranch, own, other, vectors):
    rows, width = other.shape
    block = 128
    steps = rows // block
    mine = pl.BlockSpec((block, width), lambda p, place: (place[0] * steps + p, 0))
    plain = pl.BlockSpec((block, width), lambda p, _: (p, 0))
    return pl.pallas_call(
        last_kernel,
        grid_spec=pltpu.PrefetchScalarGridSpec(
            num_scalar_prefetch=1,
            grid=(steps,),
            in_specs=[plain, mine, mine, plain, whole(vectors.shape)],
            out_specs=plain,
        ),
        out_shape=jax.ShapeDtypeStruct((rows, width), jnp.float32),
        compiler_params=settings(16),
        cost_estimate=cost(40 * rows * width, 320 * rows * width),
        name="last",
    )(place, x, dbranch, own, other, vectors)


def result_kernel(place_ref, resid_ref, own_ref, other_ref, vec_ref, out_ref):
    mixed = own_ref[...].astype(jnp.float32) + other_ref[...].astype(jnp.float32)
    total = resid_ref[...].astype(jnp.float32) + mixed + vec_ref[5:6, :]
    out_ref[...] = total.astype(LOW)


def result_product(place, resid, own, other, vectors):
    rows, width = other.shape
    block = 128
    steps = rows // block
    mine = pl.BlockSpec((block, width), lambda p, place: (place[0] * steps + p, 0))
    plain = pl.BlockSpec((block, width), lambda p, _: (p, 0))
    return pl.pallas_call(
        result_kernel,
        grid_spec=pltpu.PrefetchScalarGridSpec(
            num_scalar_prefetch=1,
            grid=(steps,),
            in_specs=[mine, mine, plain, whole(vectors.shape)],
            out_specs=plain,
        ),
        out_shape=jax.ShapeDtypeStruct((rows, width), LOW),
        compiler_params=settings(16),
        cost_estimate=cost(10 * rows * width, 320 * rows * width),
        name="result",
    )(place, resid, own, other, vectors)


def finish_kernel(own_ref, one_ref, two_ref, three_ref, proj_ref):
    total = own_ref[...]
    for ref in (one_ref, two_ref, three_ref):
        total = total + ref[...].astype(jnp.float32)
    for pair in range(proj_ref.shape[2] // 128):
        for kind in range(3):
            start = (pair * 3 + kind) * 128
            proj_ref[kind, :, pair * 128 : pair * 128 + 128] = total[:, start : start + 128]


def finish(total, sent):
    rows, columns = sent[0].shape
    return pl.pallas_call(
        finish_kernel,
        grid=(1,),
        in_specs=[whole((rows, columns))] * 4,
        out_specs=whole((3, rows, columns // 3)),
        out_shape=jax.ShapeDtypeStruct((3, rows, columns // 3), jnp.float32),
        compiler_params=settings(16),
        cost_estimate=cost(4 * rows * columns, 14 * rows * columns),
        name="finish",
    )(total, *sent)


def pack_kernel(proj_ref, out_ref, up_ref, down_ref, *refs):
    singles, pair_ref, ups_ref = refs[:6], refs[6], refs[7]
    narrow_ref, wide_ref, rows_ref = refs[8:]
    columns = proj_ref.shape[2]
    for pair in range(columns // 128):
        for kind in range(3):
            start = (pair * 3 + kind) * 128
            narrow_ref[:, start : start + 128] = proj_ref[kind, :, pair * 128 : pair * 128 + 128]
    narrow_ref[:, 3 * columns : 4 * columns] = out_ref[...]
    rows_ref[...] = jnp.zeros_like(rows_ref)
    for index, ref in enumerate(singles):
        rows_ref[index : index + 1, 0:SLOT] = ref[...].astype(jnp.float32).reshape(1, SLOT)
    rows_ref[8:10, 0:SLOT] = pair_ref[...].astype(jnp.float32)
    ups = ups_ref[...].astype(jnp.float32).reshape(2, 128)
    for half in range(2):
        rows_ref[10 + 2 * half : 11 + 2 * half, :] = ups[half : half + 1, :]
        rows_ref[11 + 2 * half : 12 + 2 * half, :] = pltpu.roll(ups[half : half + 1, :], SLOT, 1)
    turned = jnp.transpose(rows_ref[...])[0:SLOT]
    narrow_ref[:, 4 * columns :] = jnp.concatenate(
        [turned, jnp.zeros((SLOT, 112), jnp.float32)], axis=1
    ).astype(LOW)
    hidden = up_ref.shape[1]
    wide_ref[:, :hidden] = up_ref[...]
    wide_ref[:, hidden:] = down_ref[...]


def pack_shards(proj, out, up, down, singles, pair, ups):
    rows, columns = out.shape
    return pl.pallas_call(
        pack_kernel,
        out_shape=[
            jax.ShapeDtypeStruct((rows, 4 * columns + 128), LOW),
            jax.ShapeDtypeStruct((rows, 2 * up.shape[1]), LOW),
        ],
        scratch_shapes=[pltpu.VMEM((16, 128), jnp.float32)],
        compiler_params=settings(56),
        cost_estimate=cost(0, 4 * rows * (4 * columns + 2 * up.shape[1])),
        name="pack",
    )(proj, out, up, down, *singles, pair, ups)


def after(value, *events):
    return lax.optimization_barrier((value,) + events)[0]


def dp_shift(value, ranks, dz, dy, dc):
    far, near = 4, ranks // 8

    def goes(rank):
        z, y, c = rank // (near * 2), rank // 2 % near, rank % 2
        return ((z + dz) % far * near + (y + dy) % near) * 2 + (c + dc) % 2

    return lax.ppermute(value, "dp", [(rank, goes(rank)) for rank in range(ranks)])


def dp_gather(shard, ranks, event):
    far = [shard] + [dp_shift(shard, ranks, k, 0, 0) for k in (1, 2, 3)]
    near = [dp_shift(piece, ranks, 0, 1, 0) for piece in (far[0], far[1], far[3])]
    second = dp_shift(after(far[2], event, near[2]), ranks, 0, 1, 0)
    pieces = far + [near[0], near[1], second, near[2]]
    return pieces + [dp_shift(piece, ranks, 0, 0, 1) for piece in pieces], pieces


def reduce_core(left, right, ranks):
    half = left.shape[0] // 2
    return dp_shift(matmul(left[half:], right).astype(LOW), ranks, 0, 0, 1)


def reduce_near(left, right, other):
    half = left.shape[0] // 2
    part = half // 2
    sent = matmul(left[part:half], right) + other[part:].astype(jnp.float32)
    return sent.astype(LOW)


def reduce_sum(left, right, other, arrived):
    part = left.shape[0] // 4
    total = matmul(left[:part], right) + other[:part].astype(jnp.float32)
    return total + arrived.astype(jnp.float32)


def far_send(total, ranks, wire=LOW):
    rows = total.shape[0] // 4
    low = total.astype(wire)
    return [dp_shift(low[k * rows : (k + 1) * rows], ranks, -k, 0, 0) for k in (1, 3, 2)]


def far_sum(total, sent):
    result = total[: total.shape[0] // 4]
    for value in sent:
        result = result + value.astype(jnp.float32)
    return result


def swap(value):
    return lax.ppermute(value, "tensor", [(0, 1), (1, 0)])


def paired(
    inputs,
    out_grad,
    parents,
    ln1_gain,
    ln1_bias,
    w_qkv,
    qv_bias,
    w_attn_out,
    attn_out_bias,
    ln2_gain,
    ln2_bias,
    w_up,
    up_bias,
    w_down,
    down_bias,
):
    ranks = lax.axis_size("dp")
    near = ranks // 8
    rank = lax.axis_index("dp")
    side = lax.axis_index("tensor")
    rows, width = inputs.shape
    shard = width // ranks
    heads_width = w_qkv.shape[2]
    pairs = heads_width // 128
    hidden = w_up.shape[1]
    scale = 1.0 / math.sqrt(width // HEADS)

    slots = jnp.arange(ranks, dtype=jnp.int32)
    core_step, near_step, far_step = slots // (ranks // 2), slots // 4 % near, slots % 4
    my_z, my_y, my_c = rank // (2 * near), rank // 2 % near, rank % 2
    source = ((my_z - far_step) % 4 * near + (my_y - near_step) % near) * 2 + (
        my_c + core_step
    ) % 2
    place = jnp.concatenate([jnp.stack([side, my_z, my_y, my_c]), source]).astype(jnp.int32)
    feature = jnp.repeat(source * shard, shard) + jnp.tile(
        jnp.arange(shard, dtype=jnp.int32), ranks
    )
    to_local = (jnp.arange(width, dtype=jnp.int32)[:, None] == feature[None, :]).astype(LOW)
    slot_of = (slots[:, None] == source[None, :]).astype(jnp.float32)

    singles = [ln1_gain, ln1_bias, attn_out_bias, ln2_gain, ln2_bias, down_bias]
    narrow_shard, wide_shard = pack_shards(
        w_qkv, w_attn_out.T, w_up, w_down.T, singles, qv_bias, up_bias
    )
    narrow, narrow_far = dp_gather(narrow_shard, ranks, place)
    inputs_other = swap(after(inputs, narrow_shard))
    grad_other = swap(after(out_grad, inputs_other))
    wide = lax.all_gather(
        after(wide_shard, inputs_other, *narrow_far[1:6], narrow_far[7]), "dp", axis=0, tiled=True
    )

    def in_order(own, other):
        return jnp.where(
            side == 0,
            jnp.concatenate([own, other], axis=0),
            jnp.concatenate([other, own], axis=0),
        )

    def to_slots(value):
        return lax.dot_general(
            to_local, value, (((0,), (1,)), ((), ())), preferred_element_type=jnp.float32
        ).astype(LOW)

    def other_rows(value):
        return lax.dynamic_slice_in_dim(value, (1 - side) * rows, rows, 0)

    early = front(place, inputs, inputs_other, narrow, pairs, scale)
    hidden_in, xhat, norm_one, out_full, qkv, attended, logs, share, proj_full = early[:9]
    vectors, hidden_bias = early[9:]
    cotangent = after(in_order(out_grad, grad_other), share)
    lefts = jnp.stack([cotangent, jnp.zeros_like(cotangent)])
    norm_slot = to_slots(after(norm_one, share))
    resid, lefts, rights, dnorm_share, dpre_sum = feed_product(
        place, hidden_in, share, swap(after(share, grad_other)), vectors, hidden_bias, lefts, wide
    )
    dnorm_other = swap(dnorm_share)
    wide_share = lax.dot_general(
        lefts,
        after(rights, dnorm_share),
        (((1,), (1,)), ((0,), (0,))),
        preferred_element_type=jnp.float32,
    ).astype(LOW)
    wide_grad = lax.psum_scatter(wide_share, "dp", scatter_dimension=1, tiled=True)
    mixed_share = contract_last(after(rights, wide_share)[0], wide[:, hidden:]).astype(LOW)
    dbranch, dattended, mid_sum = mid_product(
        after(resid, mixed_share, norm_slot), dnorm_share, dnorm_other, lefts, vectors, out_full
    )
    dqkv, dnorm_one, dqkv_sum, front_sum = back_product(
        xhat, qkv, dattended, logs, proj_full, scale
    )
    dqkv_sum = dqkv_sum.reshape(pairs, 3, 128)
    placed = [
        place_block(value, 2 * value.shape[0], side * value.shape[0]).reshape(ranks, -1)
        for value in (
            dqkv_sum[:, 0].reshape(heads_width),
            dqkv_sum[:, 2].reshape(heads_width),
            dpre_sum[0],
        )
    ]
    pack = jnp.concatenate([front_sum, mid_sum[:4]], axis=0)
    pack = pack.reshape(6, ranks, shard).transpose(1, 0, 2).reshape(ranks, -1)
    pack = lax.dot_general(
        slot_of,
        jnp.concatenate([pack] + placed, axis=1),
        (((0,), (0,)), ((), ())),
        precision=lax.Precision.HIGHEST,
        preferred_element_type=jnp.float32,
    )
    proj_core = reduce_core(norm_slot, dqkv, ranks)
    dbranch_slot = to_slots(after(dbranch, pack))
    pack_other = swap(pack)
    out_core = reduce_core(dbranch_slot, attended, ranks)
    proj_near = reduce_near(norm_slot, dqkv, proj_core)
    pack = pack + after(pack_other, proj_near)
    pack = pack[: ranks // 2] + dp_shift(pack[ranks // 2 :], ranks, 0, 0, 1)
    proj_near, pack = lax.optimization_barrier((proj_near, pack))
    pack_arrived = dp_shift(pack[ranks // 4 :], ranks, 0, 1, 0)
    proj_arrived = dp_shift(proj_near, ranks, 0, 1, 0)
    back_other = swap(other_rows(after(dnorm_one, pack)))
    out_near = reduce_near(dbranch_slot, attended, after(out_core, proj_near))
    out_arrived = dp_shift(out_near, ranks, 0, 1, 0)
    own_other = swap(other_rows(after(mixed_share, back_other)))
    proj_arrived, pack_arrived, back_other = lax.optimization_barrier(
        (proj_arrived, pack_arrived, back_other)
    )
    slim_total, pack_total = lax.optimization_barrier(
        (
            reduce_sum(norm_slot, dqkv, proj_core, proj_arrived),
            pack[: ranks // 4] + pack_arrived,
        )
    )
    slim_sent = far_send(slim_total, ranks)
    pack = far_sum(pack_total, far_send(pack_total, ranks, jnp.float32)).reshape(-1)
    out_total = reduce_sum(dbranch_slot, attended, out_core, after(out_arrived, *slim_sent))
    out_sent = far_send(out_total, ranks)
    grad_back = wide_grad[0].T.astype(jnp.float32)
    grad_hidden = wide_grad[1].astype(jnp.float32)
    grad_proj = finish(after(slim_total, grad_back, grad_hidden), slim_sent)
    grad_out = far_sum(out_total, out_sent).T
    result = result_product(
        place, after(resid, slim_total), mixed_share, own_other, vectors
    )
    input_grad = last_product(
        place, inputs, dbranch, dnorm_one, after(back_other, slim_total), vectors
    )
    vector_grads = [pack[i * shard : (i + 1) * shard] for i in range(6)]
    return (
        result,
        input_grad,
        vector_grads[0],
        vector_grads[1],
        grad_proj,
        pack[6 * shard : 8 * shard].reshape(2, shard),
        grad_out,
        vector_grads[2],
        vector_grads[3],
        vector_grads[4],
        grad_hidden,
        pack[8 * shard :],
        grad_back,
        vector_grads[5],
    )


def local(*arrays):
    fits = lax.axis_size("tensor") == 2 and lax.axis_size("dp") == 16
    if fits and arrays[2].shape[1] == 3:
        return paired(*arrays)
    return generic(*arrays)


def solution(mesh):
    return jax.shard_map(
        local,
        mesh=mesh,
        in_specs=(
            P(("dp", "tensor"), None),
            P(("dp", "tensor"), None),
            P("dp", None),
            P("dp"),
            P("dp"),
            P(None, "dp", "tensor"),
            P(None, "dp"),
            P("tensor", "dp"),
            P("dp"),
            P("dp"),
            P("dp"),
            P("dp", "tensor"),
            P("dp"),
            P("tensor", "dp"),
            P("dp"),
        ),
        out_specs=(
            P(("dp", "tensor"), None),
            P(("dp", "tensor"), None),
            P("dp"),
            P("dp"),
            P(None, "dp", "tensor"),
            P(None, "dp"),
            P("tensor", "dp"),
            P("dp"),
            P("dp"),
            P("dp"),
            P("dp", "tensor"),
            P("dp"),
            P("tensor", "dp"),
            P("dp"),
        ),
        check_vma=False,
    )
```
